256 devices in a mesh: batch: 16 (over z_hi, x, core), patch: 16 (over y, z_lo).
Axes of the slice: x: 4, y: 4, z: 8 (z_hi: 2, z_lo: 4; z = z_hi * 4 + z_lo), core: 2. Of those that a mesh axis runs over, the one named last changes fastest.
Arguments:
- latent: bfloat16 [512, 64, 1280], P(('batch', 'patch')), parts along dimension 0, may hold values from -100 to 100
- conv_weight: bfloat16 [3, 3, 1280, 1280], P(None, None, 'patch'), may hold values from -0.25 to 0.25
- channel_bias: float32 [1280], P('patch'), may hold values from -6 to 6
- w_query: bfloat16 [1280, 1280], P('patch'), may hold values from -0.5 to 0.5
- w_key: bfloat16 [1280, 1280], P('patch'), may hold values from -0.5 to 0.5
- w_value: bfloat16 [1280, 1280], P('patch'), may hold values from -0.15625 to 0.15625
- w_out: bfloat16 [1280, 1280], P('patch'), may hold values from -0.15625 to 0.15625
Outputs:
- output: bfloat16 [512, 64, 1280], P(('batch', 'patch')), parts along dimension 0
The draws below stay inside these ranges and needn't reach their ends.
There are 16 independent parts, one for each index of `batch`. The reference program is written for one: setup_inputs(seed, part) draws one part's arguments, and reference() takes and returns one part's arrays. A program takes and returns all parts, laid end to end along the dimension named above; an argument that names none is the same for every part. Nothing has to cross between parts.
All inputs are finite; a program needn't handle non-finite values.
Results may differ from the reference program's by a relative error of at most 0.015.
Values may be sent and summed in bfloat16 or wider, within the bound.
A program may use at most 128 MiB of HBM per device.

```python
import math
import jax
import jax.numpy as jnp
from jax import lax

C = 1280
HEADS = 20
HEAD_DIM = 64
GROUPS = 32
COLS = 64
ROWS = 32


def shared_query(key):
    return jax.random.normal(jax.random.fold_in(key, 7), (C, C), jnp.float32) * (1.5 / math.sqrt(C))


def draw_w_query(key, part):
    return jnp.clip(shared_query(key), -0.5, 0.5).astype(jnp.bfloat16)


def draw_w_key(key, part):
    fresh = jax.random.normal(jax.random.fold_in(key, 13), (C, C), jnp.float32) * (1.5 / math.sqrt(C))
    return jnp.clip(fresh, -0.5, 0.5).astype(jnp.bfloat16)


def draw_conv_weight(key, part):
    stream = jax.random.fold_in(key, 41)
    raw = jax.random.normal(stream, (3, 3, C, C), jnp.float32) * (4.0 / math.sqrt(9 * C))
    return jnp.clip(raw, -0.25, 0.25).astype(jnp.bfloat16)


def draw_latent(key, part):
    streams = jax.random.split(jax.random.fold_in(key, 29), 9)
    position = jnp.arange(ROWS, dtype=jnp.float32) / max(ROWS - 1, 1)
    channel_scale = jnp.exp(jax.random.uniform(streams[1], (C,), jnp.float32, math.log(0.3), math.log(3.0)))
    group_offset = jax.random.normal(streams[8], (GROUPS,), jnp.float32) * 1.5
    channel_mean = jax.random.normal(streams[2], (C,), jnp.float32) * 0.3 + jnp.repeat(group_offset, C // GROUPS)
    roughness = jnp.exp(jax.random.uniform(streams[3], (ROWS, COLS, 1), jnp.float32, -0.7, 0.7))
    base = jax.random.normal(streams[0], (ROWS, COLS, C), jnp.float32)
    rising = jnp.exp(math.log(3.0) * position)
    mean_rise = jnp.exp(math.log(3.0) * position)
    field = base * rising[:, None, None] * roughness * channel_scale + channel_mean * mean_rise[:, None, None]
    return jnp.clip(field, -100.0, 100.0).astype(jnp.bfloat16)


def level_of(stream_key, dims, shards, smallest, high):
    def one(axis_at, parts):
        heights = jax.random.uniform(jax.random.fold_in(jax.random.fold_in(stream_key, 6), axis_at), (parts,), jnp.float32, smallest / len(shards), high / len(shards))
        return jnp.repeat(jnp.exp(heights), dims[axis_at] // parts).reshape((-1,) + (1,) * (len(dims) - axis_at - 1))

    level = one(*shards[0])
    for cut in shards[1:]:
        level = level * one(*cut)
    return level


def centred(rng, dims, scale, limit, cuts=(), kind=jnp.bfloat16):
    drawn = scale * jax.random.normal(rng, dims, jnp.float32)
    if cuts:
        drawn = drawn * level_of(rng, dims, cuts, -0.22, 0.18)
    return jnp.clip(drawn, -limit, limit).astype(kind)


def setup_inputs(seed: int = 0, part: int = 0) -> dict:
    key_list = jax.random.split(jax.random.key(seed), 8)
    own_keys = jax.random.split(jax.random.fold_in(key_list[7], part), 8)
    latent = draw_latent(jax.random.fold_in(jax.random.fold_in(key_list[7], part), 71), part)
    conv_weight = draw_conv_weight(jax.random.fold_in(key_list[7], 71), part)
    channel_bias = centred(key_list[2], (C,), 1.0, 6.0, ((0, 16),), jnp.float32)
    w_query = draw_w_query(jax.random.fold_in(key_list[7], 71), part)
    w_key = draw_w_key(jax.random.fold_in(key_list[7], 71), part)
    w_value = centred(key_list[5], (C, C), C ** -0.5, 0.15625, ((0, 16),))
    w_out = centred(key_list[6], (C, C), C ** -0.5, 0.15625, ((0, 16),))
    return {"latent": latent, "conv_weight": conv_weight, "channel_bias": channel_bias, "w_query": w_query, "w_key": w_key, "w_value": w_value, "w_out": w_out}


epsilon = 1e-05

def contract(left, right):
    return lax.dot_general(left, right, (((1,), (1,)), ((), ())), preferred_element_type=jnp.float32)

def group_norm(values):
    grouped = values.reshape(-1, GROUPS, C // GROUPS)
    centre = lax.optimization_barrier(jnp.mean(grouped, axis=(0, 2), keepdims=True))
    spread = lax.optimization_barrier(jnp.mean(jnp.square(grouped - centre), axis=(0, 2), keepdims=True))
    return ((grouped - centre) * lax.rsqrt(spread + epsilon)).reshape(values.shape)

def convolve(padded, kernel, row_count):
    running = jnp.zeros((row_count * COLS, kernel.shape[2]), jnp.float32)
    for row_shift in range(3):
        for col_shift in range(3):
            window = padded[row_shift:row_shift + row_count, col_shift:col_shift + COLS, :].reshape(-1, C)
            running = running + contract(window, kernel[row_shift, col_shift])
    return running

def attend(queries, key_all, value_all):
    query_heads = queries.reshape(-1, HEADS, HEAD_DIM).transpose(1, 0, 2)
    key_heads = key_all.reshape(-1, HEADS, HEAD_DIM).transpose(1, 0, 2)
    value_heads = value_all.reshape(-1, HEADS, HEAD_DIM).transpose(1, 0, 2)

    def one_head(triple):
        query_one, key_one, value_one = triple
        scores = jnp.dot(query_one, key_one.T, preferred_element_type=jnp.float32) * HEAD_DIM ** (-0.5)
        row_peak = lax.optimization_barrier(jnp.max(scores, axis=1, keepdims=True))
        unnormalized = jnp.exp(scores - row_peak)
        row_total = lax.optimization_barrier(jnp.sum(unnormalized, axis=1, keepdims=True))
        mixture = jnp.dot(unnormalized.astype(jnp.bfloat16), value_one, preferred_element_type=jnp.float32)
        return mixture / row_total
    heads_out = lax.map(one_head, (query_heads, key_heads, value_heads))
    return heads_out.transpose(1, 0, 2).reshape(-1, C).astype(jnp.bfloat16)

def reference(latent, conv_weight, channel_bias, w_query, w_key, w_value, w_out):
    inputs = latent.astype(jnp.float32)
    activated = jax.nn.silu(group_norm(inputs)).astype(jnp.bfloat16)
    padded = jnp.pad(activated, ((1, 1), (1, 1), (0, 0)))
    convolved = convolve(padded, conv_weight, ROWS).reshape(ROWS, COLS, C)
    hidden = (inputs + convolved + channel_bias).astype(jnp.bfloat16)
    hidden = lax.optimization_barrier(hidden)
    residual = hidden.astype(jnp.float32).reshape(-1, C)
    normed = group_norm(residual).astype(jnp.bfloat16)
    queries = contract(normed, w_query).astype(jnp.bfloat16)
    key_all = contract(normed, w_key).astype(jnp.bfloat16)
    value_all = contract(normed, w_value).astype(jnp.bfloat16)
    attended = attend(queries, key_all, value_all)
    output = (residual + contract(attended, w_out)).astype(jnp.bfloat16)
    return output.reshape(ROWS, COLS, C)
```

```python
import jax
import jax.numpy as jnp
from jax import lax
from jax.experimental import pallas as pl
from jax.experimental.pallas import tpu as pltpu
from jax.sharding import PartitionSpec as P

C = 1280
HEADS = 20
HEAD_DIM = 64
GROUPS = 32
GROUP = C // GROUPS
NY, NZ = 4, 4
BLK = 128
ROWS_Y = 512
CB = C // 16
CZ = C // 4
EPS = 1e-05
MESH = pl.DeviceIdType.MESH
F32 = jnp.float32
BF16 = jnp.bfloat16


def dot_nt(left, right):
    return lax.dot_general(left, right, (((1,), (1,)), ((), ())), preferred_element_type=F32)


def dot_nn(left, right):
    return lax.dot_general(left, right, (((1,), (0,)), ((), ())), preferred_element_type=F32)


def kernel(
    lat_in, cw_in, bias_in, wq_in, wk_in, wv_in, wo_in, out_ref,
    lat, act, cw, wown, wqkv, wo, st1s, st1, st2s, st2, gmat, gmat_t, sel,
    gn1, gn2, ubuf, hidg, nrm, hnat, qb, kv, att, attg,
    s_loc, s_st1, r_st1, s_lat, r_lat, s_halo, r_halo, s_cw, r_cw, s_cws, r_cws,
    s_qw, r_qw, s_qws, r_qws, l_qw, s_woz, r_woz, s_woy, r_woy, s_wos, r_wos,
    s_st2, r_st2, s_hid, r_hid, s_kv, r_kv, s_att, r_att,
):
    p = lax.axis_index("patch")
    b = lax.axis_index("batch")
    y = p // 4
    z = p % 4
    c = b % 2
    sib = b + 1 - 2 * c
    up = (y + 1) % 4
    down = (y + 3) % 4
    opposite = (y + 2) % 4
    half = pl.ds(pl.multiple_of(c * (C // 2), 128), C // 2)
    other = pl.ds(pl.multiple_of((1 - c) * (C // 2), 128), C // 2)
    pending = []

    def patch(yy, zz):
        return {"batch": b, "patch": 4 * yy + zz}

    sibling = {"batch": sib, "patch": p}

    def remote(src, dst, ssem, rsem, dev):
        return pltpu.make_async_remote_copy(
            src_ref=src, dst_ref=dst, send_sem=ssem, recv_sem=rsem, device_id=dev, device_id_type=MESH
        )

    def when(cond, f):
        if cond is None:
            f()
        else:
            pl.when(cond)(f)

    def send(make, cond=None):
        when(cond, lambda: make().start())
        pending.append((cond, make))

    own_rows = pl.ds(pl.multiple_of(64 + BLK * z, 64), BLK)
    loc = [
        pltpu.make_async_copy(lat_in, lat.at[own_rows], s_loc.at[0]),
        pltpu.make_async_copy(cw_in, cw.at[:, :, y], s_loc.at[1]),
        pltpu.make_async_copy(wq_in, wown.at[0], s_loc.at[2]),
        pltpu.make_async_copy(wk_in, wown.at[1], s_loc.at[3]),
        pltpu.make_async_copy(wv_in, wown.at[2], s_loc.at[4]),
        pltpu.make_async_copy(wo_in, wown.at[3], s_loc.at[5]),
        pltpu.make_async_copy(wo_in.at[:, half], wo.at[p, :, half], s_loc.at[6]),
    ]
    for copy in loc:
        copy.start()
    barrier = pltpu.get_barrier_semaphore()
    for d in range(1, 16):
        pl.semaphore_signal(
            barrier, inc=1, device_id={"batch": b, "patch": (p + d) % 16}, device_id_type=MESH
        )
    pl.semaphore_signal(barrier, inc=1, device_id=sibling, device_id_type=MESH)

    st1s[...] = jnp.zeros_like(st1s)
    loc[0].wait()
    mine = lat[own_rows].astype(F32)
    mean = jnp.sum(mine, axis=0, keepdims=True) * (1.0 / BLK)
    m2 = jnp.sum(jnp.square(mine - mean), axis=0, keepdims=True)
    for j in range(10):
        st1s[j : j + 1, :] = mean[:, 128 * j : 128 * j + 128]
        st1s[16 + j : 17 + j, :] = m2[:, 128 * j : 128 * j + 128]
    st1s[15:16, 0:CB] = bias_in[...]

    pl.semaphore_wait(barrier, 16)

    for d in range(1, 16):
        send(
            lambda d=d: remote(
                st1s, st1.at[p], s_st1.at[d], r_st1.at[d], {"batch": b, "patch": (p + d) % 16}
            )
        )
    st1[p] = st1s[...]

    def lat_rows(k):
        return lat.at[pl.ds(pl.multiple_of(64 + BLK * k, 64), BLK)]

    def lat_copy(k, way):
        zz = z + 1 if way == 0 else z - 1
        return remote(lat_rows(k), lat_rows(k), s_lat.at[way, k], r_lat.at[k], patch(y, zz))

    send(lambda: lat_copy(z, 0), z < 3)
    send(lambda: lat_copy(z, 1), z > 0)

    loc[1].wait()

    def cw_copy(src_y, to_y, slot):
        ref = cw.at[:, :, src_y, :, half]
        return remote(ref, ref, s_cw.at[slot], r_cw.at[slot], patch(to_y, z))

    def cw_forward(src_y, slot):
        ref = cw.at[:, :, src_y, :, half]
        return remote(ref, ref, s_cws.at[slot], r_cws.at[slot], sibling)

    def cw_arrival(src_y, slot):
        ref = cw.at[:, :, src_y, :, other]
        return remote(ref, ref, s_cws.at[slot], r_cws.at[slot], sibling)

    send(lambda: cw_copy(y, up, 0))
    send(lambda: cw_copy(y, down, 1))

    gi = lax.broadcasted_iota(jnp.int32, (C, 128), 0) - GROUP * lax.broadcasted_iota(jnp.int32, (C, 128), 1)
    gmat[...] = jnp.where((gi >= 0) & (gi < GROUP), 1.0, 0.0).astype(BF16)
    ti = lax.broadcasted_iota(jnp.int32, (128, C), 1) - GROUP * lax.broadcasted_iota(jnp.int32, (128, C), 0)
    gmat_t[...] = jnp.where((ti >= 0) & (ti < GROUP), 1.0, 0.0).astype(BF16)
    for yy in range(4):
        rows = lax.broadcasted_iota(jnp.int32, (CZ, CZ), 0) - CB * z
        cols = lax.broadcasted_iota(jnp.int32, (CZ, CZ), 1) - CB * yy
        hit = (rows == cols) & (cols >= 0) & (cols < CB)
        sel[CZ * yy : CZ * yy + CZ, :] = jnp.where(hit, 1.0, 0.0).astype(BF16)

    def split_rows(x):
        hi = x.astype(BF16).astype(F32)
        mid = (x - hi).astype(BF16).astype(F32)
        return jnp.concatenate([hi, mid, x - hi - mid], axis=0).astype(BF16)

    def join_rows(x):
        return x[0:8] + x[8:16] + x[16:24]

    def group_sums(x):
        n = x.shape[1]
        sums = join_rows(dot_nn(split_rows(x), gmat[0:n, :]))
        return join_rows(dot_nn(split_rows(sums), gmat_t[:, 0:n]))

    for d in range(1, 16):
        q = (p + 16 - d) % 16
        remote(st1s, st1.at[q], s_st1.at[d], r_st1.at[d], {"batch": b, "patch": q}).wait_recv()
    means = st1[:, 0:16, :]
    mean_c = jnp.sum(means, axis=0) * (1.0 / 16)
    m2_c = jnp.sum(st1[:, 16:32, :], axis=0) + BLK * jnp.sum(jnp.square(means - mean_c[None]), axis=0)

    def to_lanes(x, n):
        full = jnp.concatenate([x[j : j + 1, :] for j in range(n)], axis=1)
        return full

    mean_l = jnp.broadcast_to(to_lanes(mean_c, 10), (8, C))
    m2_l = jnp.broadcast_to(to_lanes(m2_c, 10), (8, C))
    centre = group_sums(mean_l) * (1.0 / GROUP)
    spread = group_sums(m2_l + 2048.0 * jnp.square(mean_l - centre)) * (1.0 / (2048 * GROUP))
    gn1[0] = centre
    gn1[1] = lax.rsqrt(spread + EPS)

    def activate(start, count):
        def body(i, carry):
            rows = pl.ds(pl.multiple_of(start + 16 * i, 16), 16)
            v = lat[rows].astype(F32)
            v = (v - gn1[0, 0:1, :]) * gn1[1, 0:1, :]
            act[rows] = (v / (1.0 + jnp.exp(-v))).astype(BF16)
            return carry

        lax.fori_loop(0, count // 16, body, 0)

    activate(64 + BLK * z, BLK)

    def halo_up():
        return remote(
            lat.at[pl.ds(512, 64)], lat.at[pl.ds(0, 64)], s_halo.at[0], r_halo.at[0], patch(y + 1, z)
        )

    def halo_down():
        return remote(
            lat.at[pl.ds(64, 64)], lat.at[pl.ds(576, 64)], s_halo.at[1], r_halo.at[1], patch(y - 1, z)
        )

    send(halo_up, (z == 3) & (y < 3))
    send(halo_down, (z == 0) & (y > 0))
    for k in range(1, 4):
        def below(k=k):
            lat_copy(z - k, 0).wait_recv()

        def above(k=k):
            lat_copy(z + k, 1).wait_recv()

        when(z - k >= 0, below)
        send(lambda k=k: lat_copy(z - k, 0), (z - k >= 0) & (z < 3))
        when(z + k <= 3, above)
        send(lambda k=k: lat_copy(z + k, 1), (z + k <= 3) & (z > 0))
        send(halo_up, (z + k == 3) & (y < 3))
        send(halo_down, (z - k == 0) & (y > 0))
        when(z - k >= 0, lambda k=k: activate(64 + BLK * (z - k), BLK))
        when(z + k <= 3, lambda k=k: activate(64 + BLK * (z + k), BLK))

    cw_copy(down, y, 0).wait_recv()
    send(lambda: cw_copy(down, up, 2), c == 0)
    send(lambda: cw_forward(down, 0))
    cw_copy(up, y, 1).wait_recv()
    send(lambda: cw_copy(up, down, 2), c == 1)
    send(lambda: cw_forward(up, 1))

    for copy in loc[2:]:
        copy.wait()

    def qw_rows(k):
        return pl.ds(pl.multiple_of(CB * k, 16), CB)

    def qw_copy(yy, k, zz):
        return remote(
            wown.at[0:3, :, half], wqkv.at[:, qw_rows(k), half], s_qw.at[yy], r_qw.at[k], patch(yy, zz)
        )

    def qw_local():
        return pltpu.make_async_copy(wown.at[0:3, :, half], wqkv.at[:, qw_rows(z), half], l_qw.at[0])

    for yy in range(4):
        send(lambda yy=yy: qw_copy(yy, z, y), (y != yy) | (z != y))
    when(z == y, lambda: qw_local().start())

    when(y > 0, lambda: halo_up().wait_recv())
    when(y > 0, lambda: activate(0, 64))
    when(y < 3, lambda: halo_down().wait_recv())
    when(y < 3, lambda: activate(576, 64))

    def zero_top():
        act[0:64] = jnp.zeros((64, C), BF16)

    def zero_bottom():
        act[576:640] = jnp.zeros((64, C), BF16)

    when(y == 0, zero_top)
    when(y == 3, zero_bottom)

    cw_copy(opposite, y, 2).wait_recv()
    send(lambda: cw_forward(opposite, 2))
    cw_arrival(down, 0).wait_recv()
    cw_arrival(up, 1).wait_recv()
    cw_arrival(opposite, 2).wait_recv()

    bias = jnp.concatenate([st1[4 * yy + z, 15:16, 0:CB] for yy in range(4)], axis=1)
    CHUNK = 256

    def conv_chunk(j, carry):
        total = jnp.zeros((CHUNK, 3 * CZ), F32)
        for dr in range(3):
            rows = pl.ds(pl.multiple_of(CHUNK * j + 64 * dr, 64), CHUNK)
            total = total + dot_nt(act[rows], cw[dr].reshape(3 * CZ, C))
        ubuf[...] = total
        column = lax.broadcasted_iota(jnp.int32, (CHUNK, CZ), 0) % 64
        left = pltpu.roll(ubuf[:, 0:CZ], 1, 0)
        right = pltpu.roll(ubuf[:, 2 * CZ : 3 * CZ], CHUNK - 1, 0)
        value = ubuf[:, CZ : 2 * CZ]
        value = value + jnp.where(column == 0, 0.0, left) + jnp.where(column == 63, 0.0, right)
        own = lat[pl.ds(pl.multiple_of(64 + CHUNK * j, 64), CHUNK)]
        value = value + dot_nn(own, sel[...]) + bias
        hidg[z, pl.ds(pl.multiple_of(CHUNK * j, 128), CHUNK), :] = value.astype(BF16)
        return carry

    lax.fori_loop(0, ROWS_Y // CHUNK, conv_chunk, 0)

    def hid_copy(k, way):
        zz = z + 1 if way == 0 else z - 1
        return remote(hidg.at[k], hidg.at[k], s_hid.at[way, k], r_hid.at[k], patch(y, zz))

    send(lambda: hid_copy(z, 0), z < 3)
    send(lambda: hid_copy(z, 1), z > 0)

    st2s[...] = jnp.zeros_like(st2s)
    hidden = hidg[z].astype(F32)
    mean = jnp.sum(hidden, axis=0, keepdims=True) * (1.0 / ROWS_Y)
    m2 = jnp.sum(jnp.square(hidden - mean), axis=0, keepdims=True)
    for j in range(3):
        width = min(128, CZ - 128 * j)
        st2s[j : j + 1, 0:width] = mean[:, 128 * j : 128 * j + width]
        st2s[4 + j : 5 + j, 0:width] = m2[:, 128 * j : 128 * j + width]
    for d in range(1, 16):
        send(
            lambda d=d: remote(
                st2s, st2.at[p], s_st2.at[d], r_st2.at[d], {"batch": b, "patch": (p + d) % 16}
            )
        )
    st2[p] = st2s[...]

    def qw_forward(k):
        ref = wqkv.at[:, qw_rows(k), half]
        return remote(ref, ref, s_qws.at[k], r_qws.at[k], sibling)

    def qw_arrival(k):
        ref = wqkv.at[:, qw_rows(k), other]
        return remote(ref, ref, s_qws.at[k], r_qws.at[k], sibling)

    for k in range(4):
        remote_wait = (y != z) | (z != k)
        when(remote_wait, lambda k=k: qw_copy(0, k, 0).wait_recv())
        when(~remote_wait, lambda: qw_local().wait())
        send(lambda k=k: qw_forward(k))

    for d in range(1, 16):
        q = (p + 16 - d) % 16
        remote(st2s, st2.at[q], s_st2.at[d], r_st2.at[d], {"batch": b, "patch": q}).wait_recv()
    parts = [[st2[4 * yy + zz] for zz in range(4)] for yy in range(4)]
    mean_rows, m2_rows = [], []
    for zz in range(4):
        col = [parts[yy][zz] for yy in range(4)]
        m = (col[0] + col[1] + col[2] + col[3]) * 0.25
        dev = sum(jnp.square(x - m) for x in col)
        total = col[0] + col[1] + col[2] + col[3]
        m2_all = total[4:8] + ROWS_Y * dev[0:4]
        mean_rows.append(to_lanes(m, 3)[:, 0:CZ])
        m2_rows.append(to_lanes(m2_all, 3)[:, 0:CZ])
    mean_l = jnp.concatenate(mean_rows + mean_rows, axis=0)
    m2_l = jnp.concatenate(m2_rows + m2_rows, axis=0)
    centre = group_sums(mean_l) * (1.0 / GROUP)
    spread = group_sums(m2_l + 2048.0 * jnp.square(mean_l - centre)) * (1.0 / (2048 * GROUP))
    gn2[0] = centre
    gn2[1] = lax.rsqrt(spread + EPS)

    for k in range(1, 4):
        when(z - k >= 0, lambda k=k: hid_copy(z - k, 0).wait_recv())
        send(lambda k=k: hid_copy(z - k, 0), (z - k >= 0) & (z < 3))
        when(z + k <= 3, lambda k=k: hid_copy(z + k, 1).wait_recv())
        send(lambda k=k: hid_copy(z + k, 1), (z + k <= 3) & (z > 0))

    def wo_z(k, way):
        zz = z + 1 if way == 0 else z - 1
        ref = wo.at[4 * y + k, :, half]
        return remote(ref, ref, s_woz.at[way, k], r_woz.at[k], patch(y, zz))

    send(lambda: wo_z(z, 0), z < 3)
    send(lambda: wo_z(z, 1), z > 0)

    def normalize(i, carry):
        rows = pl.ds(pl.multiple_of(16 * i, 16), 16)
        blocks = [
            (hidg[zz, rows, :].astype(F32) - gn2[0, zz : zz + 1, :]) * gn2[1, zz : zz + 1, :]
            for zz in range(4)
        ]
        nrm[rows] = jnp.concatenate(
            [blocks[zz][:, CB * yy : CB * yy + CB] for yy in range(4) for zz in range(4)], axis=1
        ).astype(BF16)
        return carry

    lax.fori_loop(0, ROWS_Y // 16, normalize, 0)

    for k in range(4):
        qw_arrival(k).wait_recv()

    def project(j, carry):
        rows = pl.ds(pl.multiple_of(256 * j, 256), 256)
        block = nrm[rows]
        kv[0, y, rows, :] = dot_nt(block, wqkv[1]).astype(BF16)
        kv[1, y, rows, :] = dot_nt(block, wqkv[2]).astype(BF16)
        qb[rows] = (dot_nt(block, wqkv[0]).astype(BF16).astype(F32) * HEAD_DIM**-0.5).astype(BF16)
        return carry

    lax.fori_loop(0, ROWS_Y // 256, project, 0)

    def kv_copy(which, src_y, to_y, slot):
        ref = kv.at[which, src_y]
        return remote(ref, ref, s_kv.at[which, slot], r_kv.at[which, slot], patch(to_y, z))

    for which in range(2):
        send(lambda which=which: kv_copy(which, y, up, 0))
        send(lambda which=which: kv_copy(which, y, down, 1))

    def residual(i, carry):
        rows = pl.ds(pl.multiple_of(BLK * z + 16 * i, 16), 16)
        blocks = [hidg[zz, rows, :].astype(F32) for zz in range(4)]
        hnat[pl.ds(pl.multiple_of(16 * i, 16), 16)] = jnp.concatenate(
            [blocks[zz][:, CB * yy : CB * yy + CB] for yy in range(4) for zz in range(4)], axis=1
        )
        return carry

    lax.fori_loop(0, BLK // 16, residual, 0)

    for k in range(1, 4):
        when(z - k >= 0, lambda k=k: wo_z(z - k, 0).wait_recv())
        send(lambda k=k: wo_z(z - k, 0), (z - k >= 0) & (z < 3))
        when(z + k <= 3, lambda k=k: wo_z(z + k, 1).wait_recv())
        send(lambda k=k: wo_z(z + k, 1), (z + k <= 3) & (z > 0))

    kv_copy(0, down, y, 0).wait_recv()
    send(lambda: kv_copy(0, down, up, 2))
    kv_copy(1, up, y, 1).wait_recv()
    send(lambda: kv_copy(1, up, down, 2))

    def wo_row(src_y, mask):
        return wo.at[pl.ds(4 * src_y, 4), :, mask]

    def wo_y(src_y, to_y, slot):
        ref = wo_row(src_y, half)
        return remote(ref, ref, s_woy.at[slot], r_woy.at[slot], patch(to_y, z))

    send(lambda: wo_y(y, up, 0))
    send(lambda: wo_y(y, down, 1))
    kv_copy(1, down, y, 0).wait_recv()
    kv_copy(0, up, y, 1).wait_recv()
    kv_copy(0, opposite, y, 2).wait_recv()
    kv_copy(1, opposite, y, 2).wait_recv()

    def att_copy(j):
        return remote(att.at[j], attg.at[z], s_att.at[j], r_att.at[z], patch(y, j))

    def att_from(k):
        return remote(att.at[k], attg.at[k], s_att.at[k], r_att.at[k], patch(y, k))

    def attend(j):
        rows = pl.ds(pl.multiple_of(BLK * j, 128), BLK)
        for pair in range(3):
            width = min(128, CZ - 128 * pair)
            lanes = slice(128 * pair, 128 * pair + width)
            query = qb[rows, lanes]
            keys = kv[0, :, :, lanes].reshape(2048, width)
            values = kv[1, :, :, lanes].reshape(2048, width)
            lane = lax.broadcasted_iota(jnp.int32, (BLK, width), 1)
            result = None
            for side in range(width // 64):
                q1 = query
                if width > 64:
                    keep = (lane >= 64 * side) & (lane < 64 * side + 64)
                    q1 = jnp.where(keep, query.astype(F32), 0.0).astype(BF16)
                scores = dot_nt(q1, keys)
                peak = jnp.max(scores, axis=1, keepdims=True)
                unnormalized = jnp.exp(scores - peak)
                row_total = jnp.sum(unnormalized, axis=1, keepdims=True)
                mix = dot_nn(unnormalized.astype(BF16), values) / row_total
                result = mix if result is None else jnp.where(lane < 64, result, mix)
            att[j, :, lanes] = result.astype(BF16)

    def attend_step(t, carry):
        j = (z + 1 + t) % 4
        attend(j)
        pl.when(t < 3)(lambda: att_copy(j).start())
        return carry

    lax.fori_loop(0, 4, attend_step, 0)
    attg[z] = att[z]
    for k in range(4):
        pending.append((z != k, lambda k=k: att_copy(k)))

    wo_y(down, y, 0).wait_recv()
    send(lambda: wo_y(down, up, 2), c == 0)
    wo_y(up, y, 1).wait_recv()
    send(lambda: wo_y(up, down, 2), c == 1)
    wo_y(opposite, y, 2).wait_recv()

    def wo_forward(k):
        ref = wo_row(k, half)
        return remote(ref, ref, s_wos.at[k], r_wos.at[k], sibling)

    def wo_arrival(k):
        ref = wo_row(k, other)
        return remote(ref, ref, s_wos.at[k], r_wos.at[k], sibling)

    for k in range(4):
        send(lambda k=k: wo_forward(k))
    for k in range(4):
        wo_arrival(k).wait_recv()
    for k in range(4):
        when(z != k, lambda k=k: att_from(k).wait_recv())

    whole = jnp.concatenate([attg[k].astype(F32) for k in range(4)], axis=1).astype(BF16)
    out_ref[...] = (hnat[...] + dot_nt(whole, wo[...].reshape(C, C))).astype(BF16)

    for cond, make in pending:
        when(cond, lambda make=make: make().wait_send())


def on_device(latent, conv_weight, channel_bias, w_query, w_key, w_value, w_out):
    any_space = pl.BlockSpec(memory_space=pl.ANY)
    vmem = pl.BlockSpec(memory_space=pltpu.VMEM)
    dma = pltpu.SemaphoreType.DMA
    out = pl.pallas_call(
        kernel,
        out_shape=jax.ShapeDtypeStruct((BLK, C), BF16),
        in_specs=[any_space, any_space, vmem, any_space, any_space, any_space, any_space],
        out_specs=vmem,
        scratch_shapes=[
            pltpu.VMEM((640, C), BF16),
            pltpu.VMEM((640, C), BF16),
            pltpu.VMEM((3, 3, 4, CB, C), BF16),
            pltpu.VMEM((4, CB, C), BF16),
            pltpu.VMEM((3, CZ, C), BF16),
            pltpu.VMEM((16, CB, C), BF16),
            pltpu.VMEM((32, 128), F32),
            pltpu.VMEM((16, 32, 128), F32),
            pltpu.VMEM((8, 128), F32),
            pltpu.VMEM((16, 8, 128), F32),
            pltpu.VMEM((C, 128), BF16),
            pltpu.VMEM((128, C), BF16),
            pltpu.VMEM((C, CZ), BF16),
            pltpu.VMEM((2, 8, C), F32),
            pltpu.VMEM((2, 8, CZ), F32),
            pltpu.VMEM((256, 3 * CZ), F32),
            pltpu.VMEM((4, ROWS_Y, CZ), BF16),
            pltpu.VMEM((ROWS_Y, C), BF16),
            pltpu.VMEM((BLK, C), F32),
            pltpu.VMEM((ROWS_Y, CZ), BF16),
            pltpu.VMEM((2, 4, ROWS_Y, CZ), BF16),
            pltpu.VMEM((4, BLK, CZ), BF16),
            pltpu.VMEM((4, BLK, CZ), BF16),
            dma((7,)), dma((16,)), dma((16,)), dma((2, 4)), dma((4,)), dma((2,)), dma((2,)),
            dma((3,)), dma((3,)), dma((3,)), dma((3,)),
            dma((4,)), dma((4,)), dma((4,)), dma((4,)), dma((1,)),
            dma((2, 4)), dma((4,)), dma((3,)), dma((3,)), dma((4,)), dma((4,)),
            dma((16,)), dma((16,)), dma((2, 4)), dma((4,)), dma((2, 3)), dma((2, 3)), dma((4,)), dma((4,)),
        ],
        compiler_params=pltpu.CompilerParams(
            collective_id=0, has_side_effects=True, vmem_limit_bytes=60 * 1024 * 1024
        ),
    )(
        latent.reshape(BLK, C), conv_weight, channel_bias.reshape(1, CB), w_query, w_key, w_value, w_out
    )
    return out.reshape(latent.shape)


def solution(mesh):
    return jax.shard_map(
        on_device,
        mesh=mesh,
        in_specs=(
            P(("batch", "patch"), None, None),
            P(None, None, "patch", None),
            P("patch"),
            P("patch", None),
            P("patch", None),
            P("patch", None),
            P("patch", None),
        ),
        out_specs=P(("batch", "patch"), None, None),
        check_vma=False,
    )
```

```python
import jax
import jax.numpy as jnp
from jax import lax
from jax.experimental import pallas as pl
from jax.experimental.pallas import tpu as pltpu
from jax.sharding import PartitionSpec as P

C = 1280
HEADS = 20
HEAD_DIM = 64
GROUPS = 32
GROUP = C // GROUPS
NY, NZ = 4, 4
BLK = 128
ROWS_Y = 512
CB = C // 16
CZ = C // 4
EPS = 1e-05
MESH = pl.DeviceIdType.MESH
F32 = jnp.float32
BF16 = jnp.bfloat16


def dot_nt(left, right):
    return lax.dot_general(left, right, (((1,), (1,)), ((), ())), preferred_element_type=F32)


def dot_nn(left, right):
    return lax.dot_general(left, right, (((1,), (0,)), ((), ())), preferred_element_type=F32)


def kernel(
    lat_in, cw_in, bias_in, wq_in, wk_in, wv_in, wo_in, out_ref,
    lat, act, cw, wown, wqkv, wo, st1s, st1, st2s, st2, gmat, gmat_t, sel,
    gn1, gn2, ubuf, hidg, nrm, hnat, qb, kv, att, attg,
    s_loc, s_st1, r_st1, s_lat, r_lat, s_halo, r_halo, s_cw, r_cw, s_cws, r_cws,
    s_ct, r_ct, s_cx, r_cx, s_cts, r_cts,
    s_qa, r_qa, l_qa, s_qb, r_qb, s_qc, r_qc, s_qd, r_qd, s_woz, r_woz, s_woy, r_woy, s_wos, r_wos,
    s_st2, r_st2, s_hid, r_hid, s_kv, r_kv, s_att, r_att,
):
    p = lax.axis_index("patch")
    b = lax.axis_index("batch")
    y = p // 4
    z = p % 4
    c = b % 2
    x = (b // 2) % 4
    sib = b + 1 - 2 * c
    up = (y + 1) % 4
    down = (y + 3) % 4
    opposite = (y + 2) % 4
    half = pl.ds(pl.multiple_of(c * (C // 2), 128), C // 2)
    other = pl.ds(pl.multiple_of((1 - c) * (C // 2), 128), C // 2)
    pending = []

    def patch(yy, zz):
        return {"batch": b, "patch": 4 * yy + zz}

    def across(d):
        return {"batch": b - 2 * x + 2 * ((x + d) % 4), "patch": p}

    sibling = {"batch": sib, "patch": p}

    def remote(src, dst, ssem, rsem, dev):
        return pltpu.make_async_remote_copy(
            src_ref=src, dst_ref=dst, send_sem=ssem, recv_sem=rsem, device_id=dev, device_id_type=MESH
        )

    def when(cond, f):
        if cond is None:
            f()
        else:
            pl.when(cond)(f)

    def send(make, cond=None):
        when(cond, lambda: make().start())
        pending.append((cond, make))

    own_rows = pl.ds(pl.multiple_of(64 + BLK * z, 64), BLK)
    loc = [
        pltpu.make_async_copy(lat_in, lat.at[own_rows], s_loc.at[0]),
        pltpu.make_async_copy(cw_in, cw.at[:, y], s_loc.at[1]),
        pltpu.make_async_copy(wq_in, wown.at[0], s_loc.at[2]),
        pltpu.make_async_copy(wk_in, wown.at[1], s_loc.at[3]),
        pltpu.make_async_copy(wv_in, wown.at[2], s_loc.at[4]),
        pltpu.make_async_copy(wo_in, wown.at[3], s_loc.at[5]),
        pltpu.make_async_copy(wo_in.at[:, half], wo.at[p, :, half], s_loc.at[6]),
    ]
    for copy in loc:
        copy.start()
    barrier = pltpu.get_barrier_semaphore()
    for d in range(1, 16):
        pl.semaphore_signal(
            barrier, inc=1, device_id={"batch": b, "patch": (p + d) % 16}, device_id_type=MESH
        )
    pl.semaphore_signal(barrier, inc=1, device_id=sibling, device_id_type=MESH)
    for d in range(1, 4):
        pl.semaphore_signal(barrier, inc=1, device_id=across(d), device_id_type=MESH)

    st1s[...] = jnp.zeros_like(st1s)
    loc[0].wait()
    mine = lat[own_rows].astype(F32)
    mean = jnp.sum(mine, axis=0, keepdims=True) * (1.0 / BLK)
    m2 = jnp.sum(jnp.square(mine - mean), axis=0, keepdims=True)
    for j in range(10):
        st1s[j : j + 1, :] = mean[:, 128 * j : 128 * j + 128]
        st1s[16 + j : 17 + j, :] = m2[:, 128 * j : 128 * j + 128]
    st1s[15:16, 0:CB] = bias_in[...]

    pl.semaphore_wait(barrier, 19)

    for d in range(1, 16):
        send(
            lambda d=d: remote(
                st1s, st1.at[p], s_st1.at[d], r_st1.at[d], {"batch": b, "patch": (p + d) % 16}
            )
        )
    st1[p] = st1s[...]

    def lat_rows(k):
        return lat.at[pl.ds(pl.multiple_of(64 + BLK * k, 64), BLK)]

    def lat_copy(k, way):
        zz = z + 1 if way == 0 else z - 1
        return remote(lat_rows(k), lat_rows(k), s_lat.at[way, k], r_lat.at[k], patch(y, zz))

    send(lambda: lat_copy(z, 0), z < 3)
    send(lambda: lat_copy(z, 1), z > 0)

    loc[1].wait()
    around = (down, up, opposite)

    def cw_ref(src_y, mask):
        return cw.at[0:5, src_y, :, mask]

    def cw_copy(src_y, to_y, slot):
        ref = cw_ref(src_y, half)
        return remote(ref, ref, s_cw.at[slot], r_cw.at[slot], patch(to_y, z))

    def cw_other(r, mask):
        ref = cw_ref(around[r], mask)
        return remote(ref, ref, s_cws.at[r], r_cws.at[r], sibling)

    def ct_copy(src_y, to_y, slot):
        ref = cw.at[5 + x, src_y, :, half]
        return remote(ref, ref, s_ct.at[slot], r_ct.at[slot], patch(to_y, z))

    def cx_copy(r, d):
        ref = cw.at[5 + x, around[r], :, half]
        return remote(ref, ref, s_cx.at[r, d], r_cx.at[r, d], across(d))

    def cx_from(r, d):
        ref = cw.at[5 + (x + 4 - d) % 4, around[r], :, half]
        return remote(ref, ref, s_cx.at[r, d], r_cx.at[r, d], across(d))

    def ct_other(r, mask):
        ref = cw.at[5:9, around[r], :, mask]
        return remote(ref, ref, s_cts.at[r], r_cts.at[r], sibling)

    send(lambda: ct_copy(y, up, 0))
    send(lambda: ct_copy(y, down, 1))

    for copy in loc[2:]:
        copy.wait()
    carrier = x < 3
    diagonal = y == z
    turn = (y - z + 4) % 4

    def qa_rows(k):
        return wqkv.at[x, pl.ds(pl.multiple_of(CB * k, 16), CB), half]

    def qa_copy(k):
        return remote(wown.at[x, :, half], qa_rows(k), s_qa.at[0], r_qa.at[k], patch(y, y))

    def qa_local():
        return pltpu.make_async_copy(wown.at[x, :, half], qa_rows(z), l_qa.at[0])

    def qb_copy(to_y, slot):
        ref = wqkv.at[x, :, half]
        return remote(ref, ref, s_qb.at[slot], r_qb.at[0], patch(to_y, z))

    def qc_copy(d):
        ref = wqkv.at[x, :, half]
        return remote(ref, ref, s_qc.at[d], r_qc.at[d], across(d))

    def qc_from(d):
        ref = wqkv.at[(x + 4 - d) % 4, :, half]
        return remote(ref, ref, s_qc.at[d], r_qc.at[d], across(d))

    def qd_other(m, mask):
        ref = wqkv.at[m, :, mask]
        return remote(ref, ref, s_qd.at[m], r_qd.at[m], sibling)

    def spread_q(cond):
        for d in range(1, 4):
            send(lambda d=d: qc_copy(d), carrier & cond)

    send(lambda: qa_copy(z), carrier & (z != y))
    when(carrier & diagonal, lambda: qa_local().start())
    send(lambda: cw_copy(y, up, 0))
    send(lambda: cw_copy(y, down, 1))

    def service_1():
        ct_copy(down, y, 0).wait_recv()
        send(lambda: ct_copy(down, up, 2), c == 0)
        ct_copy(up, y, 1).wait_recv()
        send(lambda: ct_copy(up, down, 2), c == 1)
        for r in range(2):
            for d in range(1, 4):
                send(lambda r=r, d=d: cx_copy(r, d))
        for k in range(4):
            when(carrier & diagonal & (z != k), lambda k=k: qa_copy(k).wait_recv())
        when(carrier & diagonal, lambda: qa_local().wait())
        send(lambda: qb_copy(up, 0), carrier & diagonal)
        send(lambda: qb_copy(down, 1), carrier & diagonal)
        spread_q(diagonal)

    def service_2():
        ct_copy(opposite, y, 2).wait_recv()
        for d in range(1, 4):
            send(lambda d=d: cx_copy(2, d))
        cw_copy(down, y, 0).wait_recv()
        send(lambda: cw_copy(down, up, 2), c == 0)
        cw_copy(up, y, 1).wait_recv()
        send(lambda: cw_copy(up, down, 2), c == 1)
        for r in range(2):
            send(lambda r=r: cw_other(r, half))

    def service_3():
        beside = (turn == 1) | (turn == 3)
        when(carrier & beside, lambda: qb_copy(up, 0).wait_recv())
        send(lambda: qb_copy(up, 2), carrier & (turn == 1) & (c == 0))
        send(lambda: qb_copy(down, 2), carrier & (turn == 3) & (c == 1))
        spread_q(beside)

    services = {1: service_1, 2: service_2, 3: service_3}

    gi = lax.broadcasted_iota(jnp.int32, (C, 128), 0) - GROUP * lax.broadcasted_iota(jnp.int32, (C, 128), 1)
    gmat[...] = jnp.where((gi >= 0) & (gi < GROUP), 1.0, 0.0).astype(BF16)
    ti = lax.broadcasted_iota(jnp.int32, (128, C), 1) - GROUP * lax.broadcasted_iota(jnp.int32, (128, C), 0)
    gmat_t[...] = jnp.where((ti >= 0) & (ti < GROUP), 1.0, 0.0).astype(BF16)
    for yy in range(4):
        rows = lax.broadcasted_iota(jnp.int32, (CZ, CZ), 0) - CB * z
        cols = lax.broadcasted_iota(jnp.int32, (CZ, CZ), 1) - CB * yy
        hit = (rows == cols) & (cols >= 0) & (cols < CB)
        sel[CZ * yy : CZ * yy + CZ, :] = jnp.where(hit, 1.0, 0.0).astype(BF16)

    def split_rows(x):
        hi = x.astype(BF16).astype(F32)
        mid = (x - hi).astype(BF16).astype(F32)
        return jnp.concatenate([hi, mid, x - hi - mid], axis=0).astype(BF16)

    def join_rows(x):
        return x[0:8] + x[8:16] + x[16:24]

    def group_sums(x):
        n = x.shape[1]
        sums = join_rows(dot_nn(split_rows(x), gmat[0:n, :]))
        return join_rows(dot_nn(split_rows(sums), gmat_t[:, 0:n]))

    for d in range(1, 16):
        q = (p + 16 - d) % 16
        remote(st1s, st1.at[q], s_st1.at[d], r_st1.at[d], {"batch": b, "patch": q}).wait_recv()
    means = st1[:, 0:16, :]
    mean_c = jnp.sum(means, axis=0) * (1.0 / 16)
    m2_c = jnp.sum(st1[:, 16:32, :], axis=0) + BLK * jnp.sum(jnp.square(means - mean_c[None]), axis=0)

    def to_lanes(x, n):
        full = jnp.concatenate([x[j : j + 1, :] for j in range(n)], axis=1)
        return full

    mean_l = jnp.broadcast_to(to_lanes(mean_c, 10), (8, C))
    m2_l = jnp.broadcast_to(to_lanes(m2_c, 10), (8, C))
    centre = group_sums(mean_l) * (1.0 / GROUP)
    spread = group_sums(m2_l + 2048.0 * jnp.square(mean_l - centre)) * (1.0 / (2048 * GROUP))
    gn1[0] = centre
    gn1[1] = lax.rsqrt(spread + EPS)

    def activate(start, count):
        def body(i, carry):
            rows = pl.ds(pl.multiple_of(start + 16 * i, 16), 16)
            v = lat[rows].astype(F32)
            v = (v - gn1[0, 0:1, :]) * gn1[1, 0:1, :]
            act[rows] = (v / (1.0 + jnp.exp(-v))).astype(BF16)
            return carry

        lax.fori_loop(0, count // 16, body, 0)

    activate(64 + BLK * z, BLK)

    def halo_up():
        return remote(
            lat.at[pl.ds(512, 64)], lat.at[pl.ds(0, 64)], s_halo.at[0], r_halo.at[0], patch(y + 1, z)
        )

    def halo_down():
        return remote(
            lat.at[pl.ds(64, 64)], lat.at[pl.ds(576, 64)], s_halo.at[1], r_halo.at[1], patch(y - 1, z)
        )

    send(halo_up, (z == 3) & (y < 3))
    send(halo_down, (z == 0) & (y > 0))
    for k in range(1, 4):
        def below(k=k):
            lat_copy(z - k, 0).wait_recv()

        def above(k=k):
            lat_copy(z + k, 1).wait_recv()

        when(z - k >= 0, below)
        send(lambda k=k: lat_copy(z - k, 0), (z - k >= 0) & (z < 3))
        when(z + k <= 3, above)
        send(lambda k=k: lat_copy(z + k, 1), (z + k <= 3) & (z > 0))
        send(halo_up, (z + k == 3) & (y < 3))
        send(halo_down, (z - k == 0) & (y > 0))
        services[k]()
        when(z - k >= 0, lambda k=k: activate(64 + BLK * (z - k), BLK))
        when(z + k <= 3, lambda k=k: activate(64 + BLK * (z + k), BLK))

    def wo_z(k, way):
        zz = z + 1 if way == 0 else z - 1
        ref = wo.at[4 * y + k, :, half]
        return remote(ref, ref, s_woz.at[way, k], r_woz.at[k], patch(y, zz))

    send(lambda: wo_z(z, 0), z < 3)
    send(lambda: wo_z(z, 1), z > 0)

    when(y > 0, lambda: halo_up().wait_recv())
    when(y > 0, lambda: activate(0, 64))
    when(y < 3, lambda: halo_down().wait_recv())
    when(y < 3, lambda: activate(576, 64))

    def zero_top():
        act[0:64] = jnp.zeros((64, C), BF16)

    def zero_bottom():
        act[576:640] = jnp.zeros((64, C), BF16)

    when(y == 0, zero_top)
    when(y == 3, zero_bottom)

    cw_copy(opposite, y, 2).wait_recv()
    send(lambda: cw_other(2, half))
    for r in range(3):
        for d in range(1, 4):
            cx_from(r, d).wait_recv()
        send(lambda r=r: ct_other(r, half))
    when(carrier & (turn == 2), lambda: qb_copy(up, 0).wait_recv())
    spread_q(turn == 2)
    for r in range(3):
        cw_other(r, other).wait_recv()
        ct_other(r, other).wait_recv()

    bias = jnp.concatenate([st1[4 * yy + z, 15:16, 0:CB] for yy in range(4)], axis=1)
    CHUNK = 256

    def conv_chunk(j, carry):
        total = jnp.zeros((CHUNK, 3 * CZ), F32)
        for dr in range(3):
            rows = pl.ds(pl.multiple_of(CHUNK * j + 64 * dr, 64), CHUNK)
            total = total + dot_nt(act[rows], cw[3 * dr : 3 * dr + 3].reshape(3 * CZ, C))
        ubuf[...] = total
        column = lax.broadcasted_iota(jnp.int32, (CHUNK, CZ), 0) % 64
        left = pltpu.roll(ubuf[:, 0:CZ], 1, 0)
        right = pltpu.roll(ubuf[:, 2 * CZ : 3 * CZ], CHUNK - 1, 0)
        value = ubuf[:, CZ : 2 * CZ]
        value = value + jnp.where(column == 0, 0.0, left) + jnp.where(column == 63, 0.0, right)
        own = lat[pl.ds(pl.multiple_of(64 + CHUNK * j, 64), CHUNK)]
        value = value + dot_nn(own, sel[...]) + bias
        hidg[z, pl.ds(pl.multiple_of(CHUNK * j, 128), CHUNK), :] = value.astype(BF16)
        return carry

    lax.fori_loop(0, ROWS_Y // CHUNK, conv_chunk, 0)

    def hid_copy(k, way):
        zz = z + 1 if way == 0 else z - 1
        return remote(hidg.at[k], hidg.at[k], s_hid.at[way, k], r_hid.at[k], patch(y, zz))

    send(lambda: hid_copy(z, 0), z < 3)
    send(lambda: hid_copy(z, 1), z > 0)

    st2s[...] = jnp.zeros_like(st2s)
    hidden = hidg[z].astype(F32)
    mean = jnp.sum(hidden, axis=0, keepdims=True) * (1.0 / ROWS_Y)
    m2 = jnp.sum(jnp.square(hidden - mean), axis=0, keepdims=True)
    for j in range(3):
        width = min(128, CZ - 128 * j)
        st2s[j : j + 1, 0:width] = mean[:, 128 * j : 128 * j + width]
        st2s[4 + j : 5 + j, 0:width] = m2[:, 128 * j : 128 * j + width]
    for d in range(1, 16):
        send(
            lambda d=d: remote(
                st2s, st2.at[p], s_st2.at[d], r_st2.at[d], {"batch": b, "patch": (p + d) % 16}
            )
        )
    st2[p] = st2s[...]

    for k in range(1, 4):
        when(z - k >= 0, lambda k=k: wo_z(z - k, 0).wait_recv())
        send(lambda k=k: wo_z(z - k, 0), (z - k >= 0) & (z < 3))
        when(z + k <= 3, lambda k=k: wo_z(z + k, 1).wait_recv())
        send(lambda k=k: wo_z(z + k, 1), (z + k <= 3) & (z > 0))

    def wo_row(src_y, mask):
        return wo.at[pl.ds(4 * src_y, 4), :, mask]

    def wo_y(src_y, to_y, slot):
        ref = wo_row(src_y, half)
        return remote(ref, ref, s_woy.at[slot], r_woy.at[slot], patch(to_y, z))

    send(lambda: wo_y(y, up, 0))
    send(lambda: wo_y(y, down, 1))
    for d in range(1, 4):
        when((x + 4 - d) % 4 < 3, lambda d=d: qc_from(d).wait_recv())
    for m in range(3):
        send(lambda m=m: qd_other(m, half))

    for d in range(1, 16):
        q = (p + 16 - d) % 16
        remote(st2s, st2.at[q], s_st2.at[d], r_st2.at[d], {"batch": b, "patch": q}).wait_recv()
    parts = [[st2[4 * yy + zz] for zz in range(4)] for yy in range(4)]
    mean_rows, m2_rows = [], []
    for zz in range(4):
        col = [parts[yy][zz] for yy in range(4)]
        m = (col[0] + col[1] + col[2] + col[3]) * 0.25
        dev = sum(jnp.square(x - m) for x in col)
        total = col[0] + col[1] + col[2] + col[3]
        m2_all = total[4:8] + ROWS_Y * dev[0:4]
        mean_rows.append(to_lanes(m, 3)[:, 0:CZ])
        m2_rows.append(to_lanes(m2_all, 3)[:, 0:CZ])
    mean_l = jnp.concatenate(mean_rows + mean_rows, axis=0)
    m2_l = jnp.concatenate(m2_rows + m2_rows, axis=0)
    centre = group_sums(mean_l) * (1.0 / GROUP)
    spread = group_sums(m2_l + 2048.0 * jnp.square(mean_l - centre)) * (1.0 / (2048 * GROUP))
    gn2[0] = centre
    gn2[1] = lax.rsqrt(spread + EPS)

    for k in range(1, 4):
        when(z - k >= 0, lambda k=k: hid_copy(z - k, 0).wait_recv())
        send(lambda k=k: hid_copy(z - k, 0), (z - k >= 0) & (z < 3))
        when(z + k <= 3, lambda k=k: hid_copy(z + k, 1).wait_recv())
        send(lambda k=k: hid_copy(z + k, 1), (z + k <= 3) & (z > 0))

    wo_y(down, y, 0).wait_recv()
    send(lambda: wo_y(down, up, 2), c == 0)
    wo_y(up, y, 1).wait_recv()
    send(lambda: wo_y(up, down, 2), c == 1)
    def normalize(i, carry):
        rows = pl.ds(pl.multiple_of(16 * i, 16), 16)
        blocks = [
            (hidg[zz, rows, :].astype(F32) - gn2[0, zz : zz + 1, :]) * gn2[1, zz : zz + 1, :]
            for zz in range(4)
        ]
        nrm[rows] = jnp.concatenate(
            [blocks[zz][:, CB * yy : CB * yy + CB] for yy in range(4) for zz in range(4)], axis=1
        ).astype(BF16)
        return carry

    lax.fori_loop(0, ROWS_Y // 16, normalize, 0)

    for m in range(3):
        qd_other(m, other).wait_recv()

    def project(j, carry):
        rows = pl.ds(pl.multiple_of(256 * j, 256), 256)
        block = nrm[rows]
        kv[0, y, rows, :] = dot_nt(block, wqkv[1]).astype(BF16)
        kv[1, y, rows, :] = dot_nt(block, wqkv[2]).astype(BF16)
        qb[rows] = (dot_nt(block, wqkv[0]).astype(BF16).astype(F32) * HEAD_DIM**-0.5).astype(BF16)
        return carry

    lax.fori_loop(0, ROWS_Y // 256, project, 0)

    def kv_copy(which, src_y, to_y, slot):
        ref = kv.at[which, src_y]
        return remote(ref, ref, s_kv.at[which, slot], r_kv.at[which, slot], patch(to_y, z))

    for which in range(2):
        send(lambda which=which: kv_copy(which, y, up, 0))
        send(lambda which=which: kv_copy(which, y, down, 1))

    def residual(i, carry):
        rows = pl.ds(pl.multiple_of(BLK * z + 16 * i, 16), 16)
        blocks = [hidg[zz, rows, :].astype(F32) for zz in range(4)]
        hnat[pl.ds(pl.multiple_of(16 * i, 16), 16)] = jnp.concatenate(
            [blocks[zz][:, CB * yy : CB * yy + CB] for yy in range(4) for zz in range(4)], axis=1
        )
        return carry

    lax.fori_loop(0, BLK // 16, residual, 0)

    wo_y(opposite, y, 2).wait_recv()

    def wo_forward(k):
        ref = wo_row(k, half)
        return remote(ref, ref, s_wos.at[k], r_wos.at[k], sibling)

    def wo_arrival(k):
        ref = wo_row(k, other)
        return remote(ref, ref, s_wos.at[k], r_wos.at[k], sibling)

    for k in range(4):
        send(lambda k=k: wo_forward(k))
    kv_copy(0, down, y, 0).wait_recv()
    send(lambda: kv_copy(0, down, up, 2))
    kv_copy(1, up, y, 1).wait_recv()
    send(lambda: kv_copy(1, up, down, 2))

    kv_copy(1, down, y, 0).wait_recv()
    kv_copy(0, up, y, 1).wait_recv()
    kv_copy(0, opposite, y, 2).wait_recv()
    kv_copy(1, opposite, y, 2).wait_recv()

    def att_copy(j):
        return remote(att.at[j], attg.at[z], s_att.at[j], r_att.at[z], patch(y, j))

    def att_from(k):
        return remote(att.at[k], attg.at[k], s_att.at[k], r_att.at[k], patch(y, k))

    def attend(j):
        rows = pl.ds(pl.multiple_of(BLK * j, 128), BLK)
        for pair in range(3):
            width = min(128, CZ - 128 * pair)
            lanes = slice(128 * pair, 128 * pair + width)
            query = qb[rows, lanes]
            keys = kv[0, :, :, lanes].reshape(2048, width)
            values = kv[1, :, :, lanes].reshape(2048, width)
            lane = lax.broadcasted_iota(jnp.int32, (BLK, width), 1)
            result = None
            for side in range(width // 64):
                q1 = query
                if width > 64:
                    keep = (lane >= 64 * side) & (lane < 64 * side + 64)
                    q1 = jnp.where(keep, query.astype(F32), 0.0).astype(BF16)
                scores = dot_nt(q1, keys)
                peak = jnp.max(scores, axis=1, keepdims=True)
                unnormalized = jnp.exp(scores - peak)
                row_total = jnp.sum(unnormalized, axis=1, keepdims=True)
                mix = dot_nn(unnormalized.astype(BF16), values) / row_total
                result = mix if result is None else jnp.where(lane < 64, result, mix)
            att[j, :, lanes] = result.astype(BF16)

    def attend_step(t, carry):
        j = (z + 1 + t) % 4
        attend(j)
        pl.when(t < 3)(lambda: att_copy(j).start())
        return carry

    lax.fori_loop(0, 4, attend_step, 0)
    attg[z] = att[z]
    for k in range(4):
        pending.append((z != k, lambda k=k: att_copy(k)))

    for k in range(4):
        wo_arrival(k).wait_recv()
    for k in range(4):
        when(z != k, lambda k=k: att_from(k).wait_recv())

    whole = jnp.concatenate([attg[k].astype(F32) for k in range(4)], axis=1).astype(BF16)
    out_ref[...] = (hnat[...] + dot_nt(whole, wo[...].reshape(C, C))).astype(BF16)

    for cond, make in pending:
        when(cond, lambda make=make: make().wait_send())


def on_device(latent, conv_weight, channel_bias, w_query, w_key, w_value, w_out):
    any_space = pl.BlockSpec(memory_space=pl.ANY)
    vmem = pl.BlockSpec(memory_space=pltpu.VMEM)
    dma = pltpu.SemaphoreType.DMA
    out = pl.pallas_call(
        kernel,
        out_shape=jax.ShapeDtypeStruct((BLK, C), BF16),
        in_specs=[any_space, any_space, vmem, any_space, any_space, any_space, any_space],
        out_specs=vmem,
        scratch_shapes=[
            pltpu.VMEM((640, C), BF16),
            pltpu.VMEM((640, C), BF16),
            pltpu.VMEM((9, 4, CB, C), BF16),
            pltpu.VMEM((4, CB, C), BF16),
            pltpu.VMEM((3, CZ, C), BF16),
            pltpu.VMEM((16, CB, C), BF16),
            pltpu.VMEM((32, 128), F32),
            pltpu.VMEM((16, 32, 128), F32),
            pltpu.VMEM((8, 128), F32),
            pltpu.VMEM((16, 8, 128), F32),
            pltpu.VMEM((C, 128), BF16),
            pltpu.VMEM((128, C), BF16),
            pltpu.VMEM((C, CZ), BF16),
            pltpu.VMEM((2, 8, C), F32),
            pltpu.VMEM((2, 8, CZ), F32),
            pltpu.VMEM((256, 3 * CZ), F32),
            pltpu.VMEM((4, ROWS_Y, CZ), BF16),
            pltpu.VMEM((ROWS_Y, C), BF16),
            pltpu.VMEM((BLK, C), F32),
            pltpu.VMEM((ROWS_Y, CZ), BF16),
            pltpu.VMEM((2, 4, ROWS_Y, CZ), BF16),
            pltpu.VMEM((4, BLK, CZ), BF16),
            pltpu.VMEM((4, BLK, CZ), BF16),
            dma((7,)), dma((16,)), dma((16,)), dma((2, 4)), dma((4,)), dma((2,)), dma((2,)),
            dma((3,)), dma((3,)), dma((3,)), dma((3,)),
            dma((3,)), dma((3,)), dma((3, 4)), dma((3, 4)), dma((3,)), dma((3,)),
            dma((1,)), dma((4,)), dma((1,)), dma((3,)), dma((1,)), dma((4,)), dma((4,)), dma((3,)), dma((3,)),
            dma((2, 4)), dma((4,)), dma((3,)), dma((3,)), dma((4,)), dma((4,)),
            dma((16,)), dma((16,)), dma((2, 4)), dma((4,)), dma((2, 3)), dma((2, 3)), dma((4,)), dma((4,)),
        ],
        compiler_params=pltpu.CompilerParams(
            collective_id=0, has_side_effects=True, vmem_limit_bytes=60 * 1024 * 1024
        ),
    )(
        latent.reshape(BLK, C), conv_weight.reshape(9, CB, C), channel_bias.reshape(1, CB), w_query, w_key, w_value, w_out
    )
    return out.reshape(latent.shape)


def solution(mesh):
    return jax.shard_map(
        on_device,
        mesh=mesh,
        in_specs=(
            P(("batch", "patch"), None, None),
            P(None, None, "patch", None),
            P("patch"),
            P("patch", None),
            P("patch", None),
            P("patch", None),
            P("patch", None),
        ),
        out_specs=P(("batch", "patch"), None, None),
        check_vma=False,
    )
```

```python
import jax
import jax.numpy as jnp
from jax import lax
from jax.experimental import pallas as pl
from jax.experimental.pallas import tpu as pltpu
from jax.sharding import PartitionSpec as P

C = 1280
HEADS = 20
HEAD_DIM = 64
GROUPS = 32
GROUP = C // GROUPS
NY, NZ = 4, 4
BLK = 128
ROWS_Y = 512
NCH = 4
R = ROWS_Y // NCH
HALF = R // 2
AHEAD = 1
CB = C // 16
CZ = C // 4
EPS = 1e-05
MESH = pl.DeviceIdType.MESH
F32 = jnp.float32
BF16 = jnp.bfloat16


def dot_nt(left, right):
    return lax.dot_general(left, right, (((1,), (1,)), ((), ())), preferred_element_type=F32)


def dot_nn(left, right):
    return lax.dot_general(left, right, (((1,), (0,)), ((), ())), preferred_element_type=F32)


def kernel(
    lat_in, cw_in, bias_in, wq_in, wk_in, wv_in, wo_in, out_ref,
    lat, act, cw, wown, wqkv, wo, st1s, st1, st2s, st2, gmat, gmat_t, sel,
    gn1, gn2, stc, ubuf, hidg, nrm, hnat, qb, kv, att, attg,
    s_loc, s_st1, r_st1, s_lat, r_lat, s_halo, r_halo, s_cw, r_cw, s_cws, r_cws,
    s_ct, r_ct, s_cx, r_cx, s_cts, r_cts,
    s_qa, r_qa, l_qa, s_qb, r_qb, s_qc, r_qc, s_qd, r_qd, s_woz, r_woz, s_woy, r_woy, s_wos, r_wos,
    s_st2, r_st2, s_hid, r_hid, s_kv, r_kv, s_att, r_att,
):
    p = lax.axis_index("patch")
    b = lax.axis_index("batch")
    y = p // 4
    z = p % 4
    c = b % 2
    x = (b // 2) % 4
    sib = b + 1 - 2 * c
    up = (y + 1) % 4
    down = (y + 3) % 4
    opposite = (y + 2) % 4
    half = pl.ds(pl.multiple_of(c * (C // 2), 128), C // 2)
    other = pl.ds(pl.multiple_of((1 - c) * (C // 2), 128), C // 2)
    pending = []

    def patch(yy, zz):
        return {"batch": b, "patch": 4 * yy + zz}

    def across(d):
        return {"batch": b - 2 * x + 2 * ((x + d) % 4), "patch": p}

    sibling = {"batch": sib, "patch": p}

    def remote(src, dst, ssem, rsem, dev):
        return pltpu.make_async_remote_copy(
            src_ref=src, dst_ref=dst, send_sem=ssem, recv_sem=rsem, device_id=dev, device_id_type=MESH
        )

    def when(cond, f):
        if cond is None:
            f()
        else:
            pl.when(cond)(f)

    def send(make, cond=None):
        when(cond, lambda: make().start())
        pending.append((cond, make))

    own_rows = pl.ds(pl.multiple_of(64 + BLK * z, 64), BLK)
    loc = [
        pltpu.make_async_copy(lat_in, lat.at[own_rows], s_loc.at[0]),
        pltpu.make_async_copy(cw_in, cw.at[:, y], s_loc.at[1]),
        pltpu.make_async_copy(wq_in, wown.at[0], s_loc.at[2]),
        pltpu.make_async_copy(wk_in, wown.at[1], s_loc.at[3]),
        pltpu.make_async_copy(wv_in, wown.at[2], s_loc.at[4]),
        pltpu.make_async_copy(wo_in, wown.at[3], s_loc.at[5]),
        pltpu.make_async_copy(wo_in.at[:, half], wo.at[p, :, half], s_loc.at[6]),
    ]
    for copy in loc:
        copy.start()
    barrier = pltpu.get_barrier_semaphore()
    for d in range(1, 16):
        pl.semaphore_signal(
            barrier, inc=1, device_id={"batch": b, "patch": (p + d) % 16}, device_id_type=MESH
        )
    pl.semaphore_signal(barrier, inc=1, device_id=sibling, device_id_type=MESH)
    for d in range(1, 4):
        pl.semaphore_signal(barrier, inc=1, device_id=across(d), device_id_type=MESH)

    st1s[...] = jnp.zeros_like(st1s)
    loc[0].wait()
    mine = lat[own_rows].astype(F32)
    mean = jnp.sum(mine, axis=0, keepdims=True) * (1.0 / BLK)
    m2 = jnp.sum(jnp.square(mine - mean), axis=0, keepdims=True)
    for j in range(10):
        st1s[j : j + 1, :] = mean[:, 128 * j : 128 * j + 128]
        st1s[16 + j : 17 + j, :] = m2[:, 128 * j : 128 * j + 128]
    st1s[15:16, 0:CB] = bias_in[...]

    pl.semaphore_wait(barrier, 19)

    for d in range(1, 16):
        send(
            lambda d=d: remote(
                st1s, st1.at[p], s_st1.at[d], r_st1.at[d], {"batch": b, "patch": (p + d) % 16}
            )
        )
    st1[p] = st1s[...]

    def lat_rows(k):
        return lat.at[pl.ds(pl.multiple_of(64 + BLK * k, 64), BLK)]

    def lat_copy(k, way):
        zz = z + 1 if way == 0 else z - 1
        return remote(lat_rows(k), lat_rows(k), s_lat.at[way, k], r_lat.at[k], patch(y, zz))

    send(lambda: lat_copy(z, 0), z < 3)
    send(lambda: lat_copy(z, 1), z > 0)

    loc[1].wait()
    around = (down, up, opposite)

    def cw_ref(src_y, mask):
        return cw.at[0:5, src_y, :, mask]

    def cw_copy(src_y, to_y, slot):
        ref = cw_ref(src_y, half)
        return remote(ref, ref, s_cw.at[slot], r_cw.at[slot], patch(to_y, z))

    def cw_other(r, mask):
        ref = cw_ref(around[r], mask)
        return remote(ref, ref, s_cws.at[r], r_cws.at[r], sibling)

    def ct_copy(src_y, to_y, slot):
        ref = cw.at[5 + x, src_y, :, half]
        return remote(ref, ref, s_ct.at[slot], r_ct.at[slot], patch(to_y, z))

    def cx_copy(r, d):
        ref = cw.at[5 + x, around[r], :, half]
        return remote(ref, ref, s_cx.at[r, d], r_cx.at[r, d], across(d))

    def cx_from(r, d):
        ref = cw.at[5 + (x + 4 - d) % 4, around[r], :, half]
        return remote(ref, ref, s_cx.at[r, d], r_cx.at[r, d], across(d))

    def ct_other(r, mask):
        ref = cw.at[5:9, around[r], :, mask]
        return remote(ref, ref, s_cts.at[r], r_cts.at[r], sibling)

    send(lambda: ct_copy(y, up, 0))
    send(lambda: ct_copy(y, down, 1))

    for copy in loc[2:]:
        copy.wait()
    carrier = x < 3
    diagonal = y == z
    turn = (y - z + 4) % 4

    def qa_rows(k):
        return wqkv.at[x, pl.ds(pl.multiple_of(CB * k, 16), CB), half]

    def qa_copy(k):
        return remote(wown.at[x, :, half], qa_rows(k), s_qa.at[0], r_qa.at[k], patch(y, y))

    def qa_local():
        return pltpu.make_async_copy(wown.at[x, :, half], qa_rows(z), l_qa.at[0])

    def qb_copy(to_y, slot):
        ref = wqkv.at[x, :, half]
        return remote(ref, ref, s_qb.at[slot], r_qb.at[0], patch(to_y, z))

    def qc_copy(d):
        ref = wqkv.at[x, :, half]
        return remote(ref, ref, s_qc.at[d], r_qc.at[d], across(d))

    def qc_from(d):
        ref = wqkv.at[(x + 4 - d) % 4, :, half]
        return remote(ref, ref, s_qc.at[d], r_qc.at[d], across(d))

    def qd_other(m, mask):
        ref = wqkv.at[m, :, mask]
        return remote(ref, ref, s_qd.at[m], r_qd.at[m], sibling)

    def spread_q(cond):
        for d in range(1, 4):
            send(lambda d=d: qc_copy(d), carrier & cond)

    send(lambda: qa_copy(z), carrier & (z != y))
    when(carrier & diagonal, lambda: qa_local().start())
    send(lambda: cw_copy(y, up, 0))
    send(lambda: cw_copy(y, down, 1))

    def service_1():
        ct_copy(down, y, 0).wait_recv()
        send(lambda: ct_copy(down, up, 2), c == 0)
        ct_copy(up, y, 1).wait_recv()
        send(lambda: ct_copy(up, down, 2), c == 1)
        for r in range(2):
            for d in range(1, 4):
                send(lambda r=r, d=d: cx_copy(r, d))
        for k in range(4):
            when(carrier & diagonal & (z != k), lambda k=k: qa_copy(k).wait_recv())
        when(carrier & diagonal, lambda: qa_local().wait())
        send(lambda: qb_copy(up, 0), carrier & diagonal)
        send(lambda: qb_copy(down, 1), carrier & diagonal)
        spread_q(diagonal)

    def service_2():
        ct_copy(opposite, y, 2).wait_recv()
        for d in range(1, 4):
            send(lambda d=d: cx_copy(2, d))
        cw_copy(down, y, 0).wait_recv()
        send(lambda: cw_copy(down, up, 2), c == 0)
        cw_copy(up, y, 1).wait_recv()
        send(lambda: cw_copy(up, down, 2), c == 1)
        for r in range(2):
            send(lambda r=r: cw_other(r, half))

    def service_3():
        beside = (turn == 1) | (turn == 3)
        when(carrier & beside, lambda: qb_copy(up, 0).wait_recv())
        send(lambda: qb_copy(up, 2), carrier & (turn == 1) & (c == 0))
        send(lambda: qb_copy(down, 2), carrier & (turn == 3) & (c == 1))
        spread_q(beside)

    services = {1: service_1, 2: service_2, 3: service_3}

    gi = lax.broadcasted_iota(jnp.int32, (C, 128), 0) - GROUP * lax.broadcasted_iota(jnp.int32, (C, 128), 1)
    gmat[...] = jnp.where((gi >= 0) & (gi < GROUP), 1.0, 0.0).astype(BF16)
    ti = lax.broadcasted_iota(jnp.int32, (128, C), 1) - GROUP * lax.broadcasted_iota(jnp.int32, (128, C), 0)
    gmat_t[...] = jnp.where((ti >= 0) & (ti < GROUP), 1.0, 0.0).astype(BF16)
    for yy in range(4):
        rows = lax.broadcasted_iota(jnp.int32, (CZ, CZ), 0) - CB * z
        cols = lax.broadcasted_iota(jnp.int32, (CZ, CZ), 1) - CB * yy
        hit = (rows == cols) & (cols >= 0) & (cols < CB)
        sel[CZ * yy : CZ * yy + CZ, :] = jnp.where(hit, 1.0, 0.0).astype(BF16)

    def split_rows(x):
        hi = x.astype(BF16).astype(F32)
        mid = (x - hi).astype(BF16).astype(F32)
        return jnp.concatenate([hi, mid, x - hi - mid], axis=0).astype(BF16)

    def join_rows(x):
        return x[0:8] + x[8:16] + x[16:24]

    def group_sums(x):
        n = x.shape[1]
        sums = join_rows(dot_nn(split_rows(x), gmat[0:n, :]))
        return join_rows(dot_nn(split_rows(sums), gmat_t[:, 0:n]))

    for d in range(1, 16):
        q = (p + 16 - d) % 16
        remote(st1s, st1.at[q], s_st1.at[d], r_st1.at[d], {"batch": b, "patch": q}).wait_recv()
    means = st1[:, 0:16, :]
    mean_c = jnp.sum(means, axis=0) * (1.0 / 16)
    m2_c = jnp.sum(st1[:, 16:32, :], axis=0) + BLK * jnp.sum(jnp.square(means - mean_c[None]), axis=0)

    def to_lanes(x, n):
        full = jnp.concatenate([x[j : j + 1, :] for j in range(n)], axis=1)
        return full

    mean_l = jnp.broadcast_to(to_lanes(mean_c, 10), (8, C))
    m2_l = jnp.broadcast_to(to_lanes(m2_c, 10), (8, C))
    centre = group_sums(mean_l) * (1.0 / GROUP)
    spread = group_sums(m2_l + 2048.0 * jnp.square(mean_l - centre)) * (1.0 / (2048 * GROUP))
    gn1[0] = centre
    gn1[1] = lax.rsqrt(spread + EPS)

    def activate(start, count):
        def body(i, carry):
            rows = pl.ds(pl.multiple_of(start + 16 * i, 16), 16)
            v = lat[rows].astype(F32)
            v = (v - gn1[0, 0:1, :]) * gn1[1, 0:1, :]
            act[rows] = (v / (1.0 + jnp.exp(-v))).astype(BF16)
            return carry

        lax.fori_loop(0, count // 16, body, 0)

    activate(64 + BLK * z, BLK)

    def halo_up():
        return remote(
            lat.at[pl.ds(512, 64)], lat.at[pl.ds(0, 64)], s_halo.at[0], r_halo.at[0], patch(y + 1, z)
        )

    def halo_down():
        return remote(
            lat.at[pl.ds(64, 64)], lat.at[pl.ds(576, 64)], s_halo.at[1], r_halo.at[1], patch(y - 1, z)
        )

    send(halo_up, (z == 3) & (y < 3))
    send(halo_down, (z == 0) & (y > 0))
    for k in range(1, 4):
        def below(k=k):
            lat_copy(z - k, 0).wait_recv()

        def above(k=k):
            lat_copy(z + k, 1).wait_recv()

        when(z - k >= 0, below)
        send(lambda k=k: lat_copy(z - k, 0), (z - k >= 0) & (z < 3))
        when(z + k <= 3, above)
        send(lambda k=k: lat_copy(z + k, 1), (z + k <= 3) & (z > 0))
        send(halo_up, (z + k == 3) & (y < 3))
        send(halo_down, (z - k == 0) & (y > 0))
        services[k]()
        when(z - k >= 0, lambda k=k: activate(64 + BLK * (z - k), BLK))
        when(z + k <= 3, lambda k=k: activate(64 + BLK * (z + k), BLK))

    def wo_z(k, way):
        zz = z + 1 if way == 0 else z - 1
        ref = wo.at[4 * y + k, :, half]
        return remote(ref, ref, s_woz.at[way, k], r_woz.at[k], patch(y, zz))

    send(lambda: wo_z(z, 0), z < 3)
    send(lambda: wo_z(z, 1), z > 0)

    when(y > 0, lambda: halo_up().wait_recv())
    when(y > 0, lambda: activate(0, 64))
    when(y < 3, lambda: halo_down().wait_recv())
    when(y < 3, lambda: activate(576, 64))

    def zero_top():
        act[0:64] = jnp.zeros((64, C), BF16)

    def zero_bottom():
        act[576:640] = jnp.zeros((64, C), BF16)

    when(y == 0, zero_top)
    when(y == 3, zero_bottom)

    cw_copy(opposite, y, 2).wait_recv()
    send(lambda: cw_other(2, half))
    for r in range(3):
        for d in range(1, 4):
            cx_from(r, d).wait_recv()
        send(lambda r=r: ct_other(r, half))
    when(carrier & (turn == 2), lambda: qb_copy(up, 0).wait_recv())
    spread_q(turn == 2)
    for r in range(3):
        cw_other(r, other).wait_recv()
        ct_other(r, other).wait_recv()

    bias = jnp.concatenate([st1[4 * yy + z, 15:16, 0:CB] for yy in range(4)], axis=1)
    CHUNK = 256

    def conv_chunk(j, carry):
        total = jnp.zeros((CHUNK, 3 * CZ), F32)
        for dr in range(3):
            rows = pl.ds(pl.multiple_of(CHUNK * j + 64 * dr, 64), CHUNK)
            total = total + dot_nt(act[rows], cw[3 * dr : 3 * dr + 3].reshape(3 * CZ, C))
        ubuf[...] = total
        column = lax.broadcasted_iota(jnp.int32, (CHUNK, CZ), 0) % 64
        left = pltpu.roll(ubuf[:, 0:CZ], 1, 0)
        right = pltpu.roll(ubuf[:, 2 * CZ : 3 * CZ], CHUNK - 1, 0)
        value = ubuf[:, CZ : 2 * CZ]
        value = value + jnp.where(column == 0, 0.0, left) + jnp.where(column == 63, 0.0, right)
        own = lat[pl.ds(pl.multiple_of(64 + CHUNK * j, 64), CHUNK)]
        value = value + dot_nn(own, sel[...]) + bias
        value = value.astype(BF16).astype(F32)
        mean = jnp.sum(value, axis=0, keepdims=True) * (1.0 / CHUNK)
        stc[j, 0:1, :] = mean
        stc[j, 1:2, :] = jnp.sum(jnp.square(value - mean), axis=0, keepdims=True)
        for i in range(CHUNK // R):
            upper = value[R * i : R * i + HALF]
            lower = value[R * i + HALF : R * i + R]
            ch = (CHUNK // R) * j + i
            hidg[z, ch, 0] = upper[:, 0:128].astype(BF16)
            hidg[z, ch, 1] = upper[:, 128:256].astype(BF16)
            hidg[z, ch, 2] = lower[:, 0:128].astype(BF16)
            hidg[z, ch, 3] = lower[:, 128:256].astype(BF16)
            hidg[z, ch, 4] = jnp.concatenate([upper[:, 256:CZ], lower[:, 256:CZ]], axis=1).astype(BF16)
        return carry

    def hid_copy(ch, k, way):
        zz = z + 1 if way == 0 else z - 1
        ref = hidg.at[k, ch]
        return remote(ref, ref, s_hid.at[way, ch, k], r_hid.at[ch, k], patch(y, zz))

    def hid_own(ch):
        send(lambda: hid_copy(ch, z, 0), z < 3)
        send(lambda: hid_copy(ch, z, 1), z > 0)

    conv_chunk(0, 0)
    hid_own(0)
    conv_chunk(1, 0)

    st2s[...] = jnp.zeros_like(st2s)
    mean = 0.5 * (stc[0, 0:1, :] + stc[1, 0:1, :])
    m2 = stc[0, 1:2, :] + stc[1, 1:2, :]
    m2 = m2 + CHUNK * (jnp.square(stc[0, 0:1, :] - mean) + jnp.square(stc[1, 0:1, :] - mean))
    for j in range(3):
        width = min(128, CZ - 128 * j)
        st2s[j : j + 1, 0:width] = mean[:, 128 * j : 128 * j + width]
        st2s[4 + j : 5 + j, 0:width] = m2[:, 128 * j : 128 * j + width]
    for d in range(1, 16):
        send(
            lambda d=d: remote(
                st2s, st2.at[p], s_st2.at[d], r_st2.at[d], {"batch": b, "patch": (p + d) % 16}
            )
        )
    st2[p] = st2s[...]

    def wo_row(src_y, mask):
        return wo.at[pl.ds(4 * src_y, 4), :, mask]

    def wo_y(src_y, to_y, slot):
        ref = wo_row(src_y, half)
        return remote(ref, ref, s_woy.at[slot], r_woy.at[slot], patch(to_y, z))

    def weights_1():
        for k in range(1, 4):
            when(z - k >= 0, lambda k=k: wo_z(z - k, 0).wait_recv())
            send(lambda k=k: wo_z(z - k, 0), (z - k >= 0) & (z < 3))
            when(z + k <= 3, lambda k=k: wo_z(z + k, 1).wait_recv())
            send(lambda k=k: wo_z(z + k, 1), (z + k <= 3) & (z > 0))
        send(lambda: wo_y(y, up, 0))
        send(lambda: wo_y(y, down, 1))
        for d in range(1, 4):
            when((x + 4 - d) % 4 < 3, lambda d=d: qc_from(d).wait_recv())
        for m in range(3):
            send(lambda m=m: qd_other(m, half))

    def second_norm():
        for d in range(1, 16):
            q = (p + 16 - d) % 16
            remote(st2s, st2.at[q], s_st2.at[d], r_st2.at[d], {"batch": b, "patch": q}).wait_recv()
        parts = [[st2[4 * yy + zz] for zz in range(4)] for yy in range(4)]
        mean_rows, m2_rows = [], []
        for zz in range(4):
            col = [parts[yy][zz] for yy in range(4)]
            m = (col[0] + col[1] + col[2] + col[3]) * 0.25
            dev = sum(jnp.square(x - m) for x in col)
            total = col[0] + col[1] + col[2] + col[3]
            m2_all = total[4:8] + ROWS_Y * dev[0:4]
            mean_rows.append(to_lanes(m, 3)[:, 0:CZ])
            m2_rows.append(to_lanes(m2_all, 3)[:, 0:CZ])
        mean_l = jnp.concatenate(mean_rows + mean_rows, axis=0)
        m2_l = jnp.concatenate(m2_rows + m2_rows, axis=0)
        centre = group_sums(mean_l) * (1.0 / GROUP)
        spread = group_sums(m2_l + 2048.0 * jnp.square(mean_l - centre)) * (1.0 / (2048 * GROUP))
        gn2[0] = centre
        gn2[1] = lax.rsqrt(spread + EPS)

    def hidden_rows(zz, ch, h, rows):
        tail = hidg[zz, ch, 4, rows, :].astype(F32)[:, 64 * h : 64 * h + 64]
        return jnp.concatenate(
            [hidg[zz, ch, 2 * h, rows, :].astype(F32), hidg[zz, ch, 2 * h + 1, rows, :].astype(F32), tail],
            axis=1,
        )

    def in_order(blocks):
        return jnp.concatenate(
            [blocks[zz][:, CB * yy : CB * yy + CB] for yy in range(4) for zz in range(4)], axis=1
        )

    def normalize(ch):
        for h in range(2):
            def body(i, carry, h=h):
                rows = pl.ds(pl.multiple_of(16 * i, 16), 16)
                blocks = [
                    (hidden_rows(zz, ch, h, rows) - gn2[0, zz : zz + 1, :]) * gn2[1, zz : zz + 1, :]
                    for zz in range(4)
                ]
                nrm[pl.ds(pl.multiple_of(HALF * h + 16 * i, 16), 16)] = in_order(blocks).astype(BF16)
                return carry

            lax.fori_loop(0, HALF // 16, body, 0)

    def project(ch):
        rows = pl.ds(R * ch, R)
        both = dot_nt(nrm[...], wqkv[...].reshape(3 * CZ, C))
        kv[y, rows, 0:256] = both[:, CZ : CZ + 256].astype(BF16)
        kv[y, rows, 256:512] = both[:, 2 * CZ : 2 * CZ + 256].astype(BF16)
        kv[y, rows, 512:640] = jnp.concatenate(
            [both[:, CZ + 256 : 2 * CZ], both[:, 2 * CZ + 256 : 3 * CZ]], axis=1
        ).astype(BF16)
        query = (both[:, 0:CZ].astype(BF16).astype(F32) * HEAD_DIM**-0.5).astype(BF16)
        qb[rows, 0:256] = query[:, 0:256]
        qb[rows, 256:384] = jnp.concatenate(
            [query[:, 256:CZ].astype(F32), jnp.zeros((R, 64), F32)], axis=1
        ).astype(BF16)

    def kv_copy(ch, h, src_y, to_y, slot):
        ref = kv.at[src_y, pl.ds(R * ch + HALF * h, HALF), :]
        return remote(ref, ref, s_kv.at[ch, h, slot], r_kv.at[ch, h, slot], patch(to_y, z))

    def kv_own(ch):
        send(lambda: kv_copy(ch, 0, y, up, 0))
        send(lambda: kv_copy(ch, 1, y, down, 1))
        send(lambda: kv_copy(ch, 1, y, up, 0))
        send(lambda: kv_copy(ch, 0, y, down, 1))

    def kv_on(ch):
        kv_copy(ch, 0, down, y, 0).wait_recv()
        send(lambda: kv_copy(ch, 0, down, up, 2))
        kv_copy(ch, 1, up, y, 1).wait_recv()
        send(lambda: kv_copy(ch, 1, up, down, 2))

    for ch in range(NCH):
        for k in range(1, 4):
            when(z - k >= 0, lambda k=k, ch=ch: hid_copy(ch, z - k, 0).wait_recv())
            send(lambda k=k, ch=ch: hid_copy(ch, z - k, 0), (z - k >= 0) & (z < 3))
            when(z + k <= 3, lambda k=k, ch=ch: hid_copy(ch, z + k, 1).wait_recv())
            send(lambda k=k, ch=ch: hid_copy(ch, z + k, 1), (z + k <= 3) & (z > 0))
            if k == AHEAD and ch + 1 < NCH:
                hid_own(ch + 1)
            if ch == 0 and k == 2:
                weights_1()
        if ch == 0:
            second_norm()
            for m in range(3):
                qd_other(m, other).wait_recv()
        if ch == 1:
            wo_y(down, y, 0).wait_recv()
            send(lambda: wo_y(down, up, 2), c == 0)
            wo_y(up, y, 1).wait_recv()
            send(lambda: wo_y(up, down, 2), c == 1)
        normalize(ch)
        project(ch)
        kv_own(ch)
        if ch > 0:
            kv_on(ch - 1)

    for h in range(2):
        def residual(i, carry, h=h):
            rows = pl.ds(pl.multiple_of(16 * i, 16), 16)
            blocks = [hidden_rows(zz, z, h, rows) for zz in range(4)]
            hnat[pl.ds(pl.multiple_of(HALF * h + 16 * i, 16), 16)] = in_order(blocks)
            return carry

        lax.fori_loop(0, HALF // 16, residual, 0)

    kv_on(NCH - 1)
    wo_y(opposite, y, 2).wait_recv()

    def wo_forward(k):
        ref = wo_row(k, half)
        return remote(ref, ref, s_wos.at[k], r_wos.at[k], sibling)

    def wo_arrival(k):
        ref = wo_row(k, other)
        return remote(ref, ref, s_wos.at[k], r_wos.at[k], sibling)

    for k in range(4):
        send(lambda k=k: wo_forward(k))
    for ch in range(NCH):
        kv_copy(ch, 1, down, y, 0).wait_recv()
        kv_copy(ch, 0, up, y, 1).wait_recv()
        kv_copy(ch, 0, opposite, y, 2).wait_recv()
        kv_copy(ch, 1, opposite, y, 2).wait_recv()

    def att_copy(j):
        return remote(att.at[j], attg.at[z], s_att.at[j], r_att.at[z], patch(y, j))

    def att_from(k):
        return remote(att.at[k], attg.at[k], s_att.at[k], r_att.at[k], patch(y, k))

    def attend(j):
        rows = pl.ds(pl.multiple_of(BLK * j, 128), BLK)
        for pair in range(3):
            width = min(128, CZ - 128 * pair)
            lanes = slice(128 * pair, 128 * pair + width)
            query = qb[rows, 128 * pair : 128 * pair + 128]
            key_at = 128 * pair if pair < 2 else 512
            value_at = key_at + 256 if pair < 2 else 512
            keys = kv[:, :, key_at : key_at + 128].reshape(2048, 128)
            values = kv[:, :, value_at : value_at + 128].reshape(2048, 128)
            lane = lax.broadcasted_iota(jnp.int32, (BLK, 128), 1)
            result = None
            for side in range(width // 64):
                q1 = query
                if width > 64:
                    keep = (lane >= 64 * side) & (lane < 64 * side + 64)
                    q1 = jnp.where(keep, query.astype(F32), 0.0).astype(BF16)
                scores = dot_nt(q1, keys)
                peak = jnp.max(scores, axis=1, keepdims=True)
                unnormalized = jnp.exp(scores - peak)
                row_total = jnp.sum(unnormalized, axis=1, keepdims=True)
                mix = dot_nn(unnormalized.astype(BF16), values) / row_total
                result = mix if result is None else jnp.where(lane < 64, result, mix)
            if width == 64:
                result = result[:, 64:128]
            att[j, :, lanes] = result.astype(BF16)

    def attend_step(t, carry):
        j = (z + 1 + t) % 4
        attend(j)
        pl.when(t < 3)(lambda: att_copy(j).start())
        return carry

    lax.fori_loop(0, 4, attend_step, 0)
    attg[z] = att[z]
    for k in range(4):
        pending.append((z != k, lambda k=k: att_copy(k)))

    for k in range(4):
        wo_arrival(k).wait_recv()
    for k in range(4):
        when(z != k, lambda k=k: att_from(k).wait_recv())

    whole = jnp.concatenate([attg[k].astype(F32) for k in range(4)], axis=1).astype(BF16)
    out_ref[...] = (hnat[...] + dot_nt(whole, wo[...].reshape(C, C))).astype(BF16)

    for cond, make in pending:
        when(cond, lambda make=make: make().wait_send())


def on_device(latent, conv_weight, channel_bias, w_query, w_key, w_value, w_out):
    any_space = pl.BlockSpec(memory_space=pl.ANY)
    vmem = pl.BlockSpec(memory_space=pltpu.VMEM)
    dma = pltpu.SemaphoreType.DMA
    out = pl.pallas_call(
        kernel,
        out_shape=jax.ShapeDtypeStruct((BLK, C), BF16),
        in_specs=[any_space, any_space, vmem, any_space, any_space, any_space, any_space],
        out_specs=vmem,
        scratch_shapes=[
            pltpu.VMEM((640, C), BF16),
            pltpu.VMEM((640, C), BF16),
            pltpu.VMEM((9, 4, CB, C), BF16),
            pltpu.VMEM((4, CB, C), BF16),
            pltpu.VMEM((3, CZ, C), BF16),
            pltpu.VMEM((16, CB, C), BF16),
            pltpu.VMEM((32, 128), F32),
            pltpu.VMEM((16, 32, 128), F32),
            pltpu.VMEM((8, 128), F32),
            pltpu.VMEM((16, 8, 128), F32),
            pltpu.VMEM((C, 128), BF16),
            pltpu.VMEM((128, C), BF16),
            pltpu.VMEM((C, CZ), BF16),
            pltpu.VMEM((2, 8, C), F32),
            pltpu.VMEM((2, 8, CZ), F32),
            pltpu.VMEM((2, 8, CZ), F32),
            pltpu.VMEM((256, 3 * CZ), F32),
            pltpu.VMEM((4, NCH, 5, HALF, 128), BF16),
            pltpu.VMEM((R, C), BF16),
            pltpu.VMEM((BLK, C), F32),
            pltpu.VMEM((ROWS_Y, 384), BF16),
            pltpu.VMEM((4, ROWS_Y, 2 * CZ), BF16),
            pltpu.VMEM((4, BLK, CZ), BF16),
            pltpu.VMEM((4, BLK, CZ), BF16),
            dma((7,)), dma((16,)), dma((16,)), dma((2, 4)), dma((4,)), dma((2,)), dma((2,)),
            dma((3,)), dma((3,)), dma((3,)), dma((3,)),
            dma((3,)), dma((3,)), dma((3, 4)), dma((3, 4)), dma((3,)), dma((3,)),
            dma((1,)), dma((4,)), dma((1,)), dma((3,)), dma((1,)), dma((4,)), dma((4,)), dma((3,)), dma((3,)),
            dma((2, 4)), dma((4,)), dma((3,)), dma((3,)), dma((4,)), dma((4,)),
            dma((16,)), dma((16,)), dma((2, NCH, 4)), dma((NCH, 4)), dma((NCH, 2, 3)), dma((NCH, 2, 3)),
            dma((4,)), dma((4,)),
        ],
        compiler_params=pltpu.CompilerParams(
            collective_id=0, has_side_effects=True, vmem_limit_bytes=60 * 1024 * 1024
        ),
    )(
        latent.reshape(BLK, C), conv_weight.reshape(9, CB, C), channel_bias.reshape(1, CB), w_query, w_key, w_value, w_out
    )
    return out.reshape(latent.shape)


def solution(mesh):
    return jax.shard_map(
        on_device,
        mesh=mesh,
        in_specs=(
            P(("batch", "patch"), None, None),
            P(None, None, "patch", None),
            P("patch"),
            P("patch", None),
            P("patch", None),
            P("patch", None),
            P("patch", None),
        ),
        out_specs=P(("batch", "patch"), None, None),
        check_vma=False,
    )
```

```python
import jax
import jax.numpy as jnp
from jax import lax
from jax.experimental import pallas as pl
from jax.experimental.pallas import tpu as pltpu
from jax.sharding import PartitionSpec as P

C = 1280
HEADS = 20
HEAD_DIM = 64
GROUPS = 32
GROUP = C // GROUPS
NY, NZ = 4, 4
BLK = 128
ROWS_Y = 512
NCH = 4
R = ROWS_Y // NCH
HALF = R // 2
AHEAD = 1
CB = C // 16
CZ = C // 4
EPS = 1e-05
MESH = pl.DeviceIdType.MESH
F32 = jnp.float32
BF16 = jnp.bfloat16


def dot_nt(left, right):
    return lax.dot_general(left, right, (((1,), (1,)), ((), ())), preferred_element_type=F32)


def dot_nn(left, right):
    return lax.dot_general(left, right, (((1,), (0,)), ((), ())), preferred_element_type=F32)


def kernel(
    lat_in, cw_in, bias_in, wq_in, wk_in, wv_in, wo_in, out_ref,
    lat, act, cw, wown, wqkv, wo, st1s, st1, st2s, st2, gmat, gmat_t, sel,
    gn1, gn2, stc, ubuf, hidg, nrm, hnat, qb, kv, att, attg,
    s_loc, s_st1, r_st1, s_lat, r_lat, s_halo, r_halo, s_cw, r_cw, s_cws, r_cws,
    s_ct, r_ct, s_cx, r_cx, s_cts, r_cts,
    s_qa, r_qa, l_qa, s_qb, r_qb, s_qc, r_qc, s_qd, r_qd, s_woz, r_woz, s_woy, r_woy, s_wox, r_wox, s_wos, r_wos,
    s_st2, r_st2, s_hid, r_hid, s_kv, r_kv, s_att, r_att,
):
    p = lax.axis_index("patch")
    b = lax.axis_index("batch")
    y = p // 4
    z = p % 4
    c = b % 2
    x = (b // 2) % 4
    sib = b + 1 - 2 * c
    up = (y + 1) % 4
    down = (y + 3) % 4
    opposite = (y + 2) % 4
    half = pl.ds(pl.multiple_of(c * (C // 2), 128), C // 2)
    other = pl.ds(pl.multiple_of((1 - c) * (C // 2), 128), C // 2)
    pending = []

    def patch(yy, zz):
        return {"batch": b, "patch": 4 * yy + zz}

    def across(d):
        return {"batch": b - 2 * x + 2 * ((x + d) % 4), "patch": p}

    sibling = {"batch": sib, "patch": p}

    def remote(src, dst, ssem, rsem, dev):
        return pltpu.make_async_remote_copy(
            src_ref=src, dst_ref=dst, send_sem=ssem, recv_sem=rsem, device_id=dev, device_id_type=MESH
        )

    def when(cond, f):
        if cond is None:
            f()
        else:
            pl.when(cond)(f)

    def send(make, cond=None):
        when(cond, lambda: make().start())
        pending.append((cond, make))

    own_rows = pl.ds(pl.multiple_of(64 + BLK * z, 64), BLK)
    loc = [
        pltpu.make_async_copy(lat_in, lat.at[own_rows], s_loc.at[0]),
        pltpu.make_async_copy(cw_in, cw.at[:, y], s_loc.at[1]),
        pltpu.make_async_copy(wq_in, wown.at[0], s_loc.at[2]),
        pltpu.make_async_copy(wk_in, wown.at[1], s_loc.at[3]),
        pltpu.make_async_copy(wv_in, wown.at[2], s_loc.at[4]),
        pltpu.make_async_copy(wo_in, wown.at[3], s_loc.at[5]),
    ]
    for copy in loc:
        copy.start()
    barrier = pltpu.get_barrier_semaphore()
    for d in range(1, 16):
        pl.semaphore_signal(
            barrier, inc=1, device_id={"batch": b, "patch": (p + d) % 16}, device_id_type=MESH
        )
    pl.semaphore_signal(barrier, inc=1, device_id=sibling, device_id_type=MESH)
    for d in range(1, 4):
        pl.semaphore_signal(barrier, inc=1, device_id=across(d), device_id_type=MESH)

    st1s[...] = jnp.zeros_like(st1s)
    loc[0].wait()
    mine = lat[own_rows].astype(F32)
    mean = jnp.sum(mine, axis=0, keepdims=True) * (1.0 / BLK)
    m2 = jnp.sum(jnp.square(mine - mean), axis=0, keepdims=True)
    for j in range(10):
        st1s[j : j + 1, :] = mean[:, 128 * j : 128 * j + 128]
        st1s[16 + j : 17 + j, :] = m2[:, 128 * j : 128 * j + 128]
    st1s[15:16, 0:CB] = bias_in[...]

    pl.semaphore_wait(barrier, 19)

    for d in range(1, 16):
        send(
            lambda d=d: remote(
                st1s, st1.at[p], s_st1.at[d], r_st1.at[d], {"batch": b, "patch": (p + d) % 16}
            )
        )
    st1[p] = st1s[...]

    def lat_rows(k):
        return lat.at[pl.ds(pl.multiple_of(64 + BLK * k, 64), BLK)]

    def lat_copy(k, way):
        zz = z + 1 if way == 0 else z - 1
        return remote(lat_rows(k), lat_rows(k), s_lat.at[way, k], r_lat.at[k], patch(y, zz))

    send(lambda: lat_copy(z, 0), z < 3)
    send(lambda: lat_copy(z, 1), z > 0)

    loc[1].wait()
    around = (down, up, opposite)

    def cw_ref(src_y, mask):
        return cw.at[0:5, src_y, :, mask]

    def cw_copy(src_y, to_y, slot):
        ref = cw_ref(src_y, half)
        return remote(ref, ref, s_cw.at[slot], r_cw.at[slot], patch(to_y, z))

    def cw_other(r, mask):
        ref = cw_ref(around[r], mask)
        return remote(ref, ref, s_cws.at[r], r_cws.at[r], sibling)

    def ct_copy(src_y, to_y, slot):
        ref = cw.at[5 + x, src_y, :, half]
        return remote(ref, ref, s_ct.at[slot], r_ct.at[slot], patch(to_y, z))

    nexts = ((x + 1) % 4, (x + 3) % 4, (x + 2) % 4)

    def x_send(ref, ssem, rsem):
        send(lambda: remote(ref(x), ref(x), ssem(0), rsem(1), across(1)))
        send(lambda: remote(ref(x), ref(x), ssem(1), rsem(0), across(3)))

    def x_wait(ref, ssem, rsem, i):
        remote(ref(nexts[i]), ref(nexts[i]), ssem(i), rsem(i), across(1)).wait_recv()

    def x_relay(ref, ssem, rsem):
        x_wait(ref, ssem, rsem, 1)
        send(lambda: remote(ref(nexts[1]), ref(nexts[1]), ssem(2), rsem(2), across(1)), c == 0)
        x_wait(ref, ssem, rsem, 0)
        send(lambda: remote(ref(nexts[0]), ref(nexts[0]), ssem(2), rsem(2), across(3)), c == 1)

    def cx(r):
        return (
            lambda i: cw.at[5 + i, around[r], :, half],
            lambda i: s_cx.at[r, i],
            lambda i: r_cx.at[r, i],
        )

    def ct_other(r, mask):
        ref = cw.at[5:9, around[r], :, mask]
        return remote(ref, ref, s_cts.at[r], r_cts.at[r], sibling)

    send(lambda: ct_copy(y, up, 0))
    send(lambda: ct_copy(y, down, 1))

    for copy in loc[2:]:
        copy.wait()
    carrier = z == x
    diagonal = y == z
    turn = (y - z + 4) % 4

    def q_ref(i):
        return wqkv.at[:, pl.ds(pl.multiple_of(CB * i, 16), CB), half]

    def qa_copy():
        return remote(wown.at[0:3, :, half], q_ref(x), s_qa.at[0], r_qa.at[0], patch(y, y))

    def qa_local():
        return pltpu.make_async_copy(wown.at[0:3, :, half], q_ref(x), l_qa.at[0])

    def qb_copy(to_y, slot):
        return remote(q_ref(x), q_ref(x), s_qb.at[slot], r_qb.at[0], patch(to_y, z))

    qc = (q_ref, lambda i: s_qc.at[i], lambda i: r_qc.at[i])

    def qd_other(mask):
        ref = wqkv.at[:, :, mask]
        return remote(ref, ref, s_qd.at[0], r_qd.at[0], sibling)

    send(qa_copy, carrier & (z != y))
    when(carrier & diagonal, lambda: qa_local().start())
    send(lambda: cw_copy(y, up, 0))
    send(lambda: cw_copy(y, down, 1))

    def service_1():
        ct_copy(down, y, 0).wait_recv()
        send(lambda: ct_copy(down, up, 2), c == 0)
        ct_copy(up, y, 1).wait_recv()
        send(lambda: ct_copy(up, down, 2), c == 1)
        for r in range(2):
            x_send(*cx(r))
        when(diagonal & (z != x), lambda: qa_copy().wait_recv())
        when(diagonal & carrier, lambda: qa_local().wait())
        send(lambda: qb_copy(up, 0), diagonal)
        send(lambda: qb_copy(down, 1), diagonal)

    def service_2():
        ct_copy(opposite, y, 2).wait_recv()
        x_send(*cx(2))
        cw_copy(down, y, 0).wait_recv()
        send(lambda: cw_copy(down, up, 2), c == 0)
        cw_copy(up, y, 1).wait_recv()
        send(lambda: cw_copy(up, down, 2), c == 1)
        for r in range(2):
            send(lambda r=r: cw_other(r, half))
        beside = (turn == 1) | (turn == 3)
        when(beside, lambda: qb_copy(up, 0).wait_recv())
        send(lambda: qb_copy(up, 2), (turn == 1) & (c == 0))
        send(lambda: qb_copy(down, 2), (turn == 3) & (c == 1))
        for r in range(2):
            x_relay(*cx(r))

    def service_3():
        when(turn == 2, lambda: qb_copy(up, 0).wait_recv())
        x_send(*qc)
        x_relay(*cx(2))

    services = {1: service_1, 2: service_2, 3: service_3}

    gi = lax.broadcasted_iota(jnp.int32, (C, 128), 0) - GROUP * lax.broadcasted_iota(jnp.int32, (C, 128), 1)
    gmat[...] = jnp.where((gi >= 0) & (gi < GROUP), 1.0, 0.0).astype(BF16)
    ti = lax.broadcasted_iota(jnp.int32, (128, C), 1) - GROUP * lax.broadcasted_iota(jnp.int32, (128, C), 0)
    gmat_t[...] = jnp.where((ti >= 0) & (ti < GROUP), 1.0, 0.0).astype(BF16)
    for yy in range(4):
        rows = lax.broadcasted_iota(jnp.int32, (CZ, CZ), 0) - CB * z
        cols = lax.broadcasted_iota(jnp.int32, (CZ, CZ), 1) - CB * yy
        hit = (rows == cols) & (cols >= 0) & (cols < CB)
        sel[CZ * yy : CZ * yy + CZ, :] = jnp.where(hit, 1.0, 0.0).astype(BF16)

    def split_rows(x):
        hi = x.astype(BF16).astype(F32)
        mid = (x - hi).astype(BF16).astype(F32)
        return jnp.concatenate([hi, mid, x - hi - mid], axis=0).astype(BF16)

    def join_rows(x):
        return x[0:8] + x[8:16] + x[16:24]

    def group_sums(x):
        n = x.shape[1]
        sums = join_rows(dot_nn(split_rows(x), gmat[0:n, :]))
        return join_rows(dot_nn(split_rows(sums), gmat_t[:, 0:n]))

    for d in range(1, 16):
        q = (p + 16 - d) % 16
        remote(st1s, st1.at[q], s_st1.at[d], r_st1.at[d], {"batch": b, "patch": q}).wait_recv()
    means = st1[:, 0:16, :]
    mean_c = jnp.sum(means, axis=0) * (1.0 / 16)
    m2_c = jnp.sum(st1[:, 16:32, :], axis=0) + BLK * jnp.sum(jnp.square(means - mean_c[None]), axis=0)

    def to_lanes(x, n):
        full = jnp.concatenate([x[j : j + 1, :] for j in range(n)], axis=1)
        return full

    mean_l = jnp.broadcast_to(to_lanes(mean_c, 10), (8, C))
    m2_l = jnp.broadcast_to(to_lanes(m2_c, 10), (8, C))
    centre = group_sums(mean_l) * (1.0 / GROUP)
    spread = group_sums(m2_l + 2048.0 * jnp.square(mean_l - centre)) * (1.0 / (2048 * GROUP))
    gn1[0] = centre
    gn1[1] = lax.rsqrt(spread + EPS)

    def activate(start, count):
        def body(i, carry):
            rows = pl.ds(pl.multiple_of(start + 16 * i, 16), 16)
            v = lat[rows].astype(F32)
            v = (v - gn1[0, 0:1, :]) * gn1[1, 0:1, :]
            act[rows] = (v / (1.0 + jnp.exp(-v))).astype(BF16)
            return carry

        lax.fori_loop(0, count // 16, body, 0)

    activate(64 + BLK * z, BLK)

    def halo_up():
        return remote(
            lat.at[pl.ds(512, 64)], lat.at[pl.ds(0, 64)], s_halo.at[0], r_halo.at[0], patch(y + 1, z)
        )

    def halo_down():
        return remote(
            lat.at[pl.ds(64, 64)], lat.at[pl.ds(576, 64)], s_halo.at[1], r_halo.at[1], patch(y - 1, z)
        )

    send(halo_up, (z == 3) & (y < 3))
    send(halo_down, (z == 0) & (y > 0))
    for k in range(1, 4):
        def below(k=k):
            lat_copy(z - k, 0).wait_recv()

        def above(k=k):
            lat_copy(z + k, 1).wait_recv()

        when(z - k >= 0, below)
        send(lambda k=k: lat_copy(z - k, 0), (z - k >= 0) & (z < 3))
        when(z + k <= 3, above)
        send(lambda k=k: lat_copy(z + k, 1), (z + k <= 3) & (z > 0))
        send(halo_up, (z + k == 3) & (y < 3))
        send(halo_down, (z - k == 0) & (y > 0))
        services[k]()
        when(z - k >= 0, lambda k=k: activate(64 + BLK * (z - k), BLK))
        when(z + k <= 3, lambda k=k: activate(64 + BLK * (z + k), BLK))

    def wo_ref(yy, i):
        return wo.at[yy, i, :, half]

    def wo_local():
        return pltpu.make_async_copy(wown.at[3, :, half], wo_ref(y, x), l_qa.at[1])

    def wo_z(to_z, slot):
        return remote(wo_ref(y, x), wo_ref(y, x), s_woz.at[slot], r_woz.at[0], patch(y, to_z))

    when(carrier, lambda: wo_local().start())
    when(carrier, lambda: wo_local().wait())
    send(lambda: wo_z(z + 1, 0), carrier & (z < 3))
    send(lambda: wo_z(z - 1, 1), carrier & (z > 0))

    when(y > 0, lambda: halo_up().wait_recv())
    when(y > 0, lambda: activate(0, 64))
    when(y < 3, lambda: halo_down().wait_recv())
    when(y < 3, lambda: activate(576, 64))

    def zero_top():
        act[0:64] = jnp.zeros((64, C), BF16)

    def zero_bottom():
        act[576:640] = jnp.zeros((64, C), BF16)

    when(y == 0, zero_top)
    when(y == 3, zero_bottom)

    cw_copy(opposite, y, 2).wait_recv()
    send(lambda: cw_other(2, half))
    for r in range(3):
        x_wait(*cx(r), 2)
        send(lambda r=r: ct_other(r, half))
    x_relay(*qc)
    when(z != x, lambda: wo_z(z, 0).wait_recv())
    send(lambda: wo_z(z + 1, 0), (z > x) & (z < 3))
    send(lambda: wo_z(z - 1, 1), (z < x) & (z > 0))

    def wo_y(src_y, to_y, slot):
        return remote(wo_ref(src_y, x), wo_ref(src_y, x), s_woy.at[slot], r_woy.at[slot], patch(to_y, z))

    wox = (lambda i: wo.at[:, i, :, half], lambda i: s_wox.at[i], lambda i: r_wox.at[i])

    send(lambda: wo_y(y, up, 0))
    send(lambda: wo_y(y, down, 1))
    for r in range(3):
        cw_other(r, other).wait_recv()
        ct_other(r, other).wait_recv()

    bias = jnp.concatenate([st1[4 * yy + z, 15:16, 0:CB] for yy in range(4)], axis=1)
    CHUNK = 256

    def conv_chunk(j, carry):
        total = jnp.zeros((CHUNK, 3 * CZ), F32)
        for dr in range(3):
            rows = pl.ds(pl.multiple_of(CHUNK * j + 64 * dr, 64), CHUNK)
            total = total + dot_nt(act[rows], cw[3 * dr : 3 * dr + 3].reshape(3 * CZ, C))
        ubuf[...] = total
        column = lax.broadcasted_iota(jnp.int32, (CHUNK, CZ), 0) % 64
        left = pltpu.roll(ubuf[:, 0:CZ], 1, 0)
        right = pltpu.roll(ubuf[:, 2 * CZ : 3 * CZ], CHUNK - 1, 0)
        value = ubuf[:, CZ : 2 * CZ]
        value = value + jnp.where(column == 0, 0.0, left) + jnp.where(column == 63, 0.0, right)
        own = lat[pl.ds(pl.multiple_of(64 + CHUNK * j, 64), CHUNK)]
        value = value + dot_nn(own, sel[...]) + bias
        value = value.astype(BF16).astype(F32)
        mean = jnp.sum(value, axis=0, keepdims=True) * (1.0 / CHUNK)
        stc[j, 0:1, :] = mean
        stc[j, 1:2, :] = jnp.sum(jnp.square(value - mean), axis=0, keepdims=True)
        for i in range(CHUNK // R):
            upper = value[R * i : R * i + HALF]
            lower = value[R * i + HALF : R * i + R]
            ch = (CHUNK // R) * j + i
            hidg[z, ch, 0] = upper[:, 0:128].astype(BF16)
            hidg[z, ch, 1] = upper[:, 128:256].astype(BF16)
            hidg[z, ch, 2] = lower[:, 0:128].astype(BF16)
            hidg[z, ch, 3] = lower[:, 128:256].astype(BF16)
            hidg[z, ch, 4] = jnp.concatenate([upper[:, 256:CZ], lower[:, 256:CZ]], axis=1).astype(BF16)
        return carry

    def hid_copy(ch, k, way):
        zz = z + 1 if way == 0 else z - 1
        ref = hidg.at[k, ch]
        return remote(ref, ref, s_hid.at[way, ch, k], r_hid.at[ch, k], patch(y, zz))

    def hid_own(ch):
        send(lambda: hid_copy(ch, z, 0), z < 3)
        send(lambda: hid_copy(ch, z, 1), z > 0)

    conv_chunk(0, 0)
    hid_own(0)
    conv_chunk(1, 0)

    st2s[...] = jnp.zeros_like(st2s)
    mean = 0.5 * (stc[0, 0:1, :] + stc[1, 0:1, :])
    m2 = stc[0, 1:2, :] + stc[1, 1:2, :]
    m2 = m2 + CHUNK * (jnp.square(stc[0, 0:1, :] - mean) + jnp.square(stc[1, 0:1, :] - mean))
    for j in range(3):
        width = min(128, CZ - 128 * j)
        st2s[j : j + 1, 0:width] = mean[:, 128 * j : 128 * j + width]
        st2s[4 + j : 5 + j, 0:width] = m2[:, 128 * j : 128 * j + width]
    for d in range(1, 16):
        send(
            lambda d=d: remote(
                st2s, st2.at[p], s_st2.at[d], r_st2.at[d], {"batch": b, "patch": (p + d) % 16}
            )
        )
    st2[p] = st2s[...]

    def weights_1():
        x_wait(*qc, 2)
        send(lambda: qd_other(half))
        wo_y(down, y, 0).wait_recv()
        send(lambda: wo_y(down, up, 2), c == 0)
        wo_y(up, y, 1).wait_recv()
        send(lambda: wo_y(up, down, 2), c == 1)

    def second_norm():
        for d in range(1, 16):
            q = (p + 16 - d) % 16
            remote(st2s, st2.at[q], s_st2.at[d], r_st2.at[d], {"batch": b, "patch": q}).wait_recv()
        parts = [[st2[4 * yy + zz] for zz in range(4)] for yy in range(4)]
        mean_rows, m2_rows = [], []
        for zz in range(4):
            col = [parts[yy][zz] for yy in range(4)]
            m = (col[0] + col[1] + col[2] + col[3]) * 0.25
            dev = sum(jnp.square(x - m) for x in col)
            total = col[0] + col[1] + col[2] + col[3]
            m2_all = total[4:8] + ROWS_Y * dev[0:4]
            mean_rows.append(to_lanes(m, 3)[:, 0:CZ])
            m2_rows.append(to_lanes(m2_all, 3)[:, 0:CZ])
        mean_l = jnp.concatenate(mean_rows + mean_rows, axis=0)
        m2_l = jnp.concatenate(m2_rows + m2_rows, axis=0)
        centre = group_sums(mean_l) * (1.0 / GROUP)
        spread = group_sums(m2_l + 2048.0 * jnp.square(mean_l - centre)) * (1.0 / (2048 * GROUP))
        gn2[0] = centre
        gn2[1] = lax.rsqrt(spread + EPS)

    def hidden_rows(zz, ch, h, rows):
        tail = hidg[zz, ch, 4, rows, :].astype(F32)[:, 64 * h : 64 * h + 64]
        return jnp.concatenate(
            [hidg[zz, ch, 2 * h, rows, :].astype(F32), hidg[zz, ch, 2 * h + 1, rows, :].astype(F32), tail],
            axis=1,
        )

    def in_order(blocks):
        return jnp.concatenate(
            [blocks[zz][:, CB * yy : CB * yy + CB] for yy in range(4) for zz in range(4)], axis=1
        )

    def normalize(ch):
        for h in range(2):
            def body(i, carry, h=h):
                rows = pl.ds(pl.multiple_of(16 * i, 16), 16)
                blocks = [
                    (hidden_rows(zz, ch, h, rows) - gn2[0, zz : zz + 1, :]) * gn2[1, zz : zz + 1, :]
                    for zz in range(4)
                ]
                nrm[pl.ds(pl.multiple_of(HALF * h + 16 * i, 16), 16)] = in_order(blocks).astype(BF16)
                return carry

            lax.fori_loop(0, HALF // 16, body, 0)

    def project(ch):
        rows = pl.ds(R * ch, R)
        both = dot_nt(nrm[...], wqkv[...].reshape(3 * CZ, C))
        kv[y, rows, 0:256] = both[:, CZ : CZ + 256].astype(BF16)
        kv[y, rows, 256:512] = both[:, 2 * CZ : 2 * CZ + 256].astype(BF16)
        kv[y, rows, 512:640] = jnp.concatenate(
            [both[:, CZ + 256 : 2 * CZ], both[:, 2 * CZ + 256 : 3 * CZ]], axis=1
        ).astype(BF16)
        query = (both[:, 0:CZ].astype(BF16).astype(F32) * HEAD_DIM**-0.5).astype(BF16)
        qb[rows, 0:256] = query[:, 0:256]
        qb[rows, 256:384] = jnp.concatenate(
            [query[:, 256:CZ].astype(F32), jnp.zeros((R, 64), F32)], axis=1
        ).astype(BF16)

    def kv_copy(ch, h, src_y, to_y, slot):
        ref = kv.at[src_y, pl.ds(R * ch + HALF * h, HALF), :]
        return remote(ref, ref, s_kv.at[ch, h, slot], r_kv.at[ch, h, slot], patch(to_y, z))

    def kv_own(ch):
        send(lambda: kv_copy(ch, 0, y, up, 0))
        send(lambda: kv_copy(ch, 1, y, down, 1))
        send(lambda: kv_copy(ch, 1, y, up, 0))
        send(lambda: kv_copy(ch, 0, y, down, 1))

    def kv_on(ch):
        kv_copy(ch, 0, down, y, 0).wait_recv()
        send(lambda: kv_copy(ch, 0, down, up, 2))
        kv_copy(ch, 1, up, y, 1).wait_recv()
        send(lambda: kv_copy(ch, 1, up, down, 2))

    for ch in range(NCH):
        for k in range(1, 4):
            when(z - k >= 0, lambda k=k, ch=ch: hid_copy(ch, z - k, 0).wait_recv())
            send(lambda k=k, ch=ch: hid_copy(ch, z - k, 0), (z - k >= 0) & (z < 3))
            when(z + k <= 3, lambda k=k, ch=ch: hid_copy(ch, z + k, 1).wait_recv())
            send(lambda k=k, ch=ch: hid_copy(ch, z + k, 1), (z + k <= 3) & (z > 0))
            if k == AHEAD and ch + 1 < NCH:
                hid_own(ch + 1)
            if ch == 0 and k == 2:
                weights_1()
        if ch == 0:
            second_norm()
            qd_other(other).wait_recv()
        if ch == 1:
            wo_y(opposite, y, 2).wait_recv()
            x_send(*wox)
        if ch == 3:
            x_relay(*wox)
        normalize(ch)
        project(ch)
        kv_own(ch)
        if ch > 0:
            kv_on(ch - 1)

    for h in range(2):
        def residual(i, carry, h=h):
            rows = pl.ds(pl.multiple_of(16 * i, 16), 16)
            blocks = [hidden_rows(zz, z, h, rows) for zz in range(4)]
            hnat[pl.ds(pl.multiple_of(HALF * h + 16 * i, 16), 16)] = in_order(blocks)
            return carry

        lax.fori_loop(0, HALF // 16, residual, 0)

    kv_on(NCH - 1)
    def wo_other(mask):
        ref = wo.at[:, :, :, mask]
        return remote(ref, ref, s_wos.at[0], r_wos.at[0], sibling)

    x_wait(*wox, 2)
    send(lambda: wo_other(half))
    for ch in range(NCH):
        kv_copy(ch, 1, down, y, 0).wait_recv()
        kv_copy(ch, 0, up, y, 1).wait_recv()
        kv_copy(ch, 0, opposite, y, 2).wait_recv()
        kv_copy(ch, 1, opposite, y, 2).wait_recv()

    def att_copy(j):
        return remote(att.at[j], attg.at[z], s_att.at[j], r_att.at[z], patch(y, j))

    def att_from(k):
        return remote(att.at[k], attg.at[k], s_att.at[k], r_att.at[k], patch(y, k))

    def attend(j):
        rows = pl.ds(pl.multiple_of(BLK * j, 128), BLK)
        for pair in range(3):
            width = min(128, CZ - 128 * pair)
            lanes = slice(128 * pair, 128 * pair + width)
            query = qb[rows, 128 * pair : 128 * pair + 128]
            key_at = 128 * pair if pair < 2 else 512
            value_at = key_at + 256 if pair < 2 else 512
            keys = kv[:, :, key_at : key_at + 128].reshape(2048, 128)
            values = kv[:, :, value_at : value_at + 128].reshape(2048, 128)
            lane = lax.broadcasted_iota(jnp.int32, (BLK, 128), 1)
            result = None
            for side in range(width // 64):
                q1 = query
                if width > 64:
                    keep = (lane >= 64 * side) & (lane < 64 * side + 64)
                    q1 = jnp.where(keep, query.astype(F32), 0.0).astype(BF16)
                scores = dot_nt(q1, keys)
                peak = jnp.max(scores, axis=1, keepdims=True)
                unnormalized = jnp.exp(scores - peak)
                row_total = jnp.sum(unnormalized, axis=1, keepdims=True)
                mix = dot_nn(unnormalized.astype(BF16), values) / row_total
                result = mix if result is None else jnp.where(lane < 64, result, mix)
            if width == 64:
                result = result[:, 64:128]
            att[j, :, lanes] = result.astype(BF16)

    def attend_step(t, carry):
        j = (z + 1 + t) % 4
        attend(j)
        pl.when(t < 3)(lambda: att_copy(j).start())
        return carry

    lax.fori_loop(0, 4, attend_step, 0)
    attg[z] = att[z]
    for k in range(4):
        pending.append((z != k, lambda k=k: att_copy(k)))

    wo_other(other).wait_recv()
    for k in range(4):
        when(z != k, lambda k=k: att_from(k).wait_recv())

    whole = jnp.concatenate([attg[k].astype(F32) for k in range(4)], axis=1).astype(BF16)
    out_ref[...] = (hnat[...] + dot_nt(whole, wo[...].reshape(C, C))).astype(BF16)

    for cond, make in pending:
        when(cond, lambda make=make: make().wait_send())


def on_device(latent, conv_weight, channel_bias, w_query, w_key, w_value, w_out):
    any_space = pl.BlockSpec(memory_space=pl.ANY)
    vmem = pl.BlockSpec(memory_space=pltpu.VMEM)
    dma = pltpu.SemaphoreType.DMA
    out = pl.pallas_call(
        kernel,
        out_shape=jax.ShapeDtypeStruct((BLK, C), BF16),
        in_specs=[any_space, any_space, vmem, any_space, any_space, any_space, any_space],
        out_specs=vmem,
        scratch_shapes=[
            pltpu.VMEM((640, C), BF16),
            pltpu.VMEM((640, C), BF16),
            pltpu.VMEM((9, 4, CB, C), BF16),
            pltpu.VMEM((4, CB, C), BF16),
            pltpu.VMEM((3, CZ, C), BF16),
            pltpu.VMEM((4, 4, CB, C), BF16),
            pltpu.VMEM((32, 128), F32),
            pltpu.VMEM((16, 32, 128), F32),
            pltpu.VMEM((8, 128), F32),
            pltpu.VMEM((16, 8, 128), F32),
            pltpu.VMEM((C, 128), BF16),
            pltpu.VMEM((128, C), BF16),
            pltpu.VMEM((C, CZ), BF16),
            pltpu.VMEM((2, 8, C), F32),
            pltpu.VMEM((2, 8, CZ), F32),
            pltpu.VMEM((2, 8, CZ), F32),
            pltpu.VMEM((256, 3 * CZ), F32),
            pltpu.VMEM((4, NCH, 5, HALF, 128), BF16),
            pltpu.VMEM((R, C), BF16),
            pltpu.VMEM((BLK, C), F32),
            pltpu.VMEM((ROWS_Y, 384), BF16),
            pltpu.VMEM((4, ROWS_Y, 2 * CZ), BF16),
            pltpu.VMEM((4, BLK, CZ), BF16),
            pltpu.VMEM((4, BLK, CZ), BF16),
            dma((6,)), dma((16,)), dma((16,)), dma((2, 4)), dma((4,)), dma((2,)), dma((2,)),
            dma((3,)), dma((3,)), dma((3,)), dma((3,)),
            dma((3,)), dma((3,)), dma((3, 4)), dma((3, 4)), dma((3,)), dma((3,)),
            dma((1,)), dma((1,)), dma((2,)), dma((3,)), dma((1,)), dma((3,)), dma((3,)), dma((1,)), dma((1,)),
            dma((2,)), dma((1,)), dma((3,)), dma((3,)), dma((3,)), dma((3,)), dma((1,)), dma((1,)),
            dma((16,)), dma((16,)), dma((2, NCH, 4)), dma((NCH, 4)), dma((NCH, 2, 3)), dma((NCH, 2, 3)),
            dma((4,)), dma((4,)),
        ],
        compiler_params=pltpu.CompilerParams(
            collective_id=0, has_side_effects=True, vmem_limit_bytes=60 * 1024 * 1024
        ),
    )(
        latent.reshape(BLK, C), conv_weight.reshape(9, CB, C), channel_bias.reshape(1, CB), w_query, w_key, w_value, w_out
    )
    return out.reshape(latent.shape)


def solution(mesh):
    return jax.shard_map(
        on_device,
        mesh=mesh,
        in_specs=(
            P(("batch", "patch"), None, None),
            P(None, None, "patch", None),
            P("patch"),
            P("patch", None),
            P("patch", None),
            P("patch", None),
            P("patch", None),
        ),
        out_specs=P(("batch", "patch"), None, None),
        check_vma=False,
    )
```

```python
import jax
import jax.numpy as jnp
from jax import lax
from jax.experimental import pallas as pl
from jax.experimental.pallas import tpu as pltpu
from jax.sharding import PartitionSpec as P

C = 1280
HEADS = 20
HEAD_DIM = 64
GROUPS = 32
GROUP = C // GROUPS
NY, NZ = 4, 4
BLK = 128
ROWS_Y = 512
NCH = 4
R = ROWS_Y // NCH
HALF = R // 2
AHEAD = 1
CB = C // 16
CZ = C // 4
EPS = 1e-05
MESH = pl.DeviceIdType.MESH
F32 = jnp.float32
BF16 = jnp.bfloat16


def dot_nt(left, right):
    return lax.dot_general(left, right, (((1,), (1,)), ((), ())), preferred_element_type=F32)


def dot_nn(left, right):
    return lax.dot_general(left, right, (((1,), (0,)), ((), ())), preferred_element_type=F32)


def kernel(
    lat_in, cw_in, bias_in, wq_in, wk_in, wv_in, wo_in, out_ref,
    lat, act, cw, wown, wqkv, wo, st1s, st1, st2s, st2, gmat, gmat_t, sel,
    gn1, gn2, stc, ubuf, hidg, nrm, hnat, qb, kv, att, attg,
    s_loc, s_st1, r_st1, s_lat, r_lat, s_halo, r_halo, s_cw, r_cw, s_cws, r_cws,
    s_ct, r_ct, s_cx, r_cx, s_cts, r_cts,
    s_qa, r_qa, l_qa, s_qb, r_qb, s_qc, r_qc, s_qd, r_qd, s_woz, r_woz, s_woy, r_woy, s_wox, r_wox, s_wos, r_wos,
    s_st2, r_st2, s_hid, r_hid, s_kv, r_kv, s_att, r_att,
):
    p = lax.axis_index("patch")
    b = lax.axis_index("batch")
    y = p // 4
    z = p % 4
    c = b % 2
    x = (b // 2) % 4
    sib = b + 1 - 2 * c
    up = (y + 1) % 4
    down = (y + 3) % 4
    opposite = (y + 2) % 4
    half = pl.ds(pl.multiple_of(c * (C // 2), 128), C // 2)
    other = pl.ds(pl.multiple_of((1 - c) * (C // 2), 128), C // 2)
    pending = []

    def patch(yy, zz):
        return {"batch": b, "patch": 4 * yy + zz}

    def across(d):
        return {"batch": b - 2 * x + 2 * ((x + d) % 4), "patch": p}

    sibling = {"batch": sib, "patch": p}

    def remote(src, dst, ssem, rsem, dev):
        return pltpu.make_async_remote_copy(
            src_ref=src, dst_ref=dst, send_sem=ssem, recv_sem=rsem, device_id=dev, device_id_type=MESH
        )

    def when(cond, f):
        if cond is None:
            f()
        else:
            pl.when(cond)(f)

    def send(make, cond=None):
        when(cond, lambda: make().start())
        pending.append((cond, make))

    own_rows = pl.ds(pl.multiple_of(64 + BLK * z, 64), BLK)
    loc = [
        pltpu.make_async_copy(lat_in, lat.at[own_rows], s_loc.at[0]),
        pltpu.make_async_copy(cw_in, cw.at[:, y], s_loc.at[1]),
        pltpu.make_async_copy(wq_in, wown.at[0], s_loc.at[2]),
        pltpu.make_async_copy(wk_in, wown.at[1], s_loc.at[3]),
        pltpu.make_async_copy(wv_in, wown.at[2], s_loc.at[4]),
        pltpu.make_async_copy(wo_in, wown.at[3], s_loc.at[5]),
    ]
    for copy in loc:
        copy.start()
    barrier = pltpu.get_barrier_semaphore()
    for d in range(1, 16):
        pl.semaphore_signal(
            barrier, inc=1, device_id={"batch": b, "patch": (p + d) % 16}, device_id_type=MESH
        )
    pl.semaphore_signal(barrier, inc=1, device_id=sibling, device_id_type=MESH)
    for d in range(1, 4):
        pl.semaphore_signal(barrier, inc=1, device_id=across(d), device_id_type=MESH)

    gi = lax.broadcasted_iota(jnp.int32, (C, 128), 0) - GROUP * lax.broadcasted_iota(jnp.int32, (C, 128), 1)
    gmat[...] = jnp.where((gi >= 0) & (gi < GROUP), 1.0, 0.0).astype(BF16)
    ti = lax.broadcasted_iota(jnp.int32, (128, C), 1) - GROUP * lax.broadcasted_iota(jnp.int32, (128, C), 0)
    gmat_t[...] = jnp.where((ti >= 0) & (ti < GROUP), 1.0, 0.0).astype(BF16)
    def split_rows(x):
        hi = x.astype(BF16).astype(F32)
        mid = (x - hi).astype(BF16).astype(F32)
        return jnp.concatenate([hi, mid, x - hi - mid], axis=0).astype(BF16)

    def join_rows(x):
        return x[0:8] + x[8:16] + x[16:24]

    def to_groups(x):
        return join_rows(dot_nn(split_rows(x), gmat[0 : x.shape[1], :]))

    def to_channels(x, n):
        return join_rows(dot_nn(split_rows(x), gmat_t[:, 0:n]))

    def group_sums(x):
        return to_channels(to_groups(x), x.shape[1])

    st1s[...] = jnp.zeros_like(st1s)
    loc[0].wait()
    mine = lat[own_rows].astype(F32)
    mean = jnp.sum(mine, axis=0, keepdims=True) * (1.0 / BLK)
    m2 = jnp.sum(jnp.square(mine - mean), axis=0, keepdims=True)
    mean = jnp.broadcast_to(mean, (8, C))
    group_mean = to_groups(mean) * (1.0 / GROUP)
    group_m2 = to_groups(m2 + BLK * jnp.square(mean - to_channels(group_mean, C)))
    st1s[0:1, :] = group_mean[0:1, :]
    st1s[1:2, :] = group_m2[0:1, :]
    st1s[2:3, 0:CB] = bias_in[...]

    pl.semaphore_wait(barrier, 19)

    for d in range(1, 16):
        send(
            lambda d=d: remote(
                st1s, st1.at[p], s_st1.at[d], r_st1.at[d], {"batch": b, "patch": (p + d) % 16}
            )
        )
    st1[p] = st1s[...]

    def lat_rows(k):
        return lat.at[pl.ds(pl.multiple_of(64 + BLK * k, 64), BLK)]

    def lat_copy(k, way):
        zz = z + 1 if way == 0 else z - 1
        return remote(lat_rows(k), lat_rows(k), s_lat.at[way, k], r_lat.at[k], patch(y, zz))

    send(lambda: lat_copy(z, 0), z < 3)
    send(lambda: lat_copy(z, 1), z > 0)

    loc[1].wait()
    around = (down, up, opposite)

    def cw_ref(src_y, mask):
        return cw.at[0:5, src_y, :, mask]

    def cw_copy(src_y, to_y, slot):
        ref = cw_ref(src_y, half)
        return remote(ref, ref, s_cw.at[slot], r_cw.at[slot], patch(to_y, z))

    def cw_other(r, mask):
        ref = cw_ref(around[r], mask)
        return remote(ref, ref, s_cws.at[r], r_cws.at[r], sibling)

    def ct_copy(src_y, to_y, slot):
        ref = cw.at[5 + x, src_y, :, half]
        return remote(ref, ref, s_ct.at[slot], r_ct.at[slot], patch(to_y, z))

    nexts = ((x + 1) % 4, (x + 3) % 4, (x + 2) % 4)

    def x_send(ref, ssem, rsem):
        send(lambda: remote(ref(x), ref(x), ssem(0), rsem(1), across(1)))
        send(lambda: remote(ref(x), ref(x), ssem(1), rsem(0), across(3)))

    def x_wait(ref, ssem, rsem, i):
        remote(ref(nexts[i]), ref(nexts[i]), ssem(i), rsem(i), across(1)).wait_recv()

    def x_relay(ref, ssem, rsem):
        x_wait(ref, ssem, rsem, 1)
        send(lambda: remote(ref(nexts[1]), ref(nexts[1]), ssem(2), rsem(2), across(1)), c == 0)
        x_wait(ref, ssem, rsem, 0)
        send(lambda: remote(ref(nexts[0]), ref(nexts[0]), ssem(2), rsem(2), across(3)), c == 1)

    def cx(r):
        return (
            lambda i: cw.at[5 + i, around[r], :, half],
            lambda i: s_cx.at[r, i],
            lambda i: r_cx.at[r, i],
        )

    def ct_other(r, mask):
        ref = cw.at[5:9, around[r], :, mask]
        return remote(ref, ref, s_cts.at[r], r_cts.at[r], sibling)

    send(lambda: ct_copy(y, up, 0))
    send(lambda: ct_copy(y, down, 1))

    for copy in loc[2:]:
        copy.wait()
    carrier = z == x
    diagonal = y == z
    turn = (y - z + 4) % 4

    def q_ref(i):
        return wqkv.at[:, pl.ds(pl.multiple_of(CB * i, 16), CB), half]

    def qa_copy():
        return remote(wown.at[0:3, :, half], q_ref(x), s_qa.at[0], r_qa.at[0], patch(y, y))

    def qa_local():
        return pltpu.make_async_copy(wown.at[0:3, :, half], q_ref(x), l_qa.at[0])

    def qb_copy(to_y, slot):
        return remote(q_ref(x), q_ref(x), s_qb.at[slot], r_qb.at[0], patch(to_y, z))

    qc = (q_ref, lambda i: s_qc.at[i], lambda i: r_qc.at[i])

    def qd_other(mask):
        ref = wqkv.at[:, :, mask]
        return remote(ref, ref, s_qd.at[0], r_qd.at[0], sibling)

    send(qa_copy, carrier & (z != y))
    when(carrier & diagonal, lambda: qa_local().start())
    send(lambda: cw_copy(y, up, 0))
    send(lambda: cw_copy(y, down, 1))

    def service_1():
        ct_copy(down, y, 0).wait_recv()
        send(lambda: ct_copy(down, up, 2), c == 0)
        ct_copy(up, y, 1).wait_recv()
        send(lambda: ct_copy(up, down, 2), c == 1)
        for r in range(2):
            x_send(*cx(r))

    def service_2():
        ct_copy(opposite, y, 2).wait_recv()
        x_send(*cx(2))
        cw_copy(down, y, 0).wait_recv()
        send(lambda: cw_copy(down, up, 2), c == 0)
        cw_copy(up, y, 1).wait_recv()
        send(lambda: cw_copy(up, down, 2), c == 1)
        for r in range(2):
            send(lambda r=r: cw_other(r, half))
        when(diagonal & (z != x), lambda: qa_copy().wait_recv())
        when(diagonal & carrier, lambda: qa_local().wait())
        send(lambda: qb_copy(up, 0), diagonal)
        send(lambda: qb_copy(down, 1), diagonal)
        for r in range(2):
            x_relay(*cx(r))

    def service_3():
        beside = (turn == 1) | (turn == 3)
        when(beside, lambda: qb_copy(up, 0).wait_recv())
        send(lambda: qb_copy(up, 2), (turn == 1) & (c == 0))
        send(lambda: qb_copy(down, 2), (turn == 3) & (c == 1))
        x_relay(*cx(2))

    services = {1: service_1, 2: service_2, 3: service_3}

    for yy in range(4):
        rows = lax.broadcasted_iota(jnp.int32, (CZ, CZ), 0) - CB * z
        cols = lax.broadcasted_iota(jnp.int32, (CZ, CZ), 1) - CB * yy
        hit = (rows == cols) & (cols >= 0) & (cols < CB)
        sel[CZ * yy : CZ * yy + CZ, :] = jnp.where(hit, 1.0, 0.0).astype(BF16)

    for d in range(1, 16):
        q = (p + 16 - d) % 16
        remote(st1s, st1.at[q], s_st1.at[d], r_st1.at[d], {"batch": b, "patch": q}).wait_recv()
    def to_lanes(x, n):
        full = jnp.concatenate([x[j : j + 1, :] for j in range(n)], axis=1)
        return full

    stats = st1[...]
    stats_sum = jnp.sum(stats, axis=0)
    stats_dev = jnp.sum(jnp.square(stats - (stats_sum * (1.0 / 16))[None]), axis=0)
    centre = stats_sum[0:1, :] * (1.0 / 16)
    spread = (stats_sum[1:2, :] + (BLK * GROUP) * stats_dev[0:1, :]) * (1.0 / (2048 * GROUP))
    gn1[0] = to_channels(jnp.broadcast_to(centre, (8, 128)), C)
    gn1[1] = to_channels(jnp.broadcast_to(lax.rsqrt(spread + EPS), (8, 128)), C)

    def activate(start, count):
        def body(i, carry):
            rows = pl.ds(pl.multiple_of(start + 16 * i, 16), 16)
            v = lat[rows].astype(F32)
            v = (v - gn1[0, 0:1, :]) * gn1[1, 0:1, :]
            act[rows] = (v / (1.0 + jnp.exp(-v))).astype(BF16)
            return carry

        lax.fori_loop(0, count // 16, body, 0)

    activate(64 + BLK * z, BLK)

    def halo_up():
        return remote(
            lat.at[pl.ds(512, 64)], lat.at[pl.ds(0, 64)], s_halo.at[0], r_halo.at[0], patch(y + 1, z)
        )

    def halo_down():
        return remote(
            lat.at[pl.ds(64, 64)], lat.at[pl.ds(576, 64)], s_halo.at[1], r_halo.at[1], patch(y - 1, z)
        )

    send(halo_up, (z == 3) & (y < 3))
    send(halo_down, (z == 0) & (y > 0))
    for k in range(1, 4):
        def below(k=k):
            lat_copy(z - k, 0).wait_recv()

        def above(k=k):
            lat_copy(z + k, 1).wait_recv()

        when(z - k >= 0, below)
        send(lambda k=k: lat_copy(z - k, 0), (z - k >= 0) & (z < 3))
        when(z + k <= 3, above)
        send(lambda k=k: lat_copy(z + k, 1), (z + k <= 3) & (z > 0))
        send(halo_up, (z + k == 3) & (y < 3))
        send(halo_down, (z - k == 0) & (y > 0))
        services[k]()
        when(z - k >= 0, lambda k=k: activate(64 + BLK * (z - k), BLK))
        when(z + k <= 3, lambda k=k: activate(64 + BLK * (z + k), BLK))

    def wo_ref(yy, i):
        return wo.at[yy, i, :, half]

    def wo_local():
        return pltpu.make_async_copy(wown.at[3, :, half], wo_ref(y, x), l_qa.at[1])

    def wo_z(to_z, slot):
        return remote(wo_ref(y, x), wo_ref(y, x), s_woz.at[slot], r_woz.at[0], patch(y, to_z))

    when(carrier, lambda: wo_local().start())
    when(carrier, lambda: wo_local().wait())
    send(lambda: wo_z(z + 1, 0), carrier & (z < 3))
    send(lambda: wo_z(z - 1, 1), carrier & (z > 0))

    when(y > 0, lambda: halo_up().wait_recv())
    when(y > 0, lambda: activate(0, 64))
    when(y < 3, lambda: halo_down().wait_recv())
    when(y < 3, lambda: activate(576, 64))

    def zero_top():
        act[0:64] = jnp.zeros((64, C), BF16)

    def zero_bottom():
        act[576:640] = jnp.zeros((64, C), BF16)

    when(y == 0, zero_top)
    when(y == 3, zero_bottom)

    cw_copy(opposite, y, 2).wait_recv()
    send(lambda: cw_other(2, half))
    for r in range(3):
        x_wait(*cx(r), 2)
        send(lambda r=r: ct_other(r, half))

    def wo_y(src_y, to_y, slot):
        return remote(wo_ref(src_y, x), wo_ref(src_y, x), s_woy.at[slot], r_woy.at[slot], patch(to_y, z))

    wox = (lambda i: wo.at[:, i, :, half], lambda i: s_wox.at[i], lambda i: r_wox.at[i])

    when(turn == 2, lambda: qb_copy(up, 0).wait_recv())
    x_send(*qc)
    for r in range(3):
        cw_other(r, other).wait_recv()
        ct_other(r, other).wait_recv()

    bias = jnp.concatenate([st1[4 * yy + z, 2:3, 0:CB] for yy in range(4)], axis=1)
    CHUNK = 256

    def conv_chunk(j, carry):
        total = jnp.zeros((CHUNK, 3 * CZ), F32)
        for dr in range(3):
            rows = pl.ds(pl.multiple_of(CHUNK * j + 64 * dr, 64), CHUNK)
            total = total + dot_nt(act[rows], cw[3 * dr : 3 * dr + 3].reshape(3 * CZ, C))
        ubuf[...] = total
        column = lax.broadcasted_iota(jnp.int32, (CHUNK, CZ), 0) % 64
        left = pltpu.roll(ubuf[:, 0:CZ], 1, 0)
        right = pltpu.roll(ubuf[:, 2 * CZ : 3 * CZ], CHUNK - 1, 0)
        value = ubuf[:, CZ : 2 * CZ]
        value = value + jnp.where(column == 0, 0.0, left) + jnp.where(column == 63, 0.0, right)
        own = lat[pl.ds(pl.multiple_of(64 + CHUNK * j, 64), CHUNK)]
        value = value + dot_nn(own, sel[...]) + bias
        value = value.astype(BF16).astype(F32)
        mean = jnp.sum(value, axis=0, keepdims=True) * (1.0 / CHUNK)
        stc[j, 0:1, :] = mean
        stc[j, 1:2, :] = jnp.sum(jnp.square(value - mean), axis=0, keepdims=True)
        for i in range(CHUNK // R):
            upper = value[R * i : R * i + HALF]
            lower = value[R * i + HALF : R * i + R]
            ch = (CHUNK // R) * j + i
            hidg[z, ch, 0] = upper[:, 0:128].astype(BF16)
            hidg[z, ch, 1] = upper[:, 128:256].astype(BF16)
            hidg[z, ch, 2] = lower[:, 0:128].astype(BF16)
            hidg[z, ch, 3] = lower[:, 128:256].astype(BF16)
            hidg[z, ch, 4] = jnp.concatenate([upper[:, 256:CZ], lower[:, 256:CZ]], axis=1).astype(BF16)
        return carry

    def hid_copy(ch, k, way):
        zz = z + 1 if way == 0 else z - 1
        ref = hidg.at[k, ch]
        return remote(ref, ref, s_hid.at[way, ch, k], r_hid.at[ch, k], patch(y, zz))

    def hid_own(ch):
        send(lambda: hid_copy(ch, z, 0), z < 3)
        send(lambda: hid_copy(ch, z, 1), z > 0)

    conv_chunk(0, 0)
    hid_own(0)
    x_relay(*qc)
    when(z != x, lambda: wo_z(z, 0).wait_recv())
    send(lambda: wo_z(z + 1, 0), (z > x) & (z < 3))
    send(lambda: wo_z(z - 1, 1), (z < x) & (z > 0))
    conv_chunk(1, 0)

    st2s[...] = jnp.zeros_like(st2s)
    mean = 0.5 * (stc[0, 0:1, :] + stc[1, 0:1, :])
    m2 = stc[0, 1:2, :] + stc[1, 1:2, :]
    m2 = m2 + CHUNK * (jnp.square(stc[0, 0:1, :] - mean) + jnp.square(stc[1, 0:1, :] - mean))
    for j in range(3):
        width = min(128, CZ - 128 * j)
        st2s[j : j + 1, 0:width] = mean[:, 128 * j : 128 * j + width]
        st2s[4 + j : 5 + j, 0:width] = m2[:, 128 * j : 128 * j + width]
    for d in range(1, 16):
        send(
            lambda d=d: remote(
                st2s, st2.at[p], s_st2.at[d], r_st2.at[d], {"batch": b, "patch": (p + d) % 16}
            )
        )
    st2[p] = st2s[...]

    def weights_1():
        x_wait(*qc, 2)
        send(lambda: qd_other(half))
        send(lambda: wo_y(y, up, 0))
        send(lambda: wo_y(y, down, 1))

    def second_norm():
        for d in range(1, 16):
            q = (p + 16 - d) % 16
            remote(st2s, st2.at[q], s_st2.at[d], r_st2.at[d], {"batch": b, "patch": q}).wait_recv()
        parts = [[st2[4 * yy + zz] for zz in range(4)] for yy in range(4)]
        mean_rows, m2_rows = [], []
        for zz in range(4):
            col = [parts[yy][zz] for yy in range(4)]
            m = (col[0] + col[1] + col[2] + col[3]) * 0.25
            dev = sum(jnp.square(x - m) for x in col)
            total = col[0] + col[1] + col[2] + col[3]
            m2_all = total[4:8] + ROWS_Y * dev[0:4]
            mean_rows.append(to_lanes(m, 3)[:, 0:CZ])
            m2_rows.append(to_lanes(m2_all, 3)[:, 0:CZ])
        mean_l = jnp.concatenate(mean_rows + mean_rows, axis=0)
        m2_l = jnp.concatenate(m2_rows + m2_rows, axis=0)
        centre = group_sums(mean_l) * (1.0 / GROUP)
        spread = group_sums(m2_l + 2048.0 * jnp.square(mean_l - centre)) * (1.0 / (2048 * GROUP))
        gn2[0] = centre
        gn2[1] = lax.rsqrt(spread + EPS)

    def hidden_rows(zz, ch, h, rows):
        tail = hidg[zz, ch, 4, rows, :].astype(F32)[:, 64 * h : 64 * h + 64]
        return jnp.concatenate(
            [hidg[zz, ch, 2 * h, rows, :].astype(F32), hidg[zz, ch, 2 * h + 1, rows, :].astype(F32), tail],
            axis=1,
        )

    def in_order(blocks):
        return jnp.concatenate(
            [blocks[zz][:, CB * yy : CB * yy + CB] for yy in range(4) for zz in range(4)], axis=1
        )

    def normalize(ch):
        for h in range(2):
            def body(i, carry, h=h):
                rows = pl.ds(pl.multiple_of(16 * i, 16), 16)
                blocks = [
                    (hidden_rows(zz, ch, h, rows) - gn2[0, zz : zz + 1, :]) * gn2[1, zz : zz + 1, :]
                    for zz in range(4)
                ]
                nrm[pl.ds(pl.multiple_of(HALF * h + 16 * i, 16), 16)] = in_order(blocks).astype(BF16)
                return carry

            lax.fori_loop(0, HALF // 16, body, 0)

    def project(ch):
        rows = pl.ds(R * ch, R)
        both = dot_nt(nrm[...], wqkv[...].reshape(3 * CZ, C))
        kv[y, rows, 0:256] = both[:, CZ : CZ + 256].astype(BF16)
        kv[y, rows, 256:512] = both[:, 2 * CZ : 2 * CZ + 256].astype(BF16)
        kv[y, rows, 512:640] = jnp.concatenate(
            [both[:, CZ + 256 : 2 * CZ], both[:, 2 * CZ + 256 : 3 * CZ]], axis=1
        ).astype(BF16)
        query = (both[:, 0:CZ].astype(BF16).astype(F32) * HEAD_DIM**-0.5).astype(BF16)
        qb[rows, 0:256] = query[:, 0:256]
        qb[rows, 256:384] = jnp.concatenate(
            [query[:, 256:CZ].astype(F32), jnp.zeros((R, 64), F32)], axis=1
        ).astype(BF16)

    def kv_copy(ch, h, src_y, to_y, slot):
        ref = kv.at[src_y, pl.ds(R * ch + HALF * h, HALF), :]
        return remote(ref, ref, s_kv.at[ch, h, slot], r_kv.at[ch, h, slot], patch(to_y, z))

    def kv_own(ch):
        send(lambda: kv_copy(ch, 0, y, up, 0))
        send(lambda: kv_copy(ch, 1, y, down, 1))
        send(lambda: kv_copy(ch, 1, y, up, 0))
        send(lambda: kv_copy(ch, 0, y, down, 1))

    def kv_on(ch):
        kv_copy(ch, 0, down, y, 0).wait_recv()
        send(lambda: kv_copy(ch, 0, down, up, 2))
        kv_copy(ch, 1, up, y, 1).wait_recv()
        send(lambda: kv_copy(ch, 1, up, down, 2))

    for ch in range(NCH):
        for k in range(1, 4):
            when(z - k >= 0, lambda k=k, ch=ch: hid_copy(ch, z - k, 0).wait_recv())
            send(lambda k=k, ch=ch: hid_copy(ch, z - k, 0), (z - k >= 0) & (z < 3))
            when(z + k <= 3, lambda k=k, ch=ch: hid_copy(ch, z + k, 1).wait_recv())
            send(lambda k=k, ch=ch: hid_copy(ch, z + k, 1), (z + k <= 3) & (z > 0))
            if k == AHEAD and ch + 1 < NCH:
                hid_own(ch + 1)
            if ch == 0 and k == 2:
                weights_1()
        if ch == 0:
            second_norm()
            qd_other(other).wait_recv()
        if ch == 1:
            wo_y(down, y, 0).wait_recv()
            send(lambda: wo_y(down, up, 2), c == 0)
            wo_y(up, y, 1).wait_recv()
            send(lambda: wo_y(up, down, 2), c == 1)
        if ch == 2:
            wo_y(opposite, y, 2).wait_recv()
            x_send(*wox)
        normalize(ch)
        project(ch)
        kv_own(ch)
        if ch > 0:
            kv_on(ch - 1)

    for h in range(2):
        def residual(i, carry, h=h):
            rows = pl.ds(pl.multiple_of(16 * i, 16), 16)
            blocks = [hidden_rows(zz, z, h, rows) for zz in range(4)]
            hnat[pl.ds(pl.multiple_of(HALF * h + 16 * i, 16), 16)] = in_order(blocks)
            return carry

        lax.fori_loop(0, HALF // 16, residual, 0)

    kv_on(NCH - 1)
    def wo_other(mask):
        ref = wo.at[:, :, :, mask]
        return remote(ref, ref, s_wos.at[0], r_wos.at[0], sibling)

    x_relay(*wox)
    for ch in range(NCH):
        kv_copy(ch, 1, down, y, 0).wait_recv()
        kv_copy(ch, 0, up, y, 1).wait_recv()
        kv_copy(ch, 0, opposite, y, 2).wait_recv()
        kv_copy(ch, 1, opposite, y, 2).wait_recv()

    def att_copy(j):
        return remote(att.at[j], attg.at[z], s_att.at[j], r_att.at[z], patch(y, j))

    def att_from(k):
        return remote(att.at[k], attg.at[k], s_att.at[k], r_att.at[k], patch(y, k))

    def attend(j):
        rows = pl.ds(pl.multiple_of(BLK * j, 128), BLK)
        for pair in range(3):
            width = min(128, CZ - 128 * pair)
            lanes = slice(128 * pair, 128 * pair + width)
            query = qb[rows, 128 * pair : 128 * pair + 128]
            key_at = 128 * pair if pair < 2 else 512
            value_at = key_at + 256 if pair < 2 else 512
            keys = kv[:, :, key_at : key_at + 128].reshape(2048, 128)
            values = kv[:, :, value_at : value_at + 128].reshape(2048, 128)
            lane = lax.broadcasted_iota(jnp.int32, (BLK, 128), 1)
            result = None
            for side in range(width // 64):
                q1 = query
                if width > 64:
                    keep = (lane >= 64 * side) & (lane < 64 * side + 64)
                    q1 = jnp.where(keep, query.astype(F32), 0.0).astype(BF16)
                scores = dot_nt(q1, keys)
                peak = jnp.max(scores, axis=1, keepdims=True)
                unnormalized = jnp.exp(scores - peak)
                row_total = jnp.sum(unnormalized, axis=1, keepdims=True)
                mix = dot_nn(unnormalized.astype(BF16), values) / row_total
                result = mix if result is None else jnp.where(lane < 64, result, mix)
            if width == 64:
                result = result[:, 64:128]
            att[j, :, lanes] = result.astype(BF16)

    def attend_step(t, carry):
        j = (z + 1 + t) % 4
        attend(j)
        pl.when(t < 3)(lambda: att_copy(j).start())
        return carry

    lax.fori_loop(0, 2, attend_step, 0)
    x_wait(*wox, 2)
    send(lambda: wo_other(half))
    lax.fori_loop(2, 4, attend_step, 0)
    attg[z] = att[z]
    for k in range(4):
        pending.append((z != k, lambda k=k: att_copy(k)))

    wo_other(other).wait_recv()
    for k in range(4):
        when(z != k, lambda k=k: att_from(k).wait_recv())

    whole = jnp.concatenate([attg[k].astype(F32) for k in range(4)], axis=1).astype(BF16)
    out_ref[...] = (hnat[...] + dot_nt(whole, wo[...].reshape(C, C))).astype(BF16)

    for cond, make in pending:
        when(cond, lambda make=make: make().wait_send())


def on_device(latent, conv_weight, channel_bias, w_query, w_key, w_value, w_out):
    any_space = pl.BlockSpec(memory_space=pl.ANY)
    vmem = pl.BlockSpec(memory_space=pltpu.VMEM)
    dma = pltpu.SemaphoreType.DMA
    out = pl.pallas_call(
        kernel,
        out_shape=jax.ShapeDtypeStruct((BLK, C), BF16),
        in_specs=[any_space, any_space, vmem, any_space, any_space, any_space, any_space],
        out_specs=vmem,
        scratch_shapes=[
            pltpu.VMEM((640, C), BF16),
            pltpu.VMEM((640, C), BF16),
            pltpu.VMEM((9, 4, CB, C), BF16),
            pltpu.VMEM((4, CB, C), BF16),
            pltpu.VMEM((3, CZ, C), BF16),
            pltpu.VMEM((4, 4, CB, C), BF16),
            pltpu.VMEM((8, 128), F32),
            pltpu.VMEM((16, 8, 128), F32),
            pltpu.VMEM((8, 128), F32),
            pltpu.VMEM((16, 8, 128), F32),
            pltpu.VMEM((C, 128), BF16),
            pltpu.VMEM((128, C), BF16),
            pltpu.VMEM((C, CZ), BF16),
            pltpu.VMEM((2, 8, C), F32),
            pltpu.VMEM((2, 8, CZ), F32),
            pltpu.VMEM((2, 8, CZ), F32),
            pltpu.VMEM((256, 3 * CZ), F32),
            pltpu.VMEM((4, NCH, 5, HALF, 128), BF16),
            pltpu.VMEM((R, C), BF16),
            pltpu.VMEM((BLK, C), F32),
            pltpu.VMEM((ROWS_Y, 384), BF16),
            pltpu.VMEM((4, ROWS_Y, 2 * CZ), BF16),
            pltpu.VMEM((4, BLK, CZ), BF16),
            pltpu.VMEM((4, BLK, CZ), BF16),
            dma((6,)), dma((16,)), dma((16,)), dma((2, 4)), dma((4,)), dma((2,)), dma((2,)),
            dma((3,)), dma((3,)), dma((3,)), dma((3,)),
            dma((3,)), dma((3,)), dma((3, 4)), dma((3, 4)), dma((3,)), dma((3,)),
            dma((1,)), dma((1,)), dma((2,)), dma((3,)), dma((1,)), dma((3,)), dma((3,)), dma((1,)), dma((1,)),
            dma((2,)), dma((1,)), dma((3,)), dma((3,)), dma((3,)), dma((3,)), dma((1,)), dma((1,)),
            dma((16,)), dma((16,)), dma((2, NCH, 4)), dma((NCH, 4)), dma((NCH, 2, 3)), dma((NCH, 2, 3)),
            dma((4,)), dma((4,)),
        ],
        compiler_params=pltpu.CompilerParams(
            collective_id=0, has_side_effects=True, vmem_limit_bytes=60 * 1024 * 1024
        ),
    )(
        latent.reshape(BLK, C), conv_weight.reshape(9, CB, C), channel_bias.reshape(1, CB), w_query, w_key, w_value, w_out
    )
    return out.reshape(latent.shape)


def solution(mesh):
    return jax.shard_map(
        on_device,
        mesh=mesh,
        in_specs=(
            P(("batch", "patch"), None, None),
            P(None, None, "patch", None),
            P("patch"),
            P("patch", None),
            P("patch", None),
            P("patch", None),
            P("patch", None),
        ),
        out_specs=P(("batch", "patch"), None, None),
        check_vma=False,
    )
```

```python
import jax
import jax.numpy as jnp
from jax import lax
from jax.experimental import pallas as pl
from jax.experimental.pallas import tpu as pltpu
from jax.sharding import PartitionSpec as P

C = 1280
HEADS = 20
HEAD_DIM = 64
GROUPS = 32
GROUP = C // GROUPS
NY, NZ = 4, 4
BLK = 128
ROWS_Y = 512
NCH = 4
R = ROWS_Y // NCH
HALF = R // 2
AHEAD = 1
CB = C // 16
CZ = C // 4
EPS = 1e-05
MESH = pl.DeviceIdType.MESH
F32 = jnp.float32
BF16 = jnp.bfloat16


def dot_nt(left, right):
    return lax.dot_general(left, right, (((1,), (1,)), ((), ())), preferred_element_type=F32)


def dot_nn(left, right):
    return lax.dot_general(left, right, (((1,), (0,)), ((), ())), preferred_element_type=F32)


def kernel(
    lat_in, cw_in, bias_in, wq_in, wk_in, wv_in, wo_in, out_ref,
    lat, act, cw, wown, wqkv, wo, st1s, st1, st2s, st2, gmat, gmat_t, sel,
    gn1, gn2, stc, ubuf, hidg, nrm, hnat, qb, kv, att, attg,
    s_loc, s_st1, r_st1, s_lat, r_lat, s_halo, r_halo, s_cw, r_cw, s_cws, r_cws,
    s_ct, r_ct, s_cx, r_cx, s_cts, r_cts,
    s_qa, r_qa, l_qa, s_qb, r_qb, s_qc, r_qc, s_qd, r_qd, s_woz, r_woz, s_woy, r_woy, s_wox, r_wox, s_wos, r_wos,
    s_st2, r_st2, s_hid, r_hid, s_kv, r_kv, s_att, r_att,
):
    p = lax.axis_index("patch")
    b = lax.axis_index("batch")
    y = p // 4
    z = p % 4
    c = b % 2
    x = (b // 2) % 4
    sib = b + 1 - 2 * c
    up = (y + 1) % 4
    down = (y + 3) % 4
    opposite = (y + 2) % 4
    half = pl.ds(pl.multiple_of(c * (C // 2), 128), C // 2)
    other = pl.ds(pl.multiple_of((1 - c) * (C // 2), 128), C // 2)
    pending = []

    def patch(yy, zz):
        return {"batch": b, "patch": 4 * yy + zz}

    def across(d):
        return {"batch": b - 2 * x + 2 * ((x + d) % 4), "patch": p}

    sibling = {"batch": sib, "patch": p}

    def remote(src, dst, ssem, rsem, dev):
        return pltpu.make_async_remote_copy(
            src_ref=src, dst_ref=dst, send_sem=ssem, recv_sem=rsem, device_id=dev, device_id_type=MESH
        )

    def when(cond, f):
        if cond is None:
            f()
        else:
            pl.when(cond)(f)

    def send(make, cond=None):
        when(cond, lambda: make().start())
        pending.append((cond, make))

    own_rows = pl.ds(pl.multiple_of(64 + BLK * z, 64), BLK)
    loc = [
        pltpu.make_async_copy(lat_in, lat.at[own_rows], s_loc.at[0]),
        pltpu.make_async_copy(cw_in, cw.at[:, y], s_loc.at[1]),
        pltpu.make_async_copy(wq_in, wown.at[0], s_loc.at[2]),
        pltpu.make_async_copy(wk_in, wown.at[1], s_loc.at[3]),
        pltpu.make_async_copy(wv_in, wown.at[2], s_loc.at[4]),
        pltpu.make_async_copy(wo_in, wown.at[3], s_loc.at[5]),
    ]
    for copy in loc:
        copy.start()
    barrier = pltpu.get_barrier_semaphore()
    for d in range(1, 16):
        pl.semaphore_signal(
            barrier, inc=1, device_id={"batch": b, "patch": (p + d) % 16}, device_id_type=MESH
        )
    pl.semaphore_signal(barrier, inc=1, device_id=sibling, device_id_type=MESH)
    for d in range(1, 4):
        pl.semaphore_signal(barrier, inc=1, device_id=across(d), device_id_type=MESH)

    gi = lax.broadcasted_iota(jnp.int32, (C, 128), 0) - GROUP * lax.broadcasted_iota(jnp.int32, (C, 128), 1)
    gmat[...] = jnp.where((gi >= 0) & (gi < GROUP), 1.0, 0.0).astype(BF16)
    ti = lax.broadcasted_iota(jnp.int32, (128, C), 1) - GROUP * lax.broadcasted_iota(jnp.int32, (128, C), 0)
    gmat_t[...] = jnp.where((ti >= 0) & (ti < GROUP), 1.0, 0.0).astype(BF16)
    def split_rows(x):
        hi = x.astype(BF16).astype(F32)
        mid = (x - hi).astype(BF16).astype(F32)
        return jnp.concatenate([hi, mid, x - hi - mid], axis=0).astype(BF16)

    def join_rows(x):
        return x[0:8] + x[8:16] + x[16:24]

    def to_groups(x):
        return join_rows(dot_nn(split_rows(x), gmat[0 : x.shape[1], :]))

    def to_channels(x, n):
        return join_rows(dot_nn(split_rows(x), gmat_t[:, 0:n]))

    def group_sums(x):
        return to_channels(to_groups(x), x.shape[1])

    st1s[...] = jnp.zeros_like(st1s)
    loc[0].wait()
    mine = lat[own_rows].astype(F32)
    mean = jnp.sum(mine, axis=0, keepdims=True) * (1.0 / BLK)
    m2 = jnp.sum(jnp.square(mine - mean), axis=0, keepdims=True)
    mean = jnp.broadcast_to(mean, (8, C))
    group_mean = to_groups(mean) * (1.0 / GROUP)
    group_m2 = to_groups(m2 + BLK * jnp.square(mean - to_channels(group_mean, C)))
    st1s[0:1, :] = group_mean[0:1, :]
    st1s[1:2, :] = group_m2[0:1, :]
    st1s[2:3, 0:CB] = bias_in[...]

    pl.semaphore_wait(barrier, 19)

    for d in range(1, 16):
        send(
            lambda d=d: remote(
                st1s, st1.at[p], s_st1.at[d], r_st1.at[d], {"batch": b, "patch": (p + d) % 16}
            )
        )
    st1[p] = st1s[...]

    def lat_rows(k):
        return lat.at[pl.ds(pl.multiple_of(64 + BLK * k, 64), BLK)]

    def lat_copy(k, way):
        zz = z + 1 if way == 0 else z - 1
        return remote(lat_rows(k), lat_rows(k), s_lat.at[way, k], r_lat.at[k], patch(y, zz))

    send(lambda: lat_copy(z, 0), z < 3)
    send(lambda: lat_copy(z, 1), z > 0)

    loc[1].wait()
    around = (down, up, opposite)

    def cw_ref(src_y, mask):
        return cw.at[0:5, src_y, :, mask]

    def cw_copy(src_y, to_y, slot):
        ref = cw_ref(src_y, half)
        return remote(ref, ref, s_cw.at[slot], r_cw.at[slot], patch(to_y, z))

    def cw_other(r, mask):
        ref = cw_ref(around[r], mask)
        return remote(ref, ref, s_cws.at[r], r_cws.at[r], sibling)

    def ct_copy(src_y, to_y, slot):
        ref = cw.at[5 + x, src_y, :, half]
        return remote(ref, ref, s_ct.at[slot], r_ct.at[slot], patch(to_y, z))

    nexts = ((x + 1) % 4, (x + 3) % 4, (x + 2) % 4)

    def x_send_if(cond, ref, ssem, rsem):
        send(lambda: remote(ref(x), ref(x), ssem(0), rsem(1), across(1)), cond)
        send(lambda: remote(ref(x), ref(x), ssem(1), rsem(0), across(3)), cond)

    def x_send(ref, ssem, rsem):
        x_send_if(None, ref, ssem, rsem)

    def x_wait(ref, ssem, rsem, i):
        remote(ref(nexts[i]), ref(nexts[i]), ssem(i), rsem(i), across(1)).wait_recv()

    def x_relay(ref, ssem, rsem):
        x_wait(ref, ssem, rsem, 1)
        send(lambda: remote(ref(nexts[1]), ref(nexts[1]), ssem(2), rsem(2), across(1)), c == 0)
        x_wait(ref, ssem, rsem, 0)
        send(lambda: remote(ref(nexts[0]), ref(nexts[0]), ssem(2), rsem(2), across(3)), c == 1)

    def cx(r):
        return (
            lambda i: cw.at[5 + i, around[r], :, half],
            lambda i: s_cx.at[r, i],
            lambda i: r_cx.at[r, i],
        )

    def ct_other(r, mask):
        ref = cw.at[5:9, around[r], :, mask]
        return remote(ref, ref, s_cts.at[r], r_cts.at[r], sibling)

    send(lambda: ct_copy(y, up, 0))
    send(lambda: ct_copy(y, down, 1))

    for copy in loc[2:]:
        copy.wait()
    carrier = z == x
    diagonal = y == z
    turn = (y - z + 4) % 4

    def q_ref(i):
        return wqkv.at[:, pl.ds(pl.multiple_of(CB * i, 16), CB), half]

    def qa_copy():
        return remote(wown.at[0:3, :, half], q_ref(x), s_qa.at[0], r_qa.at[0], patch(y, y))

    def qa_local():
        return pltpu.make_async_copy(wown.at[0:3, :, half], q_ref(x), l_qa.at[0])

    def qb_copy(to_y, slot):
        return remote(q_ref(x), q_ref(x), s_qb.at[slot], r_qb.at[0], patch(to_y, z))

    qc = (q_ref, lambda i: s_qc.at[i], lambda i: r_qc.at[i])

    def qd_other(mask):
        ref = wqkv.at[:, :, mask]
        return remote(ref, ref, s_qd.at[0], r_qd.at[0], sibling)

    send(lambda: cw_copy(y, up, 0))
    send(lambda: cw_copy(y, down, 1))

    def service_1():
        ct_copy(down, y, 0).wait_recv()
        send(lambda: ct_copy(down, up, 2), c == 0)
        ct_copy(up, y, 1).wait_recv()
        send(lambda: ct_copy(up, down, 2), c == 1)
        for r in range(2):
            x_send(*cx(r))

    def service_2():
        ct_copy(opposite, y, 2).wait_recv()
        x_send(*cx(2))
        cw_copy(down, y, 0).wait_recv()
        send(lambda: cw_copy(down, up, 2), c == 0)
        cw_copy(up, y, 1).wait_recv()
        send(lambda: cw_copy(up, down, 2), c == 1)
        for r in range(2):
            send(lambda r=r: cw_other(r, half))
        for r in range(2):
            x_relay(*cx(r))

    def service_3():
        send(qa_copy, carrier & (z != y))
        when(carrier & diagonal, lambda: qa_local().start())
        x_relay(*cx(2))

    services = {1: service_1, 2: service_2, 3: service_3}

    for yy in range(4):
        rows = lax.broadcasted_iota(jnp.int32, (CZ, CZ), 0) - CB * z
        cols = lax.broadcasted_iota(jnp.int32, (CZ, CZ), 1) - CB * yy
        hit = (rows == cols) & (cols >= 0) & (cols < CB)
        sel[CZ * yy : CZ * yy + CZ, :] = jnp.where(hit, 1.0, 0.0).astype(BF16)

    for d in range(1, 16):
        q = (p + 16 - d) % 16
        remote(st1s, st1.at[q], s_st1.at[d], r_st1.at[d], {"batch": b, "patch": q}).wait_recv()
    def to_lanes(x, n):
        full = jnp.concatenate([x[j : j + 1, :] for j in range(n)], axis=1)
        return full

    stats = st1[...]
    stats_sum = jnp.sum(stats, axis=0)
    stats_dev = jnp.sum(jnp.square(stats - (stats_sum * (1.0 / 16))[None]), axis=0)
    centre = stats_sum[0:1, :] * (1.0 / 16)
    spread = (stats_sum[1:2, :] + (BLK * GROUP) * stats_dev[0:1, :]) * (1.0 / (2048 * GROUP))
    gn1[0] = to_channels(jnp.broadcast_to(centre, (8, 128)), C)
    gn1[1] = to_channels(jnp.broadcast_to(lax.rsqrt(spread + EPS), (8, 128)), C)

    def activate(start, count):
        def body(i, carry):
            rows = pl.ds(pl.multiple_of(start + 16 * i, 16), 16)
            v = lat[rows].astype(F32)
            v = (v - gn1[0, 0:1, :]) * gn1[1, 0:1, :]
            act[rows] = (v / (1.0 + jnp.exp(-v))).astype(BF16)
            return carry

        lax.fori_loop(0, count // 16, body, 0)

    activate(64 + BLK * z, BLK)

    def halo_up():
        return remote(
            lat.at[pl.ds(512, 64)], lat.at[pl.ds(0, 64)], s_halo.at[0], r_halo.at[0], patch(y + 1, z)
        )

    def halo_down():
        return remote(
            lat.at[pl.ds(64, 64)], lat.at[pl.ds(576, 64)], s_halo.at[1], r_halo.at[1], patch(y - 1, z)
        )

    send(halo_up, (z == 3) & (y < 3))
    send(halo_down, (z == 0) & (y > 0))
    for k in range(1, 4):
        def below(k=k):
            lat_copy(z - k, 0).wait_recv()

        def above(k=k):
            lat_copy(z + k, 1).wait_recv()

        when(z - k >= 0, below)
        send(lambda k=k: lat_copy(z - k, 0), (z - k >= 0) & (z < 3))
        when(z + k <= 3, above)
        send(lambda k=k: lat_copy(z + k, 1), (z + k <= 3) & (z > 0))
        send(halo_up, (z + k == 3) & (y < 3))
        send(halo_down, (z - k == 0) & (y > 0))
        services[k]()
        when(z - k >= 0, lambda k=k: activate(64 + BLK * (z - k), BLK))
        when(z + k <= 3, lambda k=k: activate(64 + BLK * (z + k), BLK))

    def wo_ref(yy, i):
        return wo.at[yy, i, :, half]

    def wo_local():
        return pltpu.make_async_copy(wown.at[3, :, half], wo_ref(y, x), l_qa.at[1])

    def wo_z(to_z, slot):
        return remote(wo_ref(y, x), wo_ref(y, x), s_woz.at[slot], r_woz.at[0], patch(y, to_z))

    when(carrier, lambda: wo_local().start())
    when(carrier, lambda: wo_local().wait())
    send(lambda: wo_z(z + 1, 0), carrier & (z < 3))
    send(lambda: wo_z(z - 1, 1), carrier & (z > 0))

    when(y > 0, lambda: halo_up().wait_recv())
    when(y > 0, lambda: activate(0, 64))
    when(y < 3, lambda: halo_down().wait_recv())
    when(y < 3, lambda: activate(576, 64))

    def zero_top():
        act[0:64] = jnp.zeros((64, C), BF16)

    def zero_bottom():
        act[576:640] = jnp.zeros((64, C), BF16)

    when(y == 0, zero_top)
    when(y == 3, zero_bottom)

    cw_copy(opposite, y, 2).wait_recv()
    send(lambda: cw_other(2, half))
    for r in range(3):
        x_wait(*cx(r), 2)
        send(lambda r=r: ct_other(r, half))

    def wo_y(src_y, to_y, slot):
        return remote(wo_ref(src_y, x), wo_ref(src_y, x), s_woy.at[slot], r_woy.at[slot], patch(to_y, z))

    wox = (lambda i: wo.at[:, i, :, half], lambda i: s_wox.at[i], lambda i: r_wox.at[i])

    when(diagonal & (z != x), lambda: qa_copy().wait_recv())
    when(diagonal & carrier, lambda: qa_local().wait())
    send(lambda: qb_copy(up, 0), diagonal)
    send(lambda: qb_copy(down, 1), diagonal)
    x_send_if(diagonal, *qc)
    when(z != x, lambda: wo_z(z, 0).wait_recv())
    send(lambda: wo_z(z + 1, 0), (z > x) & (z < 3))
    send(lambda: wo_z(z - 1, 1), (z < x) & (z > 0))
    send(lambda: wo_y(y, up, 0))
    send(lambda: wo_y(y, down, 1))
    for r in range(3):
        cw_other(r, other).wait_recv()
        ct_other(r, other).wait_recv()

    bias = jnp.concatenate([st1[4 * yy + z, 2:3, 0:CB] for yy in range(4)], axis=1)
    CHUNK = 256

    def conv_chunk(j, carry):
        total = jnp.zeros((CHUNK, 3 * CZ), F32)
        for dr in range(3):
            rows = pl.ds(pl.multiple_of(CHUNK * j + 64 * dr, 64), CHUNK)
            total = total + dot_nt(act[rows], cw[3 * dr : 3 * dr + 3].reshape(3 * CZ, C))
        ubuf[...] = total
        column = lax.broadcasted_iota(jnp.int32, (CHUNK, CZ), 0) % 64
        left = pltpu.roll(ubuf[:, 0:CZ], 1, 0)
        right = pltpu.roll(ubuf[:, 2 * CZ : 3 * CZ], CHUNK - 1, 0)
        value = ubuf[:, CZ : 2 * CZ]
        value = value + jnp.where(column == 0, 0.0, left) + jnp.where(column == 63, 0.0, right)
        own = lat[pl.ds(pl.multiple_of(64 + CHUNK * j, 64), CHUNK)]
        value = value + dot_nn(own, sel[...]) + bias
        value = value.astype(BF16).astype(F32)
        mean = jnp.sum(value, axis=0, keepdims=True) * (1.0 / CHUNK)
        stc[j, 0:1, :] = mean
        stc[j, 1:2, :] = jnp.sum(jnp.square(value - mean), axis=0, keepdims=True)
        for i in range(CHUNK // R):
            upper = value[R * i : R * i + HALF]
            lower = value[R * i + HALF : R * i + R]
            ch = (CHUNK // R) * j + i
            hidg[z, ch, 0] = upper[:, 0:128].astype(BF16)
            hidg[z, ch, 1] = upper[:, 128:256].astype(BF16)
            hidg[z, ch, 2] = lower[:, 0:128].astype(BF16)
            hidg[z, ch, 3] = lower[:, 128:256].astype(BF16)
            hidg[z, ch, 4] = jnp.concatenate([upper[:, 256:CZ], lower[:, 256:CZ]], axis=1).astype(BF16)
        return carry

    def hid_copy(ch, k, way):
        zz = z + 1 if way == 0 else z - 1
        ref = hidg.at[k, ch]
        return remote(ref, ref, s_hid.at[way, ch, k], r_hid.at[ch, k], patch(y, zz))

    def hid_own(ch):
        send(lambda: hid_copy(ch, z, 0), z < 3)
        send(lambda: hid_copy(ch, z, 1), z > 0)

    conv_chunk(0, 0)
    hid_own(0)
    beside = (turn == 1) | (turn == 3)
    when(beside, lambda: qb_copy(up, 0).wait_recv())
    send(lambda: qb_copy(up, 2), (turn == 1) & (c == 0))
    send(lambda: qb_copy(down, 2), (turn == 3) & (c == 1))
    x_send_if(beside, *qc)
    conv_chunk(1, 0)

    st2s[...] = jnp.zeros_like(st2s)
    mean = 0.5 * (stc[0, 0:1, :] + stc[1, 0:1, :])
    m2 = stc[0, 1:2, :] + stc[1, 1:2, :]
    m2 = m2 + CHUNK * (jnp.square(stc[0, 0:1, :] - mean) + jnp.square(stc[1, 0:1, :] - mean))
    for j in range(3):
        width = min(128, CZ - 128 * j)
        st2s[j : j + 1, 0:width] = mean[:, 128 * j : 128 * j + width]
        st2s[4 + j : 5 + j, 0:width] = m2[:, 128 * j : 128 * j + width]
    for d in range(1, 16):
        send(
            lambda d=d: remote(
                st2s, st2.at[p], s_st2.at[d], r_st2.at[d], {"batch": b, "patch": (p + d) % 16}
            )
        )
    st2[p] = st2s[...]

    when(turn == 2, lambda: qb_copy(up, 0).wait_recv())
    x_send_if(turn == 2, *qc)
    wo_y(down, y, 0).wait_recv()
    send(lambda: wo_y(down, up, 2), c == 0)
    wo_y(up, y, 1).wait_recv()
    send(lambda: wo_y(up, down, 2), c == 1)

    def second_norm():
        for d in range(1, 16):
            q = (p + 16 - d) % 16
            remote(st2s, st2.at[q], s_st2.at[d], r_st2.at[d], {"batch": b, "patch": q}).wait_recv()
        parts = [[st2[4 * yy + zz] for zz in range(4)] for yy in range(4)]
        mean_rows, m2_rows = [], []
        for zz in range(4):
            col = [parts[yy][zz] for yy in range(4)]
            m = (col[0] + col[1] + col[2] + col[3]) * 0.25
            dev = sum(jnp.square(x - m) for x in col)
            total = col[0] + col[1] + col[2] + col[3]
            m2_all = total[4:8] + ROWS_Y * dev[0:4]
            mean_rows.append(to_lanes(m, 3)[:, 0:CZ])
            m2_rows.append(to_lanes(m2_all, 3)[:, 0:CZ])
        mean_l = jnp.concatenate(mean_rows + mean_rows, axis=0)
        m2_l = jnp.concatenate(m2_rows + m2_rows, axis=0)
        centre = group_sums(mean_l) * (1.0 / GROUP)
        spread = group_sums(m2_l + 2048.0 * jnp.square(mean_l - centre)) * (1.0 / (2048 * GROUP))
        gn2[0] = centre
        gn2[1] = lax.rsqrt(spread + EPS)

    def hidden_rows(zz, ch, h, rows):
        tail = hidg[zz, ch, 4, rows, :].astype(F32)[:, 64 * h : 64 * h + 64]
        return jnp.concatenate(
            [hidg[zz, ch, 2 * h, rows, :].astype(F32), hidg[zz, ch, 2 * h + 1, rows, :].astype(F32), tail],
            axis=1,
        )

    def in_order(blocks):
        return jnp.concatenate(
            [blocks[zz][:, CB * yy : CB * yy + CB] for yy in range(4) for zz in range(4)], axis=1
        )

    def normalize(ch):
        for h in range(2):
            def body(i, carry, h=h):
                rows = pl.ds(pl.multiple_of(16 * i, 16), 16)
                blocks = [
                    (hidden_rows(zz, ch, h, rows) - gn2[0, zz : zz + 1, :]) * gn2[1, zz : zz + 1, :]
                    for zz in range(4)
                ]
                nrm[pl.ds(pl.multiple_of(HALF * h + 16 * i, 16), 16)] = in_order(blocks).astype(BF16)
                return carry

            lax.fori_loop(0, HALF // 16, body, 0)

    def project(ch):
        rows = pl.ds(R * ch, R)
        both = dot_nt(nrm[...], wqkv[...].reshape(3 * CZ, C))
        kv[y, rows, 0:256] = both[:, CZ : CZ + 256].astype(BF16)
        kv[y, rows, 256:512] = both[:, 2 * CZ : 2 * CZ + 256].astype(BF16)
        kv[y, rows, 512:640] = jnp.concatenate(
            [both[:, CZ + 256 : 2 * CZ], both[:, 2 * CZ + 256 : 3 * CZ]], axis=1
        ).astype(BF16)
        query = (both[:, 0:CZ].astype(BF16).astype(F32) * HEAD_DIM**-0.5).astype(BF16)
        qb[rows, 0:256] = query[:, 0:256]
        qb[rows, 256:384] = jnp.concatenate(
            [query[:, 256:CZ].astype(F32), jnp.zeros((R, 64), F32)], axis=1
        ).astype(BF16)

    def kv_copy(ch, h, src_y, to_y, slot):
        ref = kv.at[src_y, pl.ds(R * ch + HALF * h, HALF), :]
        return remote(ref, ref, s_kv.at[ch, h, slot], r_kv.at[ch, h, slot], patch(to_y, z))

    def kv_own(ch):
        send(lambda: kv_copy(ch, 0, y, up, 0))
        send(lambda: kv_copy(ch, 1, y, down, 1))
        send(lambda: kv_copy(ch, 1, y, up, 0))
        send(lambda: kv_copy(ch, 0, y, down, 1))

    def kv_on(ch):
        kv_copy(ch, 0, down, y, 0).wait_recv()
        send(lambda: kv_copy(ch, 0, down, up, 2))
        kv_copy(ch, 1, up, y, 1).wait_recv()
        send(lambda: kv_copy(ch, 1, up, down, 2))

    def hid_on(ch):
        for k in range(1, 4):
            when(z - k >= 0, lambda k=k: hid_copy(ch, z - k, 0).wait_recv())
            send(lambda k=k: hid_copy(ch, z - k, 0), (z - k >= 0) & (z < 3))
            when(z + k <= 3, lambda k=k: hid_copy(ch, z + k, 1).wait_recv())
            send(lambda k=k: hid_copy(ch, z + k, 1), (z + k <= 3) & (z > 0))
            if k == AHEAD and ch + 1 < NCH:
                hid_own(ch + 1)

    def process(ch):
        normalize(ch)
        project(ch)
        kv_own(ch)
        if ch > 0:
            kv_on(ch - 1)

    hid_on(0)
    x_relay(*qc)
    hid_on(1)
    second_norm()
    x_wait(*qc, 2)
    send(lambda: qd_other(half))
    wo_y(opposite, y, 2).wait_recv()
    x_send(*wox)
    hid_on(2)
    qd_other(other).wait_recv()
    process(0)
    process(1)
    hid_on(3)
    process(2)
    process(3)

    for h in range(2):
        def residual(i, carry, h=h):
            rows = pl.ds(pl.multiple_of(16 * i, 16), 16)
            blocks = [hidden_rows(zz, z, h, rows) for zz in range(4)]
            hnat[pl.ds(pl.multiple_of(HALF * h + 16 * i, 16), 16)] = in_order(blocks)
            return carry

        lax.fori_loop(0, HALF // 16, residual, 0)

    kv_on(NCH - 1)
    def wo_other(mask):
        ref = wo.at[:, :, :, mask]
        return remote(ref, ref, s_wos.at[0], r_wos.at[0], sibling)

    x_relay(*wox)
    for ch in range(NCH):
        kv_copy(ch, 1, down, y, 0).wait_recv()
        kv_copy(ch, 0, up, y, 1).wait_recv()
        kv_copy(ch, 0, opposite, y, 2).wait_recv()
        kv_copy(ch, 1, opposite, y, 2).wait_recv()

    def att_copy(j):
        return remote(att.at[j], attg.at[z], s_att.at[j], r_att.at[z], patch(y, j))

    def att_from(k):
        return remote(att.at[k], attg.at[k], s_att.at[k], r_att.at[k], patch(y, k))

    def attend(j):
        rows = pl.ds(pl.multiple_of(BLK * j, 128), BLK)
        for pair in range(3):
            width = min(128, CZ - 128 * pair)
            lanes = slice(128 * pair, 128 * pair + width)
            query = qb[rows, 128 * pair : 128 * pair + 128]
            key_at = 128 * pair if pair < 2 else 512
            value_at = key_at + 256 if pair < 2 else 512
            keys = kv[:, :, key_at : key_at + 128].reshape(2048, 128)
            values = kv[:, :, value_at : value_at + 128].reshape(2048, 128)
            lane = lax.broadcasted_iota(jnp.int32, (BLK, 128), 1)
            result = None
            for side in range(width // 64):
                q1 = query
                if width > 64:
                    keep = (lane >= 64 * side) & (lane < 64 * side + 64)
                    q1 = jnp.where(keep, query.astype(F32), 0.0).astype(BF16)
                scores = dot_nt(q1, keys)
                peak = jnp.max(scores, axis=1, keepdims=True)
                unnormalized = jnp.exp(scores - peak)
                row_total = jnp.sum(unnormalized, axis=1, keepdims=True)
                mix = dot_nn(unnormalized.astype(BF16), values) / row_total
                result = mix if result is None else jnp.where(lane < 64, result, mix)
            if width == 64:
                result = result[:, 64:128]
            att[j, :, lanes] = result.astype(BF16)

    def attend_step(t, carry):
        j = (z + 1 + t) % 4
        attend(j)
        pl.when(t < 3)(lambda: att_copy(j).start())
        return carry

    lax.fori_loop(0, 2, attend_step, 0)
    x_wait(*wox, 2)
    send(lambda: wo_other(half))
    lax.fori_loop(2, 4, attend_step, 0)
    attg[z] = att[z]
    for k in range(4):
        pending.append((z != k, lambda k=k: att_copy(k)))

    wo_other(other).wait_recv()
    for k in range(4):
        when(z != k, lambda k=k: att_from(k).wait_recv())

    whole = jnp.concatenate([attg[k].astype(F32) for k in range(4)], axis=1).astype(BF16)
    out_ref[...] = (hnat[...] + dot_nt(whole, wo[...].reshape(C, C))).astype(BF16)

    for cond, make in pending:
        when(cond, lambda make=make: make().wait_send())


def on_device(latent, conv_weight, channel_bias, w_query, w_key, w_value, w_out):
    any_space = pl.BlockSpec(memory_space=pl.ANY)
    vmem = pl.BlockSpec(memory_space=pltpu.VMEM)
    dma = pltpu.SemaphoreType.DMA
    out = pl.pallas_call(
        kernel,
        out_shape=jax.ShapeDtypeStruct((BLK, C), BF16),
        in_specs=[any_space, any_space, vmem, any_space, any_space, any_space, any_space],
        out_specs=vmem,
        scratch_shapes=[
            pltpu.VMEM((640, C), BF16),
            pltpu.VMEM((640, C), BF16),
            pltpu.VMEM((9, 4, CB, C), BF16),
            pltpu.VMEM((4, CB, C), BF16),
            pltpu.VMEM((3, CZ, C), BF16),
            pltpu.VMEM((4, 4, CB, C), BF16),
            pltpu.VMEM((8, 128), F32),
            pltpu.VMEM((16, 8, 128), F32),
            pltpu.VMEM((8, 128), F32),
            pltpu.VMEM((16, 8, 128), F32),
            pltpu.VMEM((C, 128), BF16),
            pltpu.VMEM((128, C), BF16),
            pltpu.VMEM((C, CZ), BF16),
            pltpu.VMEM((2, 8, C), F32),
            pltpu.VMEM((2, 8, CZ), F32),
            pltpu.VMEM((2, 8, CZ), F32),
            pltpu.VMEM((256, 3 * CZ), F32),
            pltpu.VMEM((4, NCH, 5, HALF, 128), BF16),
            pltpu.VMEM((R, C), BF16),
            pltpu.VMEM((BLK, C), F32),
            pltpu.VMEM((ROWS_Y, 384), BF16),
            pltpu.VMEM((4, ROWS_Y, 2 * CZ), BF16),
            pltpu.VMEM((4, BLK, CZ), BF16),
            pltpu.VMEM((4, BLK, CZ), BF16),
            dma((6,)), dma((16,)), dma((16,)), dma((2, 4)), dma((4,)), dma((2,)), dma((2,)),
            dma((3,)), dma((3,)), dma((3,)), dma((3,)),
            dma((3,)), dma((3,)), dma((3, 4)), dma((3, 4)), dma((3,)), dma((3,)),
            dma((1,)), dma((1,)), dma((2,)), dma((3,)), dma((1,)), dma((3,)), dma((3,)), dma((1,)), dma((1,)),
            dma((2,)), dma((1,)), dma((3,)), dma((3,)), dma((3,)), dma((3,)), dma((1,)), dma((1,)),
            dma((16,)), dma((16,)), dma((2, NCH, 4)), dma((NCH, 4)), dma((NCH, 2, 3)), dma((NCH, 2, 3)),
            dma((4,)), dma((4,)),
        ],
        compiler_params=pltpu.CompilerParams(
            collective_id=0, has_side_effects=True, vmem_limit_bytes=60 * 1024 * 1024
        ),
    )(
        latent.reshape(BLK, C), conv_weight.reshape(9, CB, C), channel_bias.reshape(1, CB), w_query, w_key, w_value, w_out
    )
    return out.reshape(latent.shape)


def solution(mesh):
    return jax.shard_map(
        on_device,
        mesh=mesh,
        in_specs=(
            P(("batch", "patch"), None, None),
            P(None, None, "patch", None),
            P("patch"),
            P("patch", None),
            P("patch", None),
            P("patch", None),
            P("patch", None),
        ),
        out_specs=P(("batch", "patch"), None, None),
        check_vma=False,
    )
```

```python
import jax
import jax.numpy as jnp
from jax import lax
from jax.experimental import pallas as pl
from jax.experimental.pallas import tpu as pltpu
from jax.sharding import PartitionSpec as P

C = 1280
HEADS = 20
HEAD_DIM = 64
GROUPS = 32
GROUP = C // GROUPS
NY, NZ = 4, 4
BLK = 128
ROWS_Y = 512
NCH = 4
R = ROWS_Y // NCH
HALF = R // 2
AHEAD = 1
CB = C // 16
CZ = C // 4
EPS = 1e-05
MESH = pl.DeviceIdType.MESH
F32 = jnp.float32
BF16 = jnp.bfloat16


def dot_nt(left, right):
    return lax.dot_general(left, right, (((1,), (1,)), ((), ())), preferred_element_type=F32)


def dot_nn(left, right):
    return lax.dot_general(left, right, (((1,), (0,)), ((), ())), preferred_element_type=F32)


def kernel(
    lat_in, cw_in, bias_in, wq_in, wk_in, wv_in, wo_in, out_ref,
    lat, act, cw, wown, wqkv, wo, st1s, st1, st2s, st2, gmat, gmat_t, sel,
    gn1, gn2, stc, ubuf, hidg, nrm, hnat, qb, kv, att, attg,
    s_loc, s_st1, r_st1, s_lat, r_lat, s_halo, r_halo, s_cw, r_cw, s_cws, r_cws,
    s_ct, r_ct, s_cx, r_cx, s_cts, r_cts,
    s_qa, r_qa, l_qa, s_qb, r_qb, s_qc, r_qc, s_qd, r_qd, s_woz, r_woz, s_woy, r_woy, s_wox, r_wox, s_wos, r_wos,
    s_st2, r_st2, s_hid, r_hid, s_kv, r_kv, s_att, r_att,
):
    p = lax.axis_index("patch")
    b = lax.axis_index("batch")
    y = p // 4
    z = p % 4
    c = b % 2
    x = (b // 2) % 4
    sib = b + 1 - 2 * c
    up = (y + 1) % 4
    down = (y + 3) % 4
    opposite = (y + 2) % 4
    half = pl.ds(pl.multiple_of(c * (C // 2), 128), C // 2)
    other = pl.ds(pl.multiple_of((1 - c) * (C // 2), 128), C // 2)
    pending = []

    def patch(yy, zz):
        return {"batch": b, "patch": 4 * yy + zz}

    def across(d):
        return {"batch": b - 2 * x + 2 * ((x + d) % 4), "patch": p}

    sibling = {"batch": sib, "patch": p}

    def remote(src, dst, ssem, rsem, dev):
        return pltpu.make_async_remote_copy(
            src_ref=src, dst_ref=dst, send_sem=ssem, recv_sem=rsem, device_id=dev, device_id_type=MESH
        )

    def when(cond, f):
        if cond is None:
            f()
        else:
            pl.when(cond)(f)

    def send(make, cond=None):
        when(cond, lambda: make().start())
        pending.append((cond, make))

    own_rows = pl.ds(pl.multiple_of(64 + BLK * z, 64), BLK)
    loc = [
        pltpu.make_async_copy(lat_in, lat.at[own_rows], s_loc.at[0]),
        pltpu.make_async_copy(cw_in, cw.at[:, y], s_loc.at[1]),
        pltpu.make_async_copy(wq_in, wown.at[0], s_loc.at[2]),
        pltpu.make_async_copy(wk_in, wown.at[1], s_loc.at[3]),
        pltpu.make_async_copy(wv_in, wown.at[2], s_loc.at[4]),
        pltpu.make_async_copy(wo_in, wown.at[3], s_loc.at[5]),
    ]
    for copy in loc:
        copy.start()
    barrier = pltpu.get_barrier_semaphore()
    for d in range(1, 16):
        pl.semaphore_signal(
            barrier, inc=1, device_id={"batch": b, "patch": (p + d) % 16}, device_id_type=MESH
        )
    pl.semaphore_signal(barrier, inc=1, device_id=sibling, device_id_type=MESH)
    for d in range(1, 4):
        pl.semaphore_signal(barrier, inc=1, device_id=across(d), device_id_type=MESH)

    gi = lax.broadcasted_iota(jnp.int32, (C, 128), 0) - GROUP * lax.broadcasted_iota(jnp.int32, (C, 128), 1)
    gmat[...] = jnp.where((gi >= 0) & (gi < GROUP), 1.0, 0.0).astype(BF16)
    ti = lax.broadcasted_iota(jnp.int32, (128, C), 1) - GROUP * lax.broadcasted_iota(jnp.int32, (128, C), 0)
    gmat_t[...] = jnp.where((ti >= 0) & (ti < GROUP), 1.0, 0.0).astype(BF16)
    def split_rows(x):
        hi = x.astype(BF16).astype(F32)
        mid = (x - hi).astype(BF16).astype(F32)
        return jnp.concatenate([hi, mid, x - hi - mid], axis=0).astype(BF16)

    def join_rows(x):
        return x[0:8] + x[8:16] + x[16:24]

    def to_groups(x):
        return join_rows(dot_nn(split_rows(x), gmat[0 : x.shape[1], :]))

    def to_channels(x, n):
        return join_rows(dot_nn(split_rows(x), gmat_t[:, 0:n]))

    def group_sums(x):
        return to_channels(to_groups(x), x.shape[1])

    st1s[...] = jnp.zeros_like(st1s)
    loc[0].wait()
    mine = lat[own_rows].astype(F32)
    mean = jnp.sum(mine, axis=0, keepdims=True) * (1.0 / BLK)
    m2 = jnp.sum(jnp.square(mine - mean), axis=0, keepdims=True)
    mean = jnp.broadcast_to(mean, (8, C))
    group_mean = to_groups(mean) * (1.0 / GROUP)
    group_m2 = to_groups(m2 + BLK * jnp.square(mean - to_channels(group_mean, C)))
    st1s[0:1, :] = group_mean[0:1, :]
    st1s[1:2, :] = group_m2[0:1, :]
    st1s[2:3, 0:CB] = bias_in[...]

    pl.semaphore_wait(barrier, 19)

    for d in range(1, 16):
        send(
            lambda d=d: remote(
                st1s, st1.at[p], s_st1.at[d], r_st1.at[d], {"batch": b, "patch": (p + d) % 16}
            )
        )
    st1[p] = st1s[...]

    def lat_rows(k):
        return lat.at[pl.ds(pl.multiple_of(64 + BLK * k, 64), BLK)]

    def lat_copy(k, way):
        zz = z + 1 if way == 0 else z - 1
        return remote(lat_rows(k), lat_rows(k), s_lat.at[way, k], r_lat.at[k], patch(y, zz))

    send(lambda: lat_copy(z, 0), z < 3)
    send(lambda: lat_copy(z, 1), z > 0)

    loc[1].wait()
    around = (down, up, opposite)

    def cw_ref(src_y, mask):
        return cw.at[0:5, src_y, :, mask]

    def cw_copy(src_y, to_y, slot):
        ref = cw_ref(src_y, half)
        return remote(ref, ref, s_cw.at[slot], r_cw.at[slot], patch(to_y, z))

    def cw_other(r, mask):
        ref = cw_ref(around[r], mask)
        return remote(ref, ref, s_cws.at[r], r_cws.at[r], sibling)

    def ct_copy(src_y, to_y, slot):
        ref = cw.at[5 + x, src_y, :, half]
        return remote(ref, ref, s_ct.at[slot], r_ct.at[slot], patch(to_y, z))

    nexts = ((x + 1) % 4, (x + 3) % 4, (x + 2) % 4)

    def x_send_if(cond, ref, ssem, rsem):
        send(lambda: remote(ref(x), ref(x), ssem(0), rsem(1), across(1)), cond)
        send(lambda: remote(ref(x), ref(x), ssem(1), rsem(0), across(3)), cond)

    def x_send(ref, ssem, rsem):
        x_send_if(None, ref, ssem, rsem)

    def x_wait(ref, ssem, rsem, i):
        remote(ref(nexts[i]), ref(nexts[i]), ssem(i), rsem(i), across(1)).wait_recv()

    def x_relay(ref, ssem, rsem):
        x_wait(ref, ssem, rsem, 1)
        send(lambda: remote(ref(nexts[1]), ref(nexts[1]), ssem(2), rsem(2), across(1)), c == 0)
        x_wait(ref, ssem, rsem, 0)
        send(lambda: remote(ref(nexts[0]), ref(nexts[0]), ssem(2), rsem(2), across(3)), c == 1)

    def cx(r):
        return (
            lambda i: cw.at[5 + i, around[r], :, half],
            lambda i: s_cx.at[r, i],
            lambda i: r_cx.at[r, i],
        )

    def ct_other(r, mask):
        ref = cw.at[5:9, around[r], :, mask]
        return remote(ref, ref, s_cts.at[r], r_cts.at[r], sibling)

    send(lambda: ct_copy(y, up, 0))
    send(lambda: ct_copy(y, down, 1))

    for copy in loc[2:]:
        copy.wait()
    carrier = z == x
    diagonal = y == z
    turn = (y - z + 4) % 4

    def q_ref(i):
        return wqkv.at[:, pl.ds(pl.multiple_of(CB * i, 16), CB), half]

    def qa_copy():
        return remote(wown.at[0:3, :, half], q_ref(x), s_qa.at[0], r_qa.at[0], patch(y, y))

    def qa_local():
        return pltpu.make_async_copy(wown.at[0:3, :, half], q_ref(x), l_qa.at[0])

    def qb_copy(to_y, slot):
        return remote(q_ref(x), q_ref(x), s_qb.at[slot], r_qb.at[0], patch(to_y, z))

    qc = (q_ref, lambda i: s_qc.at[i], lambda i: r_qc.at[i])

    def qd_other(mask):
        ref = wqkv.at[:, :, mask]
        return remote(ref, ref, s_qd.at[0], r_qd.at[0], sibling)

    send(lambda: cw_copy(y, up, 0))
    send(lambda: cw_copy(y, down, 1))

    def service_1():
        ct_copy(down, y, 0).wait_recv()
        send(lambda: ct_copy(down, up, 2), c == 0)
        ct_copy(up, y, 1).wait_recv()
        send(lambda: ct_copy(up, down, 2), c == 1)
        for r in range(2):
            x_send(*cx(r))

    def service_2():
        ct_copy(opposite, y, 2).wait_recv()
        x_send(*cx(2))
        cw_copy(down, y, 0).wait_recv()
        send(lambda: cw_copy(down, up, 2), c == 0)
        cw_copy(up, y, 1).wait_recv()
        send(lambda: cw_copy(up, down, 2), c == 1)
        for r in range(2):
            send(lambda r=r: cw_other(r, half))
        send(qa_copy, carrier & (z != y))
        when(carrier & diagonal, lambda: qa_local().start())
        for r in range(2):
            x_relay(*cx(r))

    def service_3():
        x_relay(*cx(2))

    services = {1: service_1, 2: service_2, 3: service_3}

    for yy in range(4):
        rows = lax.broadcasted_iota(jnp.int32, (CZ, CZ), 0) - CB * z
        cols = lax.broadcasted_iota(jnp.int32, (CZ, CZ), 1) - CB * yy
        hit = (rows == cols) & (cols >= 0) & (cols < CB)
        sel[CZ * yy : CZ * yy + CZ, :] = jnp.where(hit, 1.0, 0.0).astype(BF16)

    for d in range(1, 16):
        q = (p + 16 - d) % 16
        remote(st1s, st1.at[q], s_st1.at[d], r_st1.at[d], {"batch": b, "patch": q}).wait_recv()
    def to_lanes(x, n):
        full = jnp.concatenate([x[j : j + 1, :] for j in range(n)], axis=1)
        return full

    stats = st1[...]
    stats_sum = jnp.sum(stats, axis=0)
    stats_dev = jnp.sum(jnp.square(stats - (stats_sum * (1.0 / 16))[None]), axis=0)
    centre = stats_sum[0:1, :] * (1.0 / 16)
    spread = (stats_sum[1:2, :] + (BLK * GROUP) * stats_dev[0:1, :]) * (1.0 / (2048 * GROUP))
    gn1[0] = to_channels(jnp.broadcast_to(centre, (8, 128)), C)
    gn1[1] = to_channels(jnp.broadcast_to(lax.rsqrt(spread + EPS), (8, 128)), C)

    def activate(start, count):
        def body(i, carry):
            rows = pl.ds(pl.multiple_of(start + 16 * i, 16), 16)
            v = lat[rows].astype(F32)
            v = (v - gn1[0, 0:1, :]) * gn1[1, 0:1, :]
            act[rows] = (v / (1.0 + jnp.exp(-v))).astype(BF16)
            return carry

        lax.fori_loop(0, count // 16, body, 0)

    activate(64 + BLK * z, BLK)

    def halo_up():
        return remote(
            lat.at[pl.ds(512, 64)], lat.at[pl.ds(0, 64)], s_halo.at[0], r_halo.at[0], patch(y + 1, z)
        )

    def halo_down():
        return remote(
            lat.at[pl.ds(64, 64)], lat.at[pl.ds(576, 64)], s_halo.at[1], r_halo.at[1], patch(y - 1, z)
        )

    send(halo_up, (z == 3) & (y < 3))
    send(halo_down, (z == 0) & (y > 0))
    for k in range(1, 4):
        def below(k=k):
            lat_copy(z - k, 0).wait_recv()

        def above(k=k):
            lat_copy(z + k, 1).wait_recv()

        when(z - k >= 0, below)
        send(lambda k=k: lat_copy(z - k, 0), (z - k >= 0) & (z < 3))
        when(z + k <= 3, above)
        send(lambda k=k: lat_copy(z + k, 1), (z + k <= 3) & (z > 0))
        send(halo_up, (z + k == 3) & (y < 3))
        send(halo_down, (z - k == 0) & (y > 0))
        services[k]()
        when(z - k >= 0, lambda k=k: activate(64 + BLK * (z - k), BLK))
        when(z + k <= 3, lambda k=k: activate(64 + BLK * (z + k), BLK))

    def wo_ref(yy, i):
        return wo.at[yy, i, :, half]

    def wo_local():
        return pltpu.make_async_copy(wown.at[3, :, half], wo_ref(y, x), l_qa.at[1])

    def wo_z(to_z, slot):
        return remote(wo_ref(y, x), wo_ref(y, x), s_woz.at[slot], r_woz.at[0], patch(y, to_z))

    when(carrier, lambda: wo_local().start())
    when(carrier, lambda: wo_local().wait())
    send(lambda: wo_z(z + 1, 0), carrier & (z < 3))
    send(lambda: wo_z(z - 1, 1), carrier & (z > 0))

    when(y > 0, lambda: halo_up().wait_recv())
    when(y > 0, lambda: activate(0, 64))
    when(y < 3, lambda: halo_down().wait_recv())
    when(y < 3, lambda: activate(576, 64))

    def zero_top():
        act[0:64] = jnp.zeros((64, C), BF16)

    def zero_bottom():
        act[576:640] = jnp.zeros((64, C), BF16)

    when(y == 0, zero_top)
    when(y == 3, zero_bottom)

    when(diagonal & (z != x), lambda: qa_copy().wait_recv())
    when(diagonal & carrier, lambda: qa_local().wait())
    send(lambda: qb_copy(up, 0), diagonal)
    send(lambda: qb_copy(down, 1), diagonal)
    x_send_if(diagonal, *qc)
    cw_copy(opposite, y, 2).wait_recv()
    send(lambda: cw_other(2, half))
    for r in range(3):
        x_wait(*cx(r), 2)
        send(lambda r=r: ct_other(r, half))

    def wo_y(src_y, to_y, slot):
        return remote(wo_ref(src_y, x), wo_ref(src_y, x), s_woy.at[slot], r_woy.at[slot], patch(to_y, z))

    wox = (lambda i: wo.at[:, i, :, half], lambda i: s_wox.at[i], lambda i: r_wox.at[i])

    for r in range(3):
        cw_other(r, other).wait_recv()
        ct_other(r, other).wait_recv()

    bias = jnp.concatenate([st1[4 * yy + z, 2:3, 0:CB] for yy in range(4)], axis=1)
    CHUNK = 256

    def conv_chunk(j, carry):
        total = jnp.zeros((CHUNK, 3 * CZ), F32)
        for dr in range(3):
            rows = pl.ds(pl.multiple_of(CHUNK * j + 64 * dr, 64), CHUNK)
            total = total + dot_nt(act[rows], cw[3 * dr : 3 * dr + 3].reshape(3 * CZ, C))
        ubuf[...] = total
        column = lax.broadcasted_iota(jnp.int32, (CHUNK, CZ), 0) % 64
        left = pltpu.roll(ubuf[:, 0:CZ], 1, 0)
        right = pltpu.roll(ubuf[:, 2 * CZ : 3 * CZ], CHUNK - 1, 0)
        value = ubuf[:, CZ : 2 * CZ]
        value = value + jnp.where(column == 0, 0.0, left) + jnp.where(column == 63, 0.0, right)
        own = lat[pl.ds(pl.multiple_of(64 + CHUNK * j, 64), CHUNK)]
        value = value + dot_nn(own, sel[...]) + bias
        value = value.astype(BF16).astype(F32)
        mean = jnp.sum(value, axis=0, keepdims=True) * (1.0 / CHUNK)
        stc[j, 0:1, :] = mean
        stc[j, 1:2, :] = jnp.sum(jnp.square(value - mean), axis=0, keepdims=True)
        for i in range(CHUNK // R):
            upper = value[R * i : R * i + HALF]
            lower = value[R * i + HALF : R * i + R]
            ch = (CHUNK // R) * j + i
            hidg[z, ch, 0] = upper[:, 0:128].astype(BF16)
            hidg[z, ch, 1] = upper[:, 128:256].astype(BF16)
            hidg[z, ch, 2] = lower[:, 0:128].astype(BF16)
            hidg[z, ch, 3] = lower[:, 128:256].astype(BF16)
            hidg[z, ch, 4] = jnp.concatenate([upper[:, 256:CZ], lower[:, 256:CZ]], axis=1).astype(BF16)
        return carry

    def hid_copy(ch, k, way):
        zz = z + 1 if way == 0 else z - 1
        ref = hidg.at[k, ch]
        return remote(ref, ref, s_hid.at[way, ch, k], r_hid.at[ch, k], patch(y, zz))

    def hid_own(ch):
        send(lambda: hid_copy(ch, z, 0), z < 3)
        send(lambda: hid_copy(ch, z, 1), z > 0)

    conv_chunk(0, 0)
    hid_own(0)
    beside = (turn == 1) | (turn == 3)
    when(beside, lambda: qb_copy(up, 0).wait_recv())
    send(lambda: qb_copy(up, 2), (turn == 1) & (c == 0))
    send(lambda: qb_copy(down, 2), (turn == 3) & (c == 1))
    x_send_if(beside, *qc)
    conv_chunk(1, 0)

    st2s[...] = jnp.zeros_like(st2s)
    mean = 0.5 * (stc[0, 0:1, :] + stc[1, 0:1, :])
    m2 = stc[0, 1:2, :] + stc[1, 1:2, :]
    m2 = m2 + CHUNK * (jnp.square(stc[0, 0:1, :] - mean) + jnp.square(stc[1, 0:1, :] - mean))
    for j in range(3):
        width = min(128, CZ - 128 * j)
        st2s[j : j + 1, 0:width] = mean[:, 128 * j : 128 * j + width]
        st2s[4 + j : 5 + j, 0:width] = m2[:, 128 * j : 128 * j + width]
    for d in range(1, 16):
        send(
            lambda d=d: remote(
                st2s, st2.at[p], s_st2.at[d], r_st2.at[d], {"batch": b, "patch": (p + d) % 16}
            )
        )
    st2[p] = st2s[...]

    when(turn == 2, lambda: qb_copy(up, 0).wait_recv())
    x_send_if(turn == 2, *qc)
    when(z != x, lambda: wo_z(z, 0).wait_recv())
    send(lambda: wo_z(z + 1, 0), (z > x) & (z < 3))
    send(lambda: wo_z(z - 1, 1), (z < x) & (z > 0))
    send(lambda: wo_y(y, up, 0))
    send(lambda: wo_y(y, down, 1))

    def second_norm():
        for d in range(1, 16):
            q = (p + 16 - d) % 16
            remote(st2s, st2.at[q], s_st2.at[d], r_st2.at[d], {"batch": b, "patch": q}).wait_recv()
        parts = [[st2[4 * yy + zz] for zz in range(4)] for yy in range(4)]
        mean_rows, m2_rows = [], []
        for zz in range(4):
            col = [parts[yy][zz] for yy in range(4)]
            m = (col[0] + col[1] + col[2] + col[3]) * 0.25
            dev = sum(jnp.square(x - m) for x in col)
            total = col[0] + col[1] + col[2] + col[3]
            m2_all = total[4:8] + ROWS_Y * dev[0:4]
            mean_rows.append(to_lanes(m, 3)[:, 0:CZ])
            m2_rows.append(to_lanes(m2_all, 3)[:, 0:CZ])
        mean_l = jnp.concatenate(mean_rows + mean_rows, axis=0)
        m2_l = jnp.concatenate(m2_rows + m2_rows, axis=0)
        centre = group_sums(mean_l) * (1.0 / GROUP)
        spread = group_sums(m2_l + 2048.0 * jnp.square(mean_l - centre)) * (1.0 / (2048 * GROUP))
        gn2[0] = centre
        gn2[1] = lax.rsqrt(spread + EPS)

    def hidden_rows(zz, ch, h, rows):
        tail = hidg[zz, ch, 4, rows, :].astype(F32)[:, 64 * h : 64 * h + 64]
        return jnp.concatenate(
            [hidg[zz, ch, 2 * h, rows, :].astype(F32), hidg[zz, ch, 2 * h + 1, rows, :].astype(F32), tail],
            axis=1,
        )

    def in_order(blocks):
        return jnp.concatenate(
            [blocks[zz][:, CB * yy : CB * yy + CB] for yy in range(4) for zz in range(4)], axis=1
        )

    def normalize(ch):
        for h in range(2):
            def body(i, carry, h=h):
                rows = pl.ds(pl.multiple_of(16 * i, 16), 16)
                blocks = [
                    (hidden_rows(zz, ch, h, rows) - gn2[0, zz : zz + 1, :]) * gn2[1, zz : zz + 1, :]
                    for zz in range(4)
                ]
                nrm[pl.ds(pl.multiple_of(HALF * h + 16 * i, 16), 16)] = in_order(blocks).astype(BF16)
                return carry

            lax.fori_loop(0, HALF // 16, body, 0)

    def project(ch):
        rows = pl.ds(R * ch, R)
        both = dot_nt(nrm[...], wqkv[...].reshape(3 * CZ, C))
        kv[y, rows, 0:256] = both[:, CZ : CZ + 256].astype(BF16)
        kv[y, rows, 256:512] = both[:, 2 * CZ : 2 * CZ + 256].astype(BF16)
        kv[y, rows, 512:640] = jnp.concatenate(
            [both[:, CZ + 256 : 2 * CZ], both[:, 2 * CZ + 256 : 3 * CZ]], axis=1
        ).astype(BF16)
        query = (both[:, 0:CZ].astype(BF16).astype(F32) * HEAD_DIM**-0.5).astype(BF16)
        qb[rows, 0:256] = query[:, 0:256]
        qb[rows, 256:384] = jnp.concatenate(
            [query[:, 256:CZ].astype(F32), jnp.zeros((R, 64), F32)], axis=1
        ).astype(BF16)

    def kv_copy(ch, h, src_y, to_y, slot):
        ref = kv.at[src_y, pl.ds(R * ch + HALF * h, HALF), :]
        return remote(ref, ref, s_kv.at[ch, h, slot], r_kv.at[ch, h, slot], patch(to_y, z))

    def kv_own(ch):
        send(lambda: kv_copy(ch, 0, y, up, 0))
        send(lambda: kv_copy(ch, 1, y, down, 1))
        send(lambda: kv_copy(ch, 1, y, up, 0))
        send(lambda: kv_copy(ch, 0, y, down, 1))

    def kv_on(ch):
        kv_copy(ch, 0, down, y, 0).wait_recv()
        send(lambda: kv_copy(ch, 0, down, up, 2))
        kv_copy(ch, 1, up, y, 1).wait_recv()
        send(lambda: kv_copy(ch, 1, up, down, 2))

    def hid_on(ch):
        for k in range(1, 4):
            when(z - k >= 0, lambda k=k: hid_copy(ch, z - k, 0).wait_recv())
            send(lambda k=k: hid_copy(ch, z - k, 0), (z - k >= 0) & (z < 3))
            when(z + k <= 3, lambda k=k: hid_copy(ch, z + k, 1).wait_recv())
            send(lambda k=k: hid_copy(ch, z + k, 1), (z + k <= 3) & (z > 0))
            if k == AHEAD and ch + 1 < NCH:
                hid_own(ch + 1)

    def process(ch):
        normalize(ch)
        project(ch)
        kv_own(ch)
        if ch > 0:
            kv_on(ch - 1)

    hid_on(0)
    x_relay(*qc)
    hid_on(1)
    second_norm()
    x_wait(*qc, 2)
    send(lambda: qd_other(half))
    wo_y(down, y, 0).wait_recv()
    send(lambda: wo_y(down, up, 2), c == 0)
    wo_y(up, y, 1).wait_recv()
    send(lambda: wo_y(up, down, 2), c == 1)
    hid_on(2)
    wo_y(opposite, y, 2).wait_recv()
    x_send(*wox)
    qd_other(other).wait_recv()
    process(0)
    process(1)
    hid_on(3)
    process(2)
    process(3)

    for h in range(2):
        def residual(i, carry, h=h):
            rows = pl.ds(pl.multiple_of(16 * i, 16), 16)
            blocks = [hidden_rows(zz, z, h, rows) for zz in range(4)]
            hnat[pl.ds(pl.multiple_of(HALF * h + 16 * i, 16), 16)] = in_order(blocks)
            return carry

        lax.fori_loop(0, HALF // 16, residual, 0)

    kv_on(NCH - 1)
    def wo_other(mask):
        ref = wo.at[:, :, :, mask]
        return remote(ref, ref, s_wos.at[0], r_wos.at[0], sibling)

    x_relay(*wox)
    for ch in range(NCH):
        kv_copy(ch, 1, down, y, 0).wait_recv()
        kv_copy(ch, 0, up, y, 1).wait_recv()
        kv_copy(ch, 0, opposite, y, 2).wait_recv()
        kv_copy(ch, 1, opposite, y, 2).wait_recv()

    def att_copy(j):
        return remote(att.at[j], attg.at[z], s_att.at[j], r_att.at[z], patch(y, j))

    def att_from(k):
        return remote(att.at[k], attg.at[k], s_att.at[k], r_att.at[k], patch(y, k))

    def attend(j):
        rows = pl.ds(pl.multiple_of(BLK * j, 128), BLK)
        for pair in range(3):
            width = min(128, CZ - 128 * pair)
            lanes = slice(128 * pair, 128 * pair + width)
            query = qb[rows, 128 * pair : 128 * pair + 128]
            key_at = 128 * pair if pair < 2 else 512
            value_at = key_at + 256 if pair < 2 else 512
            keys = kv[:, :, key_at : key_at + 128].reshape(2048, 128)
            values = kv[:, :, value_at : value_at + 128].reshape(2048, 128)
            lane = lax.broadcasted_iota(jnp.int32, (BLK, 128), 1)
            result = None
            for side in range(width // 64):
                q1 = query
                if width > 64:
                    keep = (lane >= 64 * side) & (lane < 64 * side + 64)
                    q1 = jnp.where(keep, query.astype(F32), 0.0).astype(BF16)
                scores = dot_nt(q1, keys)
                peak = jnp.max(scores, axis=1, keepdims=True)
                unnormalized = jnp.exp(scores - peak)
                row_total = jnp.sum(unnormalized, axis=1, keepdims=True)
                mix = dot_nn(unnormalized.astype(BF16), values) / row_total
                result = mix if result is None else jnp.where(lane < 64, result, mix)
            if width == 64:
                result = result[:, 64:128]
            att[j, :, lanes] = result.astype(BF16)

    def attend_step(t, carry):
        j = (z + 1 + t) % 4
        attend(j)
        pl.when(t < 3)(lambda: att_copy(j).start())
        return carry

    lax.fori_loop(0, 2, attend_step, 0)
    x_wait(*wox, 2)
    send(lambda: wo_other(half))
    lax.fori_loop(2, 4, attend_step, 0)
    attg[z] = att[z]
    for k in range(4):
        pending.append((z != k, lambda k=k: att_copy(k)))

    wo_other(other).wait_recv()
    for k in range(4):
        when(z != k, lambda k=k: att_from(k).wait_recv())

    whole = jnp.concatenate([attg[k].astype(F32) for k in range(4)], axis=1).astype(BF16)
    out_ref[...] = (hnat[...] + dot_nt(whole, wo[...].reshape(C, C))).astype(BF16)

    for cond, make in pending:
        when(cond, lambda make=make: make().wait_send())


def on_device(latent, conv_weight, channel_bias, w_query, w_key, w_value, w_out):
    any_space = pl.BlockSpec(memory_space=pl.ANY)
    vmem = pl.BlockSpec(memory_space=pltpu.VMEM)
    dma = pltpu.SemaphoreType.DMA
    out = pl.pallas_call(
        kernel,
        out_shape=jax.ShapeDtypeStruct((BLK, C), BF16),
        in_specs=[any_space, any_space, vmem, any_space, any_space, any_space, any_space],
        out_specs=vmem,
        scratch_shapes=[
            pltpu.VMEM((640, C), BF16),
            pltpu.VMEM((640, C), BF16),
            pltpu.VMEM((9, 4, CB, C), BF16),
            pltpu.VMEM((4, CB, C), BF16),
            pltpu.VMEM((3, CZ, C), BF16),
            pltpu.VMEM((4, 4, CB, C), BF16),
            pltpu.VMEM((8, 128), F32),
            pltpu.VMEM((16, 8, 128), F32),
            pltpu.VMEM((8, 128), F32),
            pltpu.VMEM((16, 8, 128), F32),
            pltpu.VMEM((C, 128), BF16),
            pltpu.VMEM((128, C), BF16),
            pltpu.VMEM((C, CZ), BF16),
            pltpu.VMEM((2, 8, C), F32),
            pltpu.VMEM((2, 8, CZ), F32),
            pltpu.VMEM((2, 8, CZ), F32),
            pltpu.VMEM((256, 3 * CZ), F32),
            pltpu.VMEM((4, NCH, 5, HALF, 128), BF16),
            pltpu.VMEM((R, C), BF16),
            pltpu.VMEM((BLK, C), F32),
            pltpu.VMEM((ROWS_Y, 384), BF16),
            pltpu.VMEM((4, ROWS_Y, 2 * CZ), BF16),
            pltpu.VMEM((4, BLK, CZ), BF16),
            pltpu.VMEM((4, BLK, CZ), BF16),
            dma((6,)), dma((16,)), dma((16,)), dma((2, 4)), dma((4,)), dma((2,)), dma((2,)),
            dma((3,)), dma((3,)), dma((3,)), dma((3,)),
            dma((3,)), dma((3,)), dma((3, 4)), dma((3, 4)), dma((3,)), dma((3,)),
            dma((1,)), dma((1,)), dma((2,)), dma((3,)), dma((1,)), dma((3,)), dma((3,)), dma((1,)), dma((1,)),
            dma((2,)), dma((1,)), dma((3,)), dma((3,)), dma((3,)), dma((3,)), dma((1,)), dma((1,)),
            dma((16,)), dma((16,)), dma((2, NCH, 4)), dma((NCH, 4)), dma((NCH, 2, 3)), dma((NCH, 2, 3)),
            dma((4,)), dma((4,)),
        ],
        compiler_params=pltpu.CompilerParams(
            collective_id=0, has_side_effects=True, vmem_limit_bytes=60 * 1024 * 1024
        ),
    )(
        latent.reshape(BLK, C), conv_weight.reshape(9, CB, C), channel_bias.reshape(1, CB), w_query, w_key, w_value, w_out
    )
    return out.reshape(latent.shape)


def solution(mesh):
    return jax.shard_map(
        on_device,
        mesh=mesh,
        in_specs=(
            P(("batch", "patch"), None, None),
            P(None, None, "patch", None),
            P("patch"),
            P("patch", None),
            P("patch", None),
            P("patch", None),
            P("patch", None),
        ),
        out_specs=P(("batch", "patch"), None, None),
        check_vma=False,
    )
```

```python
import jax
import jax.numpy as jnp
from jax import lax
from jax.experimental import pallas as pl
from jax.experimental.pallas import tpu as pltpu
from jax.sharding import PartitionSpec as P

C = 1280
HEADS = 20
HEAD_DIM = 64
GROUPS = 32
GROUP = C // GROUPS
NY, NZ = 4, 4
BLK = 128
ROWS_Y = 512
NCH = 4
R = ROWS_Y // NCH
HALF = R // 2
AHEAD = 1
CB = C // 16
CZ = C // 4
EPS = 1e-05
MESH = pl.DeviceIdType.MESH
F32 = jnp.float32
BF16 = jnp.bfloat16


def dot_nt(left, right):
    return lax.dot_general(left, right, (((1,), (1,)), ((), ())), preferred_element_type=F32)


def dot_nn(left, right):
    return lax.dot_general(left, right, (((1,), (0,)), ((), ())), preferred_element_type=F32)


def kernel(
    lat_in, cw_in, bias_in, wq_in, wk_in, wv_in, wo_in, out_ref,
    lat, act, cw, wown, wqkv, wo, st1s, st1, st2s, st2, gmat, gmat_t, sel,
    gn1, gn2, stc, peaks, totals, mixes, ubuf, hidg, nrm, hnat, qb, kv, att, attg,
    s_loc, s_st1, r_st1, s_lat, r_lat, s_halo, r_halo, s_cw, r_cw, s_cws, r_cws,
    s_ct, r_ct, s_cx, r_cx, s_cts, r_cts,
    s_qa, r_qa, l_qa, s_qb, r_qb, s_qc, r_qc, s_qd, r_qd, s_woz, r_woz, s_woy, r_woy, s_wox, r_wox, s_wos, r_wos,
    s_st2, r_st2, s_hid, r_hid, s_kv, r_kv, s_att, r_att,
):
    p = lax.axis_index("patch")
    b = lax.axis_index("batch")
    y = p // 4
    z = p % 4
    c = b % 2
    x = (b // 2) % 4
    sib = b + 1 - 2 * c
    up = (y + 1) % 4
    down = (y + 3) % 4
    opposite = (y + 2) % 4
    half = pl.ds(pl.multiple_of(c * (C // 2), 128), C // 2)
    other = pl.ds(pl.multiple_of((1 - c) * (C // 2), 128), C // 2)
    pending = []

    def patch(yy, zz):
        return {"batch": b, "patch": 4 * yy + zz}

    def across(d):
        return {"batch": b - 2 * x + 2 * ((x + d) % 4), "patch": p}

    sibling = {"batch": sib, "patch": p}

    def remote(src, dst, ssem, rsem, dev):
        return pltpu.make_async_remote_copy(
            src_ref=src, dst_ref=dst, send_sem=ssem, recv_sem=rsem, device_id=dev, device_id_type=MESH
        )

    def when(cond, f):
        if cond is None:
            f()
        else:
            pl.when(cond)(f)

    def send(make, cond=None):
        when(cond, lambda: make().start())
        pending.append((cond, make))

    own_rows = pl.ds(pl.multiple_of(64 + BLK * z, 64), BLK)
    loc = [
        pltpu.make_async_copy(lat_in, lat.at[own_rows], s_loc.at[0]),
        pltpu.make_async_copy(cw_in, cw.at[:, y], s_loc.at[1]),
        pltpu.make_async_copy(wq_in, wown.at[0], s_loc.at[2]),
        pltpu.make_async_copy(wk_in, wown.at[1], s_loc.at[3]),
        pltpu.make_async_copy(wv_in, wown.at[2], s_loc.at[4]),
        pltpu.make_async_copy(wo_in, wown.at[3], s_loc.at[5]),
    ]
    for copy in loc:
        copy.start()
    barrier = pltpu.get_barrier_semaphore()
    for d in range(1, 16):
        pl.semaphore_signal(
            barrier, inc=1, device_id={"batch": b, "patch": (p + d) % 16}, device_id_type=MESH
        )
    pl.semaphore_signal(barrier, inc=1, device_id=sibling, device_id_type=MESH)
    for d in range(1, 4):
        pl.semaphore_signal(barrier, inc=1, device_id=across(d), device_id_type=MESH)

    gi = lax.broadcasted_iota(jnp.int32, (C, 128), 0) - GROUP * lax.broadcasted_iota(jnp.int32, (C, 128), 1)
    gmat[...] = jnp.where((gi >= 0) & (gi < GROUP), 1.0, 0.0).astype(BF16)
    ti = lax.broadcasted_iota(jnp.int32, (128, C), 1) - GROUP * lax.broadcasted_iota(jnp.int32, (128, C), 0)
    gmat_t[...] = jnp.where((ti >= 0) & (ti < GROUP), 1.0, 0.0).astype(BF16)
    def split_rows(x):
        hi = x.astype(BF16).astype(F32)
        mid = (x - hi).astype(BF16).astype(F32)
        return jnp.concatenate([hi, mid, x - hi - mid], axis=0).astype(BF16)

    def join_rows(x):
        return x[0:8] + x[8:16] + x[16:24]

    def to_groups(x):
        return join_rows(dot_nn(split_rows(x), gmat[0 : x.shape[1], :]))

    def to_channels(x, n):
        return join_rows(dot_nn(split_rows(x), gmat_t[:, 0:n]))

    def group_sums(x):
        return to_channels(to_groups(x), x.shape[1])

    st1s[...] = jnp.zeros_like(st1s)
    loc[0].wait()
    mine = lat[own_rows].astype(F32)
    mean = jnp.sum(mine, axis=0, keepdims=True) * (1.0 / BLK)
    m2 = jnp.sum(jnp.square(mine - mean), axis=0, keepdims=True)
    mean = jnp.broadcast_to(mean, (8, C))
    group_mean = to_groups(mean) * (1.0 / GROUP)
    group_m2 = to_groups(m2 + BLK * jnp.square(mean - to_channels(group_mean, C)))
    st1s[0:1, :] = group_mean[0:1, :]
    st1s[1:2, :] = group_m2[0:1, :]
    st1s[2:3, 0:CB] = bias_in[...]

    pl.semaphore_wait(barrier, 19)

    for d in range(1, 16):
        send(
            lambda d=d: remote(
                st1s, st1.at[p], s_st1.at[d], r_st1.at[d], {"batch": b, "patch": (p + d) % 16}
            )
        )
    st1[p] = st1s[...]

    def lat_rows(k):
        return lat.at[pl.ds(pl.multiple_of(64 + BLK * k, 64), BLK)]

    def lat_copy(k, way):
        zz = z + 1 if way == 0 else z - 1
        return remote(lat_rows(k), lat_rows(k), s_lat.at[way, k], r_lat.at[k], patch(y, zz))

    send(lambda: lat_copy(z, 0), z < 3)
    send(lambda: lat_copy(z, 1), z > 0)

    loc[1].wait()
    around = (down, up, opposite)

    def cw_ref(src_y, mask):
        return cw.at[0:5, src_y, :, mask]

    def cw_copy(src_y, to_y, slot):
        ref = cw_ref(src_y, half)
        return remote(ref, ref, s_cw.at[slot], r_cw.at[slot], patch(to_y, z))

    def cw_other(r, mask):
        ref = cw_ref(around[r], mask)
        return remote(ref, ref, s_cws.at[r], r_cws.at[r], sibling)

    def ct_copy(src_y, to_y, slot):
        ref = cw.at[5 + x, src_y, :, half]
        return remote(ref, ref, s_ct.at[slot], r_ct.at[slot], patch(to_y, z))

    nexts = ((x + 1) % 4, (x + 3) % 4, (x + 2) % 4)

    def x_send_if(cond, ref, ssem, rsem):
        send(lambda: remote(ref(x), ref(x), ssem(0), rsem(1), across(1)), cond)
        send(lambda: remote(ref(x), ref(x), ssem(1), rsem(0), across(3)), cond)

    def x_send(ref, ssem, rsem):
        x_send_if(None, ref, ssem, rsem)

    def x_wait(ref, ssem, rsem, i):
        remote(ref(nexts[i]), ref(nexts[i]), ssem(i), rsem(i), across(1)).wait_recv()

    def x_relay(ref, ssem, rsem):
        x_wait(ref, ssem, rsem, 1)
        send(lambda: remote(ref(nexts[1]), ref(nexts[1]), ssem(2), rsem(2), across(1)), c == 0)
        x_wait(ref, ssem, rsem, 0)
        send(lambda: remote(ref(nexts[0]), ref(nexts[0]), ssem(2), rsem(2), across(3)), c == 1)

    def cx(r):
        return (
            lambda i: cw.at[5 + i, around[r], :, half],
            lambda i: s_cx.at[r, i],
            lambda i: r_cx.at[r, i],
        )

    def ct_other(r, mask):
        ref = cw.at[5:9, around[r], :, mask]
        return remote(ref, ref, s_cts.at[r], r_cts.at[r], sibling)

    send(lambda: ct_copy(y, up, 0))
    send(lambda: ct_copy(y, down, 1))

    for copy in loc[2:]:
        copy.wait()
    carrier = z == x
    diagonal = y == z
    turn = (y - z + 4) % 4

    def q_ref(i):
        return wqkv.at[:, pl.ds(pl.multiple_of(CB * i, 16), CB), half]

    def qa_copy():
        return remote(wown.at[0:3, :, half], q_ref(x), s_qa.at[0], r_qa.at[0], patch(y, y))

    def qa_local():
        return pltpu.make_async_copy(wown.at[0:3, :, half], q_ref(x), l_qa.at[0])

    def qb_copy(to_y, slot):
        return remote(q_ref(x), q_ref(x), s_qb.at[slot], r_qb.at[0], patch(to_y, z))

    qc = (q_ref, lambda i: s_qc.at[i], lambda i: r_qc.at[i])

    def qd_other(mask):
        ref = wqkv.at[:, :, mask]
        return remote(ref, ref, s_qd.at[0], r_qd.at[0], sibling)

    send(lambda: cw_copy(y, up, 0))
    send(lambda: cw_copy(y, down, 1))

    def service_1():
        ct_copy(down, y, 0).wait_recv()
        send(lambda: ct_copy(down, up, 2), c == 0)
        ct_copy(up, y, 1).wait_recv()
        send(lambda: ct_copy(up, down, 2), c == 1)
        for r in range(2):
            x_send(*cx(r))

    def service_2():
        ct_copy(opposite, y, 2).wait_recv()
        x_send(*cx(2))
        cw_copy(down, y, 0).wait_recv()
        send(lambda: cw_copy(down, up, 2), c == 0)
        cw_copy(up, y, 1).wait_recv()
        send(lambda: cw_copy(up, down, 2), c == 1)
        for r in range(2):
            send(lambda r=r: cw_other(r, half))
        send(qa_copy, carrier & (z != y))
        when(carrier & diagonal, lambda: qa_local().start())
        for r in range(2):
            x_relay(*cx(r))

    def service_3():
        x_relay(*cx(2))

    services = {1: service_1, 2: service_2, 3: service_3}

    for yy in range(4):
        rows = lax.broadcasted_iota(jnp.int32, (CZ, CZ), 0) - CB * z
        cols = lax.broadcasted_iota(jnp.int32, (CZ, CZ), 1) - CB * yy
        hit = (rows == cols) & (cols >= 0) & (cols < CB)
        sel[CZ * yy : CZ * yy + CZ, :] = jnp.where(hit, 1.0, 0.0).astype(BF16)

    for d in range(1, 16):
        q = (p + 16 - d) % 16
        remote(st1s, st1.at[q], s_st1.at[d], r_st1.at[d], {"batch": b, "patch": q}).wait_recv()
    def to_lanes(x, n):
        full = jnp.concatenate([x[j : j + 1, :] for j in range(n)], axis=1)
        return full

    stats = st1[...]
    stats_sum = jnp.sum(stats, axis=0)
    stats_dev = jnp.sum(jnp.square(stats - (stats_sum * (1.0 / 16))[None]), axis=0)
    centre = stats_sum[0:1, :] * (1.0 / 16)
    spread = (stats_sum[1:2, :] + (BLK * GROUP) * stats_dev[0:1, :]) * (1.0 / (2048 * GROUP))
    gn1[0] = to_channels(jnp.broadcast_to(centre, (8, 128)), C)
    gn1[1] = to_channels(jnp.broadcast_to(lax.rsqrt(spread + EPS), (8, 128)), C)

    def activate(start, count):
        def body(i, carry):
            rows = pl.ds(pl.multiple_of(start + 16 * i, 16), 16)
            v = lat[rows].astype(F32)
            v = (v - gn1[0, 0:1, :]) * gn1[1, 0:1, :]
            act[rows] = (v / (1.0 + jnp.exp(-v))).astype(BF16)
            return carry

        lax.fori_loop(0, count // 16, body, 0)

    activate(64 + BLK * z, BLK)

    def halo_up():
        return remote(
            lat.at[pl.ds(512, 64)], lat.at[pl.ds(0, 64)], s_halo.at[0], r_halo.at[0], patch(y + 1, z)
        )

    def halo_down():
        return remote(
            lat.at[pl.ds(64, 64)], lat.at[pl.ds(576, 64)], s_halo.at[1], r_halo.at[1], patch(y - 1, z)
        )

    send(halo_up, (z == 3) & (y < 3))
    send(halo_down, (z == 0) & (y > 0))
    for k in range(1, 4):
        def below(k=k):
            lat_copy(z - k, 0).wait_recv()

        def above(k=k):
            lat_copy(z + k, 1).wait_recv()

        when(z - k >= 0, below)
        send(lambda k=k: lat_copy(z - k, 0), (z - k >= 0) & (z < 3))
        when(z + k <= 3, above)
        send(lambda k=k: lat_copy(z + k, 1), (z + k <= 3) & (z > 0))
        send(halo_up, (z + k == 3) & (y < 3))
        send(halo_down, (z - k == 0) & (y > 0))
        services[k]()
        when(z - k >= 0, lambda k=k: activate(64 + BLK * (z - k), BLK))
        when(z + k <= 3, lambda k=k: activate(64 + BLK * (z + k), BLK))

    def wo_ref(yy, i):
        return wo.at[yy, i, :, half]

    def wo_local():
        return pltpu.make_async_copy(wown.at[3, :, half], wo_ref(y, x), l_qa.at[1])

    def wo_z(to_z, slot):
        return remote(wo_ref(y, x), wo_ref(y, x), s_woz.at[slot], r_woz.at[0], patch(y, to_z))

    when(carrier, lambda: wo_local().start())
    when(carrier, lambda: wo_local().wait())
    send(lambda: wo_z(z + 1, 0), carrier & (z < 3))
    send(lambda: wo_z(z - 1, 1), carrier & (z > 0))

    when(y > 0, lambda: halo_up().wait_recv())
    when(y > 0, lambda: activate(0, 64))
    when(y < 3, lambda: halo_down().wait_recv())
    when(y < 3, lambda: activate(576, 64))

    def zero_top():
        act[0:64] = jnp.zeros((64, C), BF16)

    def zero_bottom():
        act[576:640] = jnp.zeros((64, C), BF16)

    when(y == 0, zero_top)
    when(y == 3, zero_bottom)

    when(diagonal & (z != x), lambda: qa_copy().wait_recv())
    when(diagonal & carrier, lambda: qa_local().wait())
    send(lambda: qb_copy(up, 0), diagonal)
    send(lambda: qb_copy(down, 1), diagonal)
    x_send_if(diagonal, *qc)
    cw_copy(opposite, y, 2).wait_recv()
    send(lambda: cw_other(2, half))
    for r in range(3):
        x_wait(*cx(r), 2)
        send(lambda r=r: ct_other(r, half))

    def wo_y(src_y, to_y, slot):
        return remote(wo_ref(src_y, x), wo_ref(src_y, x), s_woy.at[slot], r_woy.at[slot], patch(to_y, z))

    wox = (lambda i: wo.at[:, i, :, half], lambda i: s_wox.at[i], lambda i: r_wox.at[i])

    for r in range(3):
        cw_other(r, other).wait_recv()
        ct_other(r, other).wait_recv()

    bias = jnp.concatenate([st1[4 * yy + z, 2:3, 0:CB] for yy in range(4)], axis=1)
    CHUNK = 256

    def conv_chunk(j, carry):
        total = jnp.zeros((CHUNK, 3 * CZ), F32)
        for dr in range(3):
            rows = pl.ds(pl.multiple_of(CHUNK * j + 64 * dr, 64), CHUNK)
            total = total + dot_nt(act[rows], cw[3 * dr : 3 * dr + 3].reshape(3 * CZ, C))
        ubuf[...] = total
        column = lax.broadcasted_iota(jnp.int32, (CHUNK, CZ), 0) % 64
        left = pltpu.roll(ubuf[:, 0:CZ], 1, 0)
        right = pltpu.roll(ubuf[:, 2 * CZ : 3 * CZ], CHUNK - 1, 0)
        value = ubuf[:, CZ : 2 * CZ]
        value = value + jnp.where(column == 0, 0.0, left) + jnp.where(column == 63, 0.0, right)
        own = lat[pl.ds(pl.multiple_of(64 + CHUNK * j, 64), CHUNK)]
        value = value + dot_nn(own, sel[...]) + bias
        value = value.astype(BF16).astype(F32)
        mean = jnp.sum(value, axis=0, keepdims=True) * (1.0 / CHUNK)
        stc[j, 0:1, :] = mean
        stc[j, 1:2, :] = jnp.sum(jnp.square(value - mean), axis=0, keepdims=True)
        for i in range(CHUNK // R):
            upper = value[R * i : R * i + HALF]
            lower = value[R * i + HALF : R * i + R]
            ch = (CHUNK // R) * j + i
            hidg[z, ch, 0] = upper[:, 0:128].astype(BF16)
            hidg[z, ch, 1] = upper[:, 128:256].astype(BF16)
            hidg[z, ch, 2] = lower[:, 0:128].astype(BF16)
            hidg[z, ch, 3] = lower[:, 128:256].astype(BF16)
            hidg[z, ch, 4] = jnp.concatenate([upper[:, 256:CZ], lower[:, 256:CZ]], axis=1).astype(BF16)
        return carry

    def hid_copy(ch, k, way):
        zz = z + 1 if way == 0 else z - 1
        ref = hidg.at[k, ch]
        return remote(ref, ref, s_hid.at[way, ch, k], r_hid.at[ch, k], patch(y, zz))

    def hid_own(ch):
        send(lambda: hid_copy(ch, z, 0), z < 3)
        send(lambda: hid_copy(ch, z, 1), z > 0)

    conv_chunk(0, 0)
    hid_own(0)
    beside = (turn == 1) | (turn == 3)
    when(beside, lambda: qb_copy(up, 0).wait_recv())
    send(lambda: qb_copy(up, 2), (turn == 1) & (c == 0))
    send(lambda: qb_copy(down, 2), (turn == 3) & (c == 1))
    x_send_if(beside, *qc)
    conv_chunk(1, 0)

    st2s[...] = jnp.zeros_like(st2s)
    mean = 0.5 * (stc[0, 0:1, :] + stc[1, 0:1, :])
    m2 = stc[0, 1:2, :] + stc[1, 1:2, :]
    m2 = m2 + CHUNK * (jnp.square(stc[0, 0:1, :] - mean) + jnp.square(stc[1, 0:1, :] - mean))
    for j in range(3):
        width = min(128, CZ - 128 * j)
        st2s[j : j + 1, 0:width] = mean[:, 128 * j : 128 * j + width]
        st2s[4 + j : 5 + j, 0:width] = m2[:, 128 * j : 128 * j + width]
    for d in range(1, 16):
        send(
            lambda d=d: remote(
                st2s, st2.at[p], s_st2.at[d], r_st2.at[d], {"batch": b, "patch": (p + d) % 16}
            )
        )
    st2[p] = st2s[...]

    when(turn == 2, lambda: qb_copy(up, 0).wait_recv())
    x_send_if(turn == 2, *qc)
    when(z != x, lambda: wo_z(z, 0).wait_recv())
    send(lambda: wo_z(z + 1, 0), (z > x) & (z < 3))
    send(lambda: wo_z(z - 1, 1), (z < x) & (z > 0))
    send(lambda: wo_y(y, up, 0))
    send(lambda: wo_y(y, down, 1))

    def second_norm():
        for d in range(1, 16):
            q = (p + 16 - d) % 16
            remote(st2s, st2.at[q], s_st2.at[d], r_st2.at[d], {"batch": b, "patch": q}).wait_recv()
        parts = [[st2[4 * yy + zz] for zz in range(4)] for yy in range(4)]
        mean_rows, m2_rows = [], []
        for zz in range(4):
            col = [parts[yy][zz] for yy in range(4)]
            m = (col[0] + col[1] + col[2] + col[3]) * 0.25
            dev = sum(jnp.square(x - m) for x in col)
            total = col[0] + col[1] + col[2] + col[3]
            m2_all = total[4:8] + ROWS_Y * dev[0:4]
            mean_rows.append(to_lanes(m, 3)[:, 0:CZ])
            m2_rows.append(to_lanes(m2_all, 3)[:, 0:CZ])
        mean_l = jnp.concatenate(mean_rows + mean_rows, axis=0)
        m2_l = jnp.concatenate(m2_rows + m2_rows, axis=0)
        centre = group_sums(mean_l) * (1.0 / GROUP)
        spread = group_sums(m2_l + 2048.0 * jnp.square(mean_l - centre)) * (1.0 / (2048 * GROUP))
        gn2[0] = centre
        gn2[1] = lax.rsqrt(spread + EPS)

    def hidden_rows(zz, ch, h, rows):
        tail = hidg[zz, ch, 4, rows, :].astype(F32)[:, 64 * h : 64 * h + 64]
        return jnp.concatenate(
            [hidg[zz, ch, 2 * h, rows, :].astype(F32), hidg[zz, ch, 2 * h + 1, rows, :].astype(F32), tail],
            axis=1,
        )

    def in_order(blocks):
        return jnp.concatenate(
            [blocks[zz][:, CB * yy : CB * yy + CB] for yy in range(4) for zz in range(4)], axis=1
        )

    def normalize(ch):
        for h in range(2):
            def body(i, carry, h=h):
                rows = pl.ds(pl.multiple_of(16 * i, 16), 16)
                blocks = [
                    (hidden_rows(zz, ch, h, rows) - gn2[0, zz : zz + 1, :]) * gn2[1, zz : zz + 1, :]
                    for zz in range(4)
                ]
                nrm[pl.ds(pl.multiple_of(HALF * h + 16 * i, 16), 16)] = in_order(blocks).astype(BF16)
                return carry

            lax.fori_loop(0, HALF // 16, body, 0)

    def project(ch):
        rows = pl.ds(R * ch, R)
        both = dot_nt(nrm[...], wqkv[...].reshape(3 * CZ, C))
        kv[y, rows, 0:256] = both[:, CZ : CZ + 256].astype(BF16)
        kv[y, rows, 256:512] = both[:, 2 * CZ : 2 * CZ + 256].astype(BF16)
        kv[y, rows, 512:640] = jnp.concatenate(
            [both[:, CZ + 256 : 2 * CZ], both[:, 2 * CZ + 256 : 3 * CZ]], axis=1
        ).astype(BF16)
        query = (both[:, 0:CZ].astype(BF16).astype(F32) * HEAD_DIM**-0.5).astype(BF16)
        qb[rows, 0:256] = query[:, 0:256]
        qb[rows, 256:384] = jnp.concatenate(
            [query[:, 256:CZ].astype(F32), jnp.zeros((R, 64), F32)], axis=1
        ).astype(BF16)

    def kv_copy(ch, h, src_y, to_y, slot):
        ref = kv.at[src_y, pl.ds(R * ch + HALF * h, HALF), :]
        return remote(ref, ref, s_kv.at[ch, h, slot], r_kv.at[ch, h, slot], patch(to_y, z))

    def kv_own(ch):
        send(lambda: kv_copy(ch, 0, y, up, 0))
        send(lambda: kv_copy(ch, 1, y, down, 1))
        send(lambda: kv_copy(ch, 1, y, up, 0))
        send(lambda: kv_copy(ch, 0, y, down, 1))

    def kv_on(ch):
        kv_copy(ch, 0, down, y, 0).wait_recv()
        send(lambda: kv_copy(ch, 0, down, up, 2))
        kv_copy(ch, 1, up, y, 1).wait_recv()
        send(lambda: kv_copy(ch, 1, up, down, 2))

    def hid_on(ch):
        for k in range(1, 4):
            when(z - k >= 0, lambda k=k: hid_copy(ch, z - k, 0).wait_recv())
            send(lambda k=k: hid_copy(ch, z - k, 0), (z - k >= 0) & (z < 3))
            when(z + k <= 3, lambda k=k: hid_copy(ch, z + k, 1).wait_recv())
            send(lambda k=k: hid_copy(ch, z + k, 1), (z + k <= 3) & (z > 0))
            if k == AHEAD and ch + 1 < NCH:
                hid_own(ch + 1)

    def process(ch):
        normalize(ch)
        project(ch)
        kv_own(ch)
        if ch > 0:
            kv_on(ch - 1)

    hid_on(0)
    x_relay(*qc)
    hid_on(1)
    second_norm()
    x_wait(*qc, 2)
    send(lambda: qd_other(half))
    wo_y(down, y, 0).wait_recv()
    send(lambda: wo_y(down, up, 2), c == 0)
    wo_y(up, y, 1).wait_recv()
    send(lambda: wo_y(up, down, 2), c == 1)
    hid_on(2)
    wo_y(opposite, y, 2).wait_recv()
    x_send(*wox)
    qd_other(other).wait_recv()
    process(0)
    process(1)
    hid_on(3)
    process(2)
    process(3)

    for h in range(2):
        def residual(i, carry, h=h):
            rows = pl.ds(pl.multiple_of(16 * i, 16), 16)
            blocks = [hidden_rows(zz, z, h, rows) for zz in range(4)]
            hnat[pl.ds(pl.multiple_of(HALF * h + 16 * i, 16), 16)] = in_order(blocks)
            return carry

        lax.fori_loop(0, HALF // 16, residual, 0)

    kv_on(NCH - 1)
    def wo_other(mask):
        ref = wo.at[:, :, :, mask]
        return remote(ref, ref, s_wos.at[0], r_wos.at[0], sibling)

    x_relay(*wox)
    for ch in range(NCH):
        kv_copy(ch, 1, down, y, 0).wait_recv()
        kv_copy(ch, 0, up, y, 1).wait_recv()

    def att_copy(j):
        return remote(att.at[j], attg.at[z], s_att.at[j], r_att.at[z], patch(y, j))

    def att_from(k):
        return remote(att.at[k], attg.at[k], s_att.at[k], r_att.at[k], patch(y, k))

    def softmax_part(rows, pair, side, blocks):
        key_at = 128 * pair if pair < 2 else 512
        value_at = key_at + 256 if pair < 2 else 512
        query = qb[rows, 128 * pair : 128 * pair + 128]
        if pair < 2:
            lane = lax.broadcasted_iota(jnp.int32, (BLK, 128), 1)
            keep = (lane >= 64 * side) & (lane < 64 * side + 64)
            query = jnp.where(keep, query.astype(F32), 0.0).astype(BF16)
        scores = [dot_nt(query, kv[i, :, key_at : key_at + 128]) for i in blocks]
        peak = jnp.max(scores[0], axis=1, keepdims=True)
        for one in scores[1:]:
            peak = jnp.maximum(peak, jnp.max(one, axis=1, keepdims=True))
        total, mix = None, None
        for i, one in zip(blocks, scores):
            unnormalized = jnp.exp(one - peak)
            part = jnp.sum(unnormalized, axis=1, keepdims=True)
            value = dot_nn(unnormalized.astype(BF16), kv[i, :, value_at : value_at + 128])
            total = part if total is None else total + part
            mix = value if mix is None else mix + value
        return peak, total, mix

    heads = [(0, 0), (0, 1), (1, 0), (1, 1), (2, 0)]

    def attend_first(j, carry):
        rows = pl.ds(pl.multiple_of(BLK * j, 128), BLK)
        for h, (pair, side) in enumerate(heads):
            peak, total, mix = softmax_part(rows, pair, side, (y, down, up))
            peaks[h, rows, :] = peak
            totals[h, rows, :] = total
            mixes[h, rows, :] = mix
        return carry

    def attend(j):
        rows = pl.ds(pl.multiple_of(BLK * j, 128), BLK)
        lane = lax.broadcasted_iota(jnp.int32, (BLK, 128), 1)
        done = []
        for h, (pair, side) in enumerate(heads):
            peak, total, mix = softmax_part(rows, pair, side, (opposite,))
            before = peaks[h, rows, :]
            peak_all = jnp.maximum(before, peak)
            old, new = jnp.exp(before - peak_all), jnp.exp(peak - peak_all)
            row_total = old * totals[h, rows, :] + new * total
            done.append((old * mixes[h, rows, :] + new * mix) / row_total)
        att[j, :, 0:128] = jnp.where(lane < 64, done[0], done[1]).astype(BF16)
        att[j, :, 128:256] = jnp.where(lane < 64, done[2], done[3]).astype(BF16)
        att[j, :, 256:CZ] = done[4][:, 64:128].astype(BF16)

    def attend_step(t, carry):
        j = (z + 1 + t) % 4
        attend(j)
        pl.when(t < 3)(lambda: att_copy(j).start())
        return carry

    lax.fori_loop(0, 4, attend_first, 0)
    x_wait(*wox, 2)
    send(lambda: wo_other(half))
    for ch in range(NCH):
        kv_copy(ch, 0, opposite, y, 2).wait_recv()
        kv_copy(ch, 1, opposite, y, 2).wait_recv()
    lax.fori_loop(0, 4, attend_step, 0)
    attg[z] = att[z]
    for k in range(4):
        pending.append((z != k, lambda k=k: att_copy(k)))

    wo_other(other).wait_recv()
    for k in range(4):
        when(z != k, lambda k=k: att_from(k).wait_recv())

    whole = jnp.concatenate([attg[k].astype(F32) for k in range(4)], axis=1).astype(BF16)
    out_ref[...] = (hnat[...] + dot_nt(whole, wo[...].reshape(C, C))).astype(BF16)

    for cond, make in pending:
        when(cond, lambda make=make: make().wait_send())


def on_device(latent, conv_weight, channel_bias, w_query, w_key, w_value, w_out):
    any_space = pl.BlockSpec(memory_space=pl.ANY)
    vmem = pl.BlockSpec(memory_space=pltpu.VMEM)
    dma = pltpu.SemaphoreType.DMA
    out = pl.pallas_call(
        kernel,
        out_shape=jax.ShapeDtypeStruct((BLK, C), BF16),
        in_specs=[any_space, any_space, vmem, any_space, any_space, any_space, any_space],
        out_specs=vmem,
        scratch_shapes=[
            pltpu.VMEM((640, C), BF16),
            pltpu.VMEM((640, C), BF16),
            pltpu.VMEM((9, 4, CB, C), BF16),
            pltpu.VMEM((4, CB, C), BF16),
            pltpu.VMEM((3, CZ, C), BF16),
            pltpu.VMEM((4, 4, CB, C), BF16),
            pltpu.VMEM((8, 128), F32),
            pltpu.VMEM((16, 8, 128), F32),
            pltpu.VMEM((8, 128), F32),
            pltpu.VMEM((16, 8, 128), F32),
            pltpu.VMEM((C, 128), BF16),
            pltpu.VMEM((128, C), BF16),
            pltpu.VMEM((C, CZ), BF16),
            pltpu.VMEM((2, 8, C), F32),
            pltpu.VMEM((2, 8, CZ), F32),
            pltpu.VMEM((2, 8, CZ), F32),
            pltpu.VMEM((5, ROWS_Y, 1), F32),
            pltpu.VMEM((5, ROWS_Y, 1), F32),
            pltpu.VMEM((5, ROWS_Y, 128), F32),
            pltpu.VMEM((256, 3 * CZ), F32),
            pltpu.VMEM((4, NCH, 5, HALF, 128), BF16),
            pltpu.VMEM((R, C), BF16),
            pltpu.VMEM((BLK, C), F32),
            pltpu.VMEM((ROWS_Y, 384), BF16),
            pltpu.VMEM((4, ROWS_Y, 2 * CZ), BF16),
            pltpu.VMEM((4, BLK, CZ), BF16),
            pltpu.VMEM((4, BLK, CZ), BF16),
            dma((6,)), dma((16,)), dma((16,)), dma((2, 4)), dma((4,)), dma((2,)), dma((2,)),
            dma((3,)), dma((3,)), dma((3,)), dma((3,)),
            dma((3,)), dma((3,)), dma((3, 4)), dma((3, 4)), dma((3,)), dma((3,)),
            dma((1,)), dma((1,)), dma((2,)), dma((3,)), dma((1,)), dma((3,)), dma((3,)), dma((1,)), dma((1,)),
            dma((2,)), dma((1,)), dma((3,)), dma((3,)), dma((3,)), dma((3,)), dma((1,)), dma((1,)),
            dma((16,)), dma((16,)), dma((2, NCH, 4)), dma((NCH, 4)), dma((NCH, 2, 3)), dma((NCH, 2, 3)),
            dma((4,)), dma((4,)),
        ],
        compiler_params=pltpu.CompilerParams(
            collective_id=0, has_side_effects=True, vmem_limit_bytes=60 * 1024 * 1024
        ),
    )(
        latent.reshape(BLK, C), conv_weight.reshape(9, CB, C), channel_bias.reshape(1, CB), w_query, w_key, w_value, w_out
    )
    return out.reshape(latent.shape)


def solution(mesh):
    return jax.shard_map(
        on_device,
        mesh=mesh,
        in_specs=(
            P(("batch", "patch"), None, None),
            P(None, None, "patch", None),
            P("patch"),
            P("patch", None),
            P("patch", None),
            P("patch", None),
            P("patch", None),
        ),
        out_specs=P(("batch", "patch"), None, None),
        check_vma=False,
    )
```

```python
import jax
import jax.numpy as jnp
from jax import lax
from jax.experimental import pallas as pl
from jax.experimental.pallas import tpu as pltpu
from jax.sharding import PartitionSpec as P

C = 1280
HEADS = 20
HEAD_DIM = 64
GROUPS = 32
GROUP = C // GROUPS
NY, NZ = 4, 4
BLK = 128
ROWS_Y = 512
NCH = 4
R = ROWS_Y // NCH
HALF = R // 2
AHEAD = 1
CB = C // 16
CZ = C // 4
EPS = 1e-05
MESH = pl.DeviceIdType.MESH
F32 = jnp.float32
BF16 = jnp.bfloat16


def dot_nt(left, right):
    return lax.dot_general(left, right, (((1,), (1,)), ((), ())), preferred_element_type=F32)


def dot_nn(left, right):
    return lax.dot_general(left, right, (((1,), (0,)), ((), ())), preferred_element_type=F32)


def kernel(
    lat_in, cw_in, bias_in, wq_in, wk_in, wv_in, wo_in, out_ref,
    lat, act, cw, wown, wqkv, wo, st1s, st1, st2s, st2, gmat, gmat_t, sel,
    gn1, gn2, stc, ubuf, hidg, nrm, hnat, qb, kv, att, attg,
    s_loc, s_st1, r_st1, s_lat, r_lat, s_halo, r_halo, s_cw, r_cw, s_cws, r_cws,
    s_ct, r_ct, s_cx, r_cx, s_cts, r_cts,
    s_qa, r_qa, l_qa, s_qb, r_qb, s_qc, r_qc, s_qd, r_qd, s_woz, r_woz, s_woy, r_woy, s_wox, r_wox, s_wos, r_wos,
    s_st2, r_st2, s_hid, r_hid, s_kv, r_kv, s_att, r_att,
):
    p = lax.axis_index("patch")
    b = lax.axis_index("batch")
    y = p // 4
    z = p % 4
    c = b % 2
    x = (b // 2) % 4
    sib = b + 1 - 2 * c
    up = (y + 1) % 4
    down = (y + 3) % 4
    opposite = (y + 2) % 4
    half = pl.ds(pl.multiple_of(c * (C // 2), 128), C // 2)
    other = pl.ds(pl.multiple_of((1 - c) * (C // 2), 128), C // 2)
    pending = []

    def patch(yy, zz):
        return {"batch": b, "patch": 4 * yy + zz}

    def across(d):
        return {"batch": b - 2 * x + 2 * ((x + d) % 4), "patch": p}

    sibling = {"batch": sib, "patch": p}

    def remote(src, dst, ssem, rsem, dev):
        return pltpu.make_async_remote_copy(
            src_ref=src, dst_ref=dst, send_sem=ssem, recv_sem=rsem, device_id=dev, device_id_type=MESH
        )

    def when(cond, f):
        if cond is None:
            f()
        else:
            pl.when(cond)(f)

    def send(make, cond=None):
        when(cond, lambda: make().start())
        pending.append((cond, make))

    own_rows = pl.ds(pl.multiple_of(64 + BLK * z, 64), BLK)
    loc = [
        pltpu.make_async_copy(lat_in, lat.at[own_rows], s_loc.at[0]),
        pltpu.make_async_copy(cw_in, cw.at[:, y], s_loc.at[1]),
        pltpu.make_async_copy(wq_in, wown.at[0], s_loc.at[2]),
        pltpu.make_async_copy(wk_in, wown.at[1], s_loc.at[3]),
        pltpu.make_async_copy(wv_in, wown.at[2], s_loc.at[4]),
        pltpu.make_async_copy(wo_in, wown.at[3], s_loc.at[5]),
    ]
    for copy in loc:
        copy.start()
    barrier = pltpu.get_barrier_semaphore()
    for d in range(1, 16):
        pl.semaphore_signal(
            barrier, inc=1, device_id={"batch": b, "patch": (p + d) % 16}, device_id_type=MESH
        )
    pl.semaphore_signal(barrier, inc=1, device_id=sibling, device_id_type=MESH)
    for d in range(1, 4):
        pl.semaphore_signal(barrier, inc=1, device_id=across(d), device_id_type=MESH)

    gi = lax.broadcasted_iota(jnp.int32, (C, 128), 0) - GROUP * lax.broadcasted_iota(jnp.int32, (C, 128), 1)
    gmat[...] = jnp.where((gi >= 0) & (gi < GROUP), 1.0, 0.0).astype(BF16)
    ti = lax.broadcasted_iota(jnp.int32, (128, C), 1) - GROUP * lax.broadcasted_iota(jnp.int32, (128, C), 0)
    gmat_t[...] = jnp.where((ti >= 0) & (ti < GROUP), 1.0, 0.0).astype(BF16)
    def split_rows(x):
        hi = x.astype(BF16).astype(F32)
        mid = (x - hi).astype(BF16).astype(F32)
        return jnp.concatenate([hi, mid, x - hi - mid], axis=0).astype(BF16)

    def join_rows(x):
        return x[0:8] + x[8:16] + x[16:24]

    def to_groups(x):
        return join_rows(dot_nn(split_rows(x), gmat[0 : x.shape[1], :]))

    def to_channels(x, n):
        return join_rows(dot_nn(split_rows(x), gmat_t[:, 0:n]))

    def group_sums(x):
        return to_channels(to_groups(x), x.shape[1])

    st1s[...] = jnp.zeros_like(st1s)
    loc[0].wait()
    mine = lat[own_rows].astype(F32)
    mean = jnp.sum(mine, axis=0, keepdims=True) * (1.0 / BLK)
    m2 = jnp.sum(jnp.square(mine - mean), axis=0, keepdims=True)
    mean = jnp.broadcast_to(mean, (8, C))
    group_mean = to_groups(mean) * (1.0 / GROUP)
    group_m2 = to_groups(m2 + BLK * jnp.square(mean - to_channels(group_mean, C)))
    st1s[0:1, :] = group_mean[0:1, :]
    st1s[1:2, :] = group_m2[0:1, :]
    st1s[2:3, 0:CB] = bias_in[...]

    pl.semaphore_wait(barrier, 19)

    for d in range(1, 16):
        send(
            lambda d=d: remote(
                st1s, st1.at[p], s_st1.at[d], r_st1.at[d], {"batch": b, "patch": (p + d) % 16}
            )
        )
    st1[p] = st1s[...]

    def lat_rows(k):
        return lat.at[pl.ds(pl.multiple_of(64 + BLK * k, 64), BLK)]

    def lat_copy(k, way):
        zz = z + 1 if way == 0 else z - 1
        return remote(lat_rows(k), lat_rows(k), s_lat.at[way, k], r_lat.at[k], patch(y, zz))

    send(lambda: lat_copy(z, 0), z < 3)
    send(lambda: lat_copy(z, 1), z > 0)

    loc[1].wait()
    around = (down, up, opposite)

    def cw_ref(src_y, mask):
        return cw.at[0:5, src_y, :, mask]

    def cw_copy(src_y, to_y, slot):
        ref = cw_ref(src_y, half)
        return remote(ref, ref, s_cw.at[slot], r_cw.at[slot], patch(to_y, z))

    def cw_other(r, mask):
        ref = cw_ref(around[r], mask)
        return remote(ref, ref, s_cws.at[r], r_cws.at[r], sibling)

    def ct_copy(src_y, to_y, slot):
        ref = cw.at[5 + x, src_y, :, half]
        return remote(ref, ref, s_ct.at[slot], r_ct.at[slot], patch(to_y, z))

    nexts = ((x + 1) % 4, (x + 3) % 4, (x + 2) % 4)

    def x_send_if(cond, ref, ssem, rsem):
        send(lambda: remote(ref(x), ref(x), ssem(0), rsem(1), across(1)), cond)
        send(lambda: remote(ref(x), ref(x), ssem(1), rsem(0), across(3)), cond)

    def x_send(ref, ssem, rsem):
        x_send_if(None, ref, ssem, rsem)

    def x_wait(ref, ssem, rsem, i):
        remote(ref(nexts[i]), ref(nexts[i]), ssem(i), rsem(i), across(1)).wait_recv()

    def x_relay(ref, ssem, rsem):
        x_wait(ref, ssem, rsem, 1)
        send(lambda: remote(ref(nexts[1]), ref(nexts[1]), ssem(2), rsem(2), across(1)), c == 0)
        x_wait(ref, ssem, rsem, 0)
        send(lambda: remote(ref(nexts[0]), ref(nexts[0]), ssem(2), rsem(2), across(3)), c == 1)

    def cx(r):
        return (
            lambda i: cw.at[5 + i, around[r], :, half],
            lambda i: s_cx.at[r, i],
            lambda i: r_cx.at[r, i],
        )

    def ct_other(r, mask):
        ref = cw.at[5:9, around[r], :, mask]
        return remote(ref, ref, s_cts.at[r], r_cts.at[r], sibling)

    send(lambda: ct_copy(y, up, 0))
    send(lambda: ct_copy(y, down, 1))

    for copy in loc[2:]:
        copy.wait()
    carrier = z == x
    diagonal = y == z
    turn = (y - z + 4) % 4

    def q_ref(i):
        return wqkv.at[:, pl.ds(pl.multiple_of(CB * i, 16), CB), half]

    def qa_copy():
        return remote(wown.at[0:3, :, half], q_ref(x), s_qa.at[0], r_qa.at[0], patch(y, y))

    def qa_local():
        return pltpu.make_async_copy(wown.at[0:3, :, half], q_ref(x), l_qa.at[0])

    def qb_copy(to_y, slot):
        return remote(q_ref(x), q_ref(x), s_qb.at[slot], r_qb.at[0], patch(to_y, z))

    qc = (q_ref, lambda i: s_qc.at[i], lambda i: r_qc.at[i])

    def qd_other(mask):
        ref = wqkv.at[:, :, mask]
        return remote(ref, ref, s_qd.at[0], r_qd.at[0], sibling)

    send(lambda: cw_copy(y, up, 0))
    send(lambda: cw_copy(y, down, 1))

    def service_1():
        ct_copy(down, y, 0).wait_recv()
        send(lambda: ct_copy(down, up, 2), c == 0)
        ct_copy(up, y, 1).wait_recv()
        send(lambda: ct_copy(up, down, 2), c == 1)
        for r in range(2):
            x_send(*cx(r))

    def service_2():
        ct_copy(opposite, y, 2).wait_recv()
        x_send(*cx(2))
        cw_copy(down, y, 0).wait_recv()
        send(lambda: cw_copy(down, up, 2), c == 0)
        cw_copy(up, y, 1).wait_recv()
        send(lambda: cw_copy(up, down, 2), c == 1)
        for r in range(2):
            send(lambda r=r: cw_other(r, half))
        send(qa_copy, carrier & (z != y))
        when(carrier & diagonal, lambda: qa_local().start())
        for r in range(2):
            x_relay(*cx(r))

    def service_3():
        x_relay(*cx(2))

    services = {1: service_1, 2: service_2, 3: service_3}

    for yy in range(4):
        rows = lax.broadcasted_iota(jnp.int32, (CZ, CZ), 0) - CB * z
        cols = lax.broadcasted_iota(jnp.int32, (CZ, CZ), 1) - CB * yy
        hit = (rows == cols) & (cols >= 0) & (cols < CB)
        sel[CZ * yy : CZ * yy + CZ, :] = jnp.where(hit, 1.0, 0.0).astype(BF16)

    for d in range(1, 16):
        q = (p + 16 - d) % 16
        remote(st1s, st1.at[q], s_st1.at[d], r_st1.at[d], {"batch": b, "patch": q}).wait_recv()
    def to_lanes(x, n):
        full = jnp.concatenate([x[j : j + 1, :] for j in range(n)], axis=1)
        return full

    stats = st1[...]
    stats_sum = jnp.sum(stats, axis=0)
    stats_dev = jnp.sum(jnp.square(stats - (stats_sum * (1.0 / 16))[None]), axis=0)
    centre = stats_sum[0:1, :] * (1.0 / 16)
    spread = (stats_sum[1:2, :] + (BLK * GROUP) * stats_dev[0:1, :]) * (1.0 / (2048 * GROUP))
    gn1[0] = to_channels(jnp.broadcast_to(centre, (8, 128)), C)
    gn1[1] = to_channels(jnp.broadcast_to(lax.rsqrt(spread + EPS), (8, 128)), C)

    def activate(start, count):
        def body(i, carry):
            rows = pl.ds(pl.multiple_of(start + 16 * i, 16), 16)
            v = lat[rows].astype(F32)
            v = (v - gn1[0, 0:1, :]) * gn1[1, 0:1, :]
            act[rows] = (v / (1.0 + jnp.exp(-v))).astype(BF16)
            return carry

        lax.fori_loop(0, count // 16, body, 0)

    activate(64 + BLK * z, BLK)

    def halo_up():
        return remote(
            lat.at[pl.ds(512, 64)], lat.at[pl.ds(0, 64)], s_halo.at[0], r_halo.at[0], patch(y + 1, z)
        )

    def halo_down():
        return remote(
            lat.at[pl.ds(64, 64)], lat.at[pl.ds(576, 64)], s_halo.at[1], r_halo.at[1], patch(y - 1, z)
        )

    send(halo_up, (z == 3) & (y < 3))
    send(halo_down, (z == 0) & (y > 0))
    for k in range(1, 4):
        def below(k=k):
            lat_copy(z - k, 0).wait_recv()

        def above(k=k):
            lat_copy(z + k, 1).wait_recv()

        when(z - k >= 0, below)
        send(lambda k=k: lat_copy(z - k, 0), (z - k >= 0) & (z < 3))
        when(z + k <= 3, above)
        send(lambda k=k: lat_copy(z + k, 1), (z + k <= 3) & (z > 0))
        send(halo_up, (z + k == 3) & (y < 3))
        send(halo_down, (z - k == 0) & (y > 0))
        services[k]()
        when(z - k >= 0, lambda k=k: activate(64 + BLK * (z - k), BLK))
        when(z + k <= 3, lambda k=k: activate(64 + BLK * (z + k), BLK))

    def wo_ref(yy, i):
        return wo.at[yy, i, :, half]

    def wo_local():
        return pltpu.make_async_copy(wown.at[3, :, half], wo_ref(y, x), l_qa.at[1])

    def wo_z(to_z, slot):
        return remote(wo_ref(y, x), wo_ref(y, x), s_woz.at[slot], r_woz.at[0], patch(y, to_z))

    when(carrier, lambda: wo_local().start())
    when(carrier, lambda: wo_local().wait())
    send(lambda: wo_z(z + 1, 0), carrier & (z < 3))
    send(lambda: wo_z(z - 1, 1), carrier & (z > 0))

    when(y > 0, lambda: halo_up().wait_recv())
    when(y > 0, lambda: activate(0, 64))
    when(y < 3, lambda: halo_down().wait_recv())
    when(y < 3, lambda: activate(576, 64))

    def zero_top():
        act[0:64] = jnp.zeros((64, C), BF16)

    def zero_bottom():
        act[576:640] = jnp.zeros((64, C), BF16)

    when(y == 0, zero_top)
    when(y == 3, zero_bottom)

    when(diagonal & (z != x), lambda: qa_copy().wait_recv())
    when(diagonal & carrier, lambda: qa_local().wait())
    send(lambda: qb_copy(up, 0), diagonal)
    send(lambda: qb_copy(down, 1), diagonal)
    x_send_if(diagonal, *qc)
    cw_copy(opposite, y, 2).wait_recv()
    send(lambda: cw_other(2, half))
    for r in range(3):
        x_wait(*cx(r), 2)
        send(lambda r=r: ct_other(r, half))

    def wo_y(src_y, to_y, slot):
        return remote(wo_ref(src_y, x), wo_ref(src_y, x), s_woy.at[slot], r_woy.at[slot], patch(to_y, z))

    wox = (lambda i: wo.at[:, i, :, half], lambda i: s_wox.at[i], lambda i: r_wox.at[i])

    for r in range(3):
        cw_other(r, other).wait_recv()
        ct_other(r, other).wait_recv()

    bias = jnp.concatenate([st1[4 * yy + z, 2:3, 0:CB] for yy in range(4)], axis=1)
    CHUNK = 256

    def conv_chunk(j, carry):
        total = jnp.zeros((CHUNK, 3 * CZ), F32)
        for dr in range(3):
            rows = pl.ds(pl.multiple_of(CHUNK * j + 64 * dr, 64), CHUNK)
            total = total + dot_nt(act[rows], cw[3 * dr : 3 * dr + 3].reshape(3 * CZ, C))
        ubuf[...] = total
        column = lax.broadcasted_iota(jnp.int32, (CHUNK, CZ), 0) % 64
        left = pltpu.roll(ubuf[:, 0:CZ], 1, 0)
        right = pltpu.roll(ubuf[:, 2 * CZ : 3 * CZ], CHUNK - 1, 0)
        value = ubuf[:, CZ : 2 * CZ]
        value = value + jnp.where(column == 0, 0.0, left) + jnp.where(column == 63, 0.0, right)
        own = lat[pl.ds(pl.multiple_of(64 + CHUNK * j, 64), CHUNK)]
        value = value + dot_nn(own, sel[...]) + bias
        value = value.astype(BF16).astype(F32)
        mean = jnp.sum(value, axis=0, keepdims=True) * (1.0 / CHUNK)
        stc[j, 0:1, :] = mean
        stc[j, 1:2, :] = jnp.sum(jnp.square(value - mean), axis=0, keepdims=True)
        for i in range(CHUNK // R):
            upper = value[R * i : R * i + HALF]
            lower = value[R * i + HALF : R * i + R]
            ch = (CHUNK // R) * j + i
            hidg[z, ch, 0] = upper[:, 0:128].astype(BF16)
            hidg[z, ch, 1] = upper[:, 128:256].astype(BF16)
            hidg[z, ch, 2] = lower[:, 0:128].astype(BF16)
            hidg[z, ch, 3] = lower[:, 128:256].astype(BF16)
            hidg[z, ch, 4] = jnp.concatenate([upper[:, 256:CZ], lower[:, 256:CZ]], axis=1).astype(BF16)
        return carry

    def hid_copy(ch, k, way):
        zz = z + 1 if way == 0 else z - 1
        ref = hidg.at[k, ch]
        return remote(ref, ref, s_hid.at[way, ch, k], r_hid.at[ch, k], patch(y, zz))

    def hid_own(ch):
        send(lambda: hid_copy(ch, z, 0), z < 3)
        send(lambda: hid_copy(ch, z, 1), z > 0)

    conv_chunk(0, 0)
    hid_own(0)
    beside = (turn == 1) | (turn == 3)
    when(beside, lambda: qb_copy(up, 0).wait_recv())
    send(lambda: qb_copy(up, 2), (turn == 1) & (c == 0))
    send(lambda: qb_copy(down, 2), (turn == 3) & (c == 1))
    x_send_if(beside, *qc)
    conv_chunk(1, 0)

    st2s[...] = jnp.zeros_like(st2s)
    mean = 0.5 * (stc[0, 0:1, :] + stc[1, 0:1, :])
    m2 = stc[0, 1:2, :] + stc[1, 1:2, :]
    m2 = m2 + CHUNK * (jnp.square(stc[0, 0:1, :] - mean) + jnp.square(stc[1, 0:1, :] - mean))
    for j in range(3):
        width = min(128, CZ - 128 * j)
        st2s[j : j + 1, 0:width] = mean[:, 128 * j : 128 * j + width]
        st2s[4 + j : 5 + j, 0:width] = m2[:, 128 * j : 128 * j + width]
    for d in range(1, 16):
        send(
            lambda d=d: remote(
                st2s, st2.at[p], s_st2.at[d], r_st2.at[d], {"batch": b, "patch": (p + d) % 16}
            )
        )
    st2[p] = st2s[...]

    when(turn == 2, lambda: qb_copy(up, 0).wait_recv())
    x_send_if(turn == 2, *qc)
    when(z != x, lambda: wo_z(z, 0).wait_recv())
    send(lambda: wo_z(z + 1, 0), (z > x) & (z < 3))
    send(lambda: wo_z(z - 1, 1), (z < x) & (z > 0))
    send(lambda: wo_y(y, up, 0))
    send(lambda: wo_y(y, down, 1))

    def second_norm():
        for d in range(1, 16):
            q = (p + 16 - d) % 16
            remote(st2s, st2.at[q], s_st2.at[d], r_st2.at[d], {"batch": b, "patch": q}).wait_recv()
        parts = [[st2[4 * yy + zz] for zz in range(4)] for yy in range(4)]
        mean_rows, m2_rows = [], []
        for zz in range(4):
            col = [parts[yy][zz] for yy in range(4)]
            m = (col[0] + col[1] + col[2] + col[3]) * 0.25
            dev = sum(jnp.square(x - m) for x in col)
            total = col[0] + col[1] + col[2] + col[3]
            m2_all = total[4:8] + ROWS_Y * dev[0:4]
            mean_rows.append(to_lanes(m, 3)[:, 0:CZ])
            m2_rows.append(to_lanes(m2_all, 3)[:, 0:CZ])
        mean_l = jnp.concatenate(mean_rows + mean_rows, axis=0)
        m2_l = jnp.concatenate(m2_rows + m2_rows, axis=0)
        centre = group_sums(mean_l) * (1.0 / GROUP)
        spread = group_sums(m2_l + 2048.0 * jnp.square(mean_l - centre)) * (1.0 / (2048 * GROUP))
        gn2[0] = centre
        gn2[1] = lax.rsqrt(spread + EPS)

    def hidden_rows(zz, ch, h, rows):
        tail = hidg[zz, ch, 4, rows, :].astype(F32)[:, 64 * h : 64 * h + 64]
        return jnp.concatenate(
            [hidg[zz, ch, 2 * h, rows, :].astype(F32), hidg[zz, ch, 2 * h + 1, rows, :].astype(F32), tail],
            axis=1,
        )

    def in_order(blocks):
        return jnp.concatenate(
            [blocks[zz][:, CB * yy : CB * yy + CB] for yy in range(4) for zz in range(4)], axis=1
        )

    def normalize(ch):
        for h in range(2):
            def body(i, carry, h=h):
                rows = pl.ds(pl.multiple_of(16 * i, 16), 16)
                blocks = [
                    (hidden_rows(zz, ch, h, rows) - gn2[0, zz : zz + 1, :]) * gn2[1, zz : zz + 1, :]
                    for zz in range(4)
                ]
                nrm[pl.ds(pl.multiple_of(HALF * h + 16 * i, 16), 16)] = in_order(blocks).astype(BF16)
                return carry

            lax.fori_loop(0, HALF // 16, body, 0)

    def project(ch):
        rows = pl.ds(R * ch, R)
        both = dot_nt(nrm[...], wqkv[...].reshape(3 * CZ, C))
        kv[y, rows, 0:256] = both[:, CZ : CZ + 256].astype(BF16)
        kv[y, rows, 256:512] = both[:, 2 * CZ : 2 * CZ + 256].astype(BF16)
        kv[y, rows, 512:640] = jnp.concatenate(
            [both[:, CZ + 256 : 2 * CZ], both[:, 2 * CZ + 256 : 3 * CZ]], axis=1
        ).astype(BF16)
        query = (both[:, 0:CZ].astype(BF16).astype(F32) * HEAD_DIM**-0.5).astype(BF16)
        qb[rows, 0:256] = query[:, 0:256]
        qb[rows, 256:384] = jnp.concatenate(
            [query[:, 256:CZ].astype(F32), jnp.zeros((R, 64), F32)], axis=1
        ).astype(BF16)

    def kv_copy(ch, h, src_y, to_y, slot):
        ref = kv.at[src_y, pl.ds(R * ch + HALF * h, HALF), :]
        return remote(ref, ref, s_kv.at[ch, h, slot], r_kv.at[ch, h, slot], patch(to_y, z))

    def kv_own(ch):
        send(lambda: kv_copy(ch, 0, y, up, 0))
        send(lambda: kv_copy(ch, 1, y, down, 1))
        send(lambda: kv_copy(ch, 1, y, up, 0))
        send(lambda: kv_copy(ch, 0, y, down, 1))

    def kv_on(ch):
        kv_copy(ch, 0, down, y, 0).wait_recv()
        send(lambda: kv_copy(ch, 0, down, up, 2))
        kv_copy(ch, 1, up, y, 1).wait_recv()
        send(lambda: kv_copy(ch, 1, up, down, 2))

    def hid_on(ch):
        for k in range(1, 4):
            when(z - k >= 0, lambda k=k: hid_copy(ch, z - k, 0).wait_recv())
            send(lambda k=k: hid_copy(ch, z - k, 0), (z - k >= 0) & (z < 3))
            when(z + k <= 3, lambda k=k: hid_copy(ch, z + k, 1).wait_recv())
            send(lambda k=k: hid_copy(ch, z + k, 1), (z + k <= 3) & (z > 0))
            if k == AHEAD and ch + 1 < NCH:
                hid_own(ch + 1)

    def process(ch):
        normalize(ch)
        project(ch)
        kv_own(ch)
        if ch > 0:
            kv_on(ch - 1)

    hid_on(0)
    x_relay(*qc)
    hid_on(1)
    x_wait(*qc, 2)
    send(lambda: qd_other(half))
    second_norm()
    wo_y(down, y, 0).wait_recv()
    send(lambda: wo_y(down, up, 2), c == 0)
    wo_y(up, y, 1).wait_recv()
    send(lambda: wo_y(up, down, 2), c == 1)
    hid_on(2)
    wo_y(opposite, y, 2).wait_recv()
    x_send(*wox)
    qd_other(other).wait_recv()
    process(0)
    process(1)
    hid_on(3)
    process(2)
    process(3)

    kv_on(NCH - 1)

    for h in range(2):
        def residual(i, carry, h=h):
            rows = pl.ds(pl.multiple_of(16 * i, 16), 16)
            blocks = [hidden_rows(zz, z, h, rows) for zz in range(4)]
            hnat[pl.ds(pl.multiple_of(HALF * h + 16 * i, 16), 16)] = in_order(blocks)
            return carry

        lax.fori_loop(0, HALF // 16, residual, 0)

    def wo_other(mask):
        ref = wo.at[:, :, :, mask]
        return remote(ref, ref, s_wos.at[0], r_wos.at[0], sibling)

    x_relay(*wox)
    for ch in range(NCH):
        kv_copy(ch, 1, down, y, 0).wait_recv()
        kv_copy(ch, 0, up, y, 1).wait_recv()
        kv_copy(ch, 0, opposite, y, 2).wait_recv()
        kv_copy(ch, 1, opposite, y, 2).wait_recv()

    def att_copy(j):
        return remote(att.at[j], attg.at[z], s_att.at[j], r_att.at[z], patch(y, j))

    def att_from(k):
        return remote(att.at[k], attg.at[k], s_att.at[k], r_att.at[k], patch(y, k))

    def attend(j):
        rows = pl.ds(pl.multiple_of(BLK * j, 128), BLK)
        for pair in range(3):
            width = min(128, CZ - 128 * pair)
            lanes = slice(128 * pair, 128 * pair + width)
            query = qb[rows, 128 * pair : 128 * pair + 128]
            key_at = 128 * pair if pair < 2 else 512
            value_at = key_at + 256 if pair < 2 else 512
            keys = kv[:, :, key_at : key_at + 128].reshape(2048, 128)
            values = kv[:, :, value_at : value_at + 128].reshape(2048, 128)
            lane = lax.broadcasted_iota(jnp.int32, (BLK, 128), 1)
            result = None
            for side in range(width // 64):
                q1 = query
                if width > 64:
                    keep = (lane >= 64 * side) & (lane < 64 * side + 64)
                    q1 = jnp.where(keep, query.astype(F32), 0.0).astype(BF16)
                scores = dot_nt(q1, keys)
                peak = jnp.max(scores, axis=1, keepdims=True)
                unnormalized = jnp.exp(scores - peak)
                row_total = jnp.sum(unnormalized, axis=1, keepdims=True)
                mix = dot_nn(unnormalized.astype(BF16), values) / row_total
                result = mix if result is None else jnp.where(lane < 64, result, mix)
            if width == 64:
                result = result[:, 64:128]
            att[j, :, lanes] = result.astype(BF16)

    def attend_step(t, carry):
        j = (z + 1 + t) % 4
        attend(j)
        pl.when(t < 3)(lambda: att_copy(j).start())
        return carry

    lax.fori_loop(0, 2, attend_step, 0)
    x_wait(*wox, 2)
    send(lambda: wo_other(half))
    lax.fori_loop(2, 4, attend_step, 0)
    attg[z] = att[z]
    for k in range(4):
        pending.append((z != k, lambda k=k: att_copy(k)))

    wo_other(other).wait_recv()
    for k in range(4):
        when(z != k, lambda k=k: att_from(k).wait_recv())

    whole = jnp.concatenate([attg[k].astype(F32) for k in range(4)], axis=1).astype(BF16)
    out_ref[...] = (hnat[...] + dot_nt(whole, wo[...].reshape(C, C))).astype(BF16)

    for cond, make in pending:
        when(cond, lambda make=make: make().wait_send())


def on_device(latent, conv_weight, channel_bias, w_query, w_key, w_value, w_out):
    any_space = pl.BlockSpec(memory_space=pl.ANY)
    vmem = pl.BlockSpec(memory_space=pltpu.VMEM)
    dma = pltpu.SemaphoreType.DMA
    out = pl.pallas_call(
        kernel,
        out_shape=jax.ShapeDtypeStruct((BLK, C), BF16),
        in_specs=[any_space, any_space, vmem, any_space, any_space, any_space, any_space],
        out_specs=vmem,
        scratch_shapes=[
            pltpu.VMEM((640, C), BF16),
            pltpu.VMEM((640, C), BF16),
            pltpu.VMEM((9, 4, CB, C), BF16),
            pltpu.VMEM((4, CB, C), BF16),
            pltpu.VMEM((3, CZ, C), BF16),
            pltpu.VMEM((4, 4, CB, C), BF16),
            pltpu.VMEM((8, 128), F32),
            pltpu.VMEM((16, 8, 128), F32),
            pltpu.VMEM((8, 128), F32),
            pltpu.VMEM((16, 8, 128), F32),
            pltpu.VMEM((C, 128), BF16),
            pltpu.VMEM((128, C), BF16),
            pltpu.VMEM((C, CZ), BF16),
            pltpu.VMEM((2, 8, C), F32),
            pltpu.VMEM((2, 8, CZ), F32),
            pltpu.VMEM((2, 8, CZ), F32),
            pltpu.VMEM((256, 3 * CZ), F32),
            pltpu.VMEM((4, NCH, 5, HALF, 128), BF16),
            pltpu.VMEM((R, C), BF16),
            pltpu.VMEM((BLK, C), F32),
            pltpu.VMEM((ROWS_Y, 384), BF16),
            pltpu.VMEM((4, ROWS_Y, 2 * CZ), BF16),
            pltpu.VMEM((4, BLK, CZ), BF16),
            pltpu.VMEM((4, BLK, CZ), BF16),
            dma((6,)), dma((16,)), dma((16,)), dma((2, 4)), dma((4,)), dma((2,)), dma((2,)),
            dma((3,)), dma((3,)), dma((3,)), dma((3,)),
            dma((3,)), dma((3,)), dma((3, 4)), dma((3, 4)), dma((3,)), dma((3,)),
            dma((1,)), dma((1,)), dma((2,)), dma((3,)), dma((1,)), dma((3,)), dma((3,)), dma((1,)), dma((1,)),
            dma((2,)), dma((1,)), dma((3,)), dma((3,)), dma((3,)), dma((3,)), dma((1,)), dma((1,)),
            dma((16,)), dma((16,)), dma((2, NCH, 4)), dma((NCH, 4)), dma((NCH, 2, 3)), dma((NCH, 2, 3)),
            dma((4,)), dma((4,)),
        ],
        compiler_params=pltpu.CompilerParams(
            collective_id=0, has_side_effects=True, vmem_limit_bytes=60 * 1024 * 1024
        ),
    )(
        latent.reshape(BLK, C), conv_weight.reshape(9, CB, C), channel_bias.reshape(1, CB), w_query, w_key, w_value, w_out
    )
    return out.reshape(latent.shape)


def solution(mesh):
    return jax.shard_map(
        on_device,
        mesh=mesh,
        in_specs=(
            P(("batch", "patch"), None, None),
            P(None, None, "patch", None),
            P("patch"),
            P("patch", None),
            P("patch", None),
            P("patch", None),
            P("patch", None),
        ),
        out_specs=P(("batch", "patch"), None, None),
        check_vma=False,
    )
```
